256 devices in a mesh: dp: 2 (over core), ctx: 32 (over y, z), head: 4 (over x).
Axes of the slice: x: 4, y: 4, z: 8, core: 2. Of those that a mesh axis runs over, the one named last changes fastest.
Arguments:
- query_states: bfloat16 [32768, 4096], P(('dp', 'ctx'), 'head'), parts along dimension 0, may hold values from -72 to 72
- key_states: bfloat16 [32768, 4096], P(('dp', 'ctx'), 'head'), parts along dimension 0, may hold values from -18 to 18
- value_states: bfloat16 [32768, 4096], P(('dp', 'ctx'), 'head'), parts along dimension 0, may hold values from -6 to 6
- gate_logits: bfloat16 [32, 32768], P('head', ('dp', 'ctx')), parts along dimension 1, may hold values from -16 to 6
- selected_blocks: int32 [256, 8], P(('dp', 'ctx')), parts along dimension 0, may hold values from 0 to 127, as said below
Outputs:
- attn_output: bfloat16 [32768, 4096], P(('dp', 'ctx'), 'head'), parts along dimension 0
The draws below stay inside these ranges and needn't reach their ends.
There are 2 independent parts, one for each index of `dp`. The reference program is written for one: setup_inputs(seed, part) draws one part's arguments, and reference() takes and returns one part's arrays. A program takes and returns all parts, laid end to end along the dimension named above; each array names one. Nothing has to cross between parts.
Inputs may be any that keep to these rules, and one draw needn't show every extreme that they name: `selected_blocks`: row b holds 8 block numbers: each is b itself, which selects nothing, or an earlier block, and the earlier ones of a row are distinct. Over the rows of the blocks inside one aligned span of 512 tokens, the earlier blocks selected that lie inside any other aligned span of 512 tokens are at most one distinct block.
All inputs are finite; a program needn't handle non-finite values.
Results may differ from the reference program's by a relative error of at most 0.012.
Values may be sent and summed in bfloat16 or wider, within the bound.
No kernel may reach another device: no remote copies, remote signals or barrier semaphores. Data moves between devices by JAX's collectives and lax.ppermute only.
A program may use at most 128 MiB of HBM per device.

```python
import jax
import jax.numpy as jnp
from jax import lax

HEADS = 32
HEAD_DIM = 128
BLOCK = 128
TOPK = 8
TOK_DEV = 512
SEQ = 16384
FEAT = 4096


def draw_query_states(key, part):
    drawn_rows = jnp.clip(jax.random.normal(jax.random.fold_in(key, 301), (SEQ, HEADS * HEAD_DIM), jnp.float32), -6.0, 6.0)
    return drawn_rows.astype(jnp.bfloat16)


def draw_key_states(key, part):
    drawn_rows = jnp.clip(jax.random.normal(jax.random.fold_in(key, 202), (SEQ, HEADS * HEAD_DIM), jnp.float32), -6.0, 6.0)
    return drawn_rows.astype(jnp.bfloat16)


def draw_gate_logits(key, part):
    logits = 1.5 * jnp.clip(jax.random.normal(jax.random.fold_in(key, 402), (HEADS, SEQ), jnp.float32), -4.0, 4.0)
    return logits.astype(jnp.bfloat16)


def draw_selected_blocks(key, part):
    dev_count = SEQ // TOK_DEV
    per_dev = TOK_DEV // BLOCK
    block_total = SEQ // BLOCK
    width_all = dev_count + per_dev
    picked = jax.random.randint(jax.random.fold_in(key, 11), (dev_count, dev_count), 0, per_dev)
    block_ids = jnp.arange(block_total)
    block_dev = block_ids // per_dev
    block_pos = block_ids % per_dev
    dev_ids = jnp.arange(dev_count)
    remote_ids = dev_ids[None, :] * per_dev + picked[block_dev]
    remote_ok = dev_ids[None, :] < block_dev[:, None]
    local_pos = jnp.arange(per_dev)
    local_ids = block_dev[:, None] * per_dev + local_pos[None, :]
    local_ok = local_pos[None, :] < block_pos[:, None]
    candidates = jnp.concatenate([remote_ids, local_ids], axis=1)
    usable = jnp.concatenate([remote_ok, local_ok], axis=1)
    column = jnp.arange(width_all)
    ranking = jax.random.randint(jax.random.fold_in(key, 12), (block_total, width_all), 0, 1 << 20) * width_all + column[None, :]
    ranking = jnp.where(usable, ranking, (1 << 28) + column[None, :])
    ranked_cols = jnp.argsort(ranking, axis=1, stable=True)[:, :TOPK]
    chosen = jnp.take_along_axis(candidates, ranked_cols, axis=1)
    chosen_ok = jnp.take_along_axis(usable, ranked_cols, axis=1)
    return jnp.where(chosen_ok, chosen, block_ids[:, None]).astype(jnp.int32)


def level_of(own_key, extent, cuts, smallest, largest):
    gain, own = 1.0, jax.random.fold_in(own_key, 6)
    for position, shards_of in cuts:
        steps = jnp.exp(jax.random.uniform(jax.random.fold_in(own, position), (shards_of,), jnp.float32, smallest / len(cuts), largest / len(cuts)))
        gain = gain * jnp.repeat(steps, extent[position] // shards_of).reshape([-1 if axis == position else 1 for axis in range(len(extent))])
    return gain


def normal_values(rng, dims, spread, limit, split=(), kind=jnp.bfloat16):
    factor_of = level_of(rng, dims, split, -0.22, 0.18) if split else 1.0
    drawn = jax.random.normal(rng, dims, jnp.float32) * spread * factor_of
    return jnp.minimum(jnp.maximum(drawn, -limit), limit).astype(kind)


def setup_inputs(seed: int = 0, part: int = 0) -> dict:
    arg_keys = jax.random.split(jax.random.key(seed), 6)
    part_keys = jax.random.split(jax.random.fold_in(arg_keys[5], part), 6)
    query_states = draw_query_states(jax.random.fold_in(jax.random.fold_in(arg_keys[5], part), 71), part)
    key_states = draw_key_states(jax.random.fold_in(jax.random.fold_in(arg_keys[5], part), 71), part)
    value_states = normal_values(part_keys[2], (SEQ, FEAT), 1.0, 6.0, ((0, 32), (1, 4)))
    gate_logits = draw_gate_logits(jax.random.fold_in(jax.random.fold_in(arg_keys[5], part), 71), part)
    selected_blocks = draw_selected_blocks(jax.random.fold_in(jax.random.fold_in(arg_keys[5], part), 71), part)
    return {"query_states": query_states, "key_states": key_states, "value_states": value_states, "gate_logits": gate_logits, "selected_blocks": selected_blocks}


NEG_FILL = -1e30
ROPE_BASE = 10000.0


def rotate(inputs, angles):
    row_count = inputs.shape[0]
    head_count = angles.shape[0]
    widened = inputs.astype(jnp.float32).reshape(row_count, head_count, -1)
    half_width = widened.shape[-1] // 2
    inv_freq = ROPE_BASE ** (-jnp.arange(half_width).astype(jnp.float32) / half_width)
    phases = angles.T[:, :, None] * inv_freq
    cos_part = jnp.cos(phases)
    sin_part = jnp.sin(phases)
    first_half = widened[..., :half_width]
    second_half = widened[..., half_width:]
    rotated = jnp.concatenate([first_half * cos_part - second_half * sin_part, second_half * cos_part + first_half * sin_part], axis=-1)
    return rotated.reshape(row_count, -1).astype(jnp.bfloat16)


def reference(query_states, key_states, value_states, gate_logits, selected_blocks):
    gate_values = jax.nn.sigmoid(gate_logits.astype(jnp.float32))
    angles = jnp.cumsum(gate_values, axis=1)
    query_rot = rotate(query_states, angles)
    key_rot = rotate(key_states, angles)
    block_count = SEQ // BLOCK
    q_blocks = query_rot.reshape(block_count, BLOCK, HEADS, HEAD_DIM)
    k_blocks = key_rot.reshape(block_count, BLOCK, HEADS, HEAD_DIM)
    v_blocks = value_states.reshape(block_count, BLOCK, HEADS, HEAD_DIM)
    score_scale = HEAD_DIM ** -0.5
    causal_mask = jnp.tril(jnp.ones((BLOCK, BLOCK), dtype=bool))

    def one_block(block_idx):
        chosen = selected_blocks[block_idx]
        keep_mask = jnp.repeat(chosen != block_idx, BLOCK)
        sel_keys = k_blocks[chosen].reshape(TOPK * BLOCK, HEADS, HEAD_DIM).astype(jnp.float32)
        sel_values = v_blocks[chosen].reshape(TOPK * BLOCK, HEADS, HEAD_DIM).astype(jnp.float32)
        group_query = q_blocks[block_idx].astype(jnp.float32)
        own_keys = k_blocks[block_idx].astype(jnp.float32)
        own_values = v_blocks[block_idx].astype(jnp.float32)
        sel_scores = jnp.einsum('qhd,khd->hqk', group_query, sel_keys) * score_scale
        sel_scores = jnp.where(keep_mask[None, None, :], sel_scores, NEG_FILL)
        own_scores = jnp.einsum('qhd,khd->hqk', group_query, own_keys) * score_scale
        own_scores = jnp.where(causal_mask[None], own_scores, NEG_FILL)
        row_max = jnp.maximum(sel_scores.max(-1), own_scores.max(-1))
        sel_weight = jnp.exp(sel_scores - row_max[..., None])
        own_weight = jnp.exp(own_scores - row_max[..., None])
        weight_sum = sel_weight.sum(-1) + own_weight.sum(-1)
        sel_low = lax.optimization_barrier(sel_weight.astype(jnp.bfloat16)).astype(jnp.float32)
        own_low = lax.optimization_barrier(own_weight.astype(jnp.bfloat16)).astype(jnp.float32)
        mixed = jnp.einsum('hqk,khd->qhd', sel_low, sel_values) + jnp.einsum('hqk,khd->qhd', own_low, own_values)
        mixed = mixed / weight_sum.T[:, :, None]
        return mixed.astype(jnp.bfloat16).reshape(BLOCK, HEADS * HEAD_DIM)

    blocks_out = lax.map(one_block, jnp.arange(block_count).astype(jnp.int32))
    return blocks_out.reshape(SEQ, HEADS * HEAD_DIM)
```

```python
import functools
import math

import jax
import jax.numpy as jnp
from jax import lax
from jax.experimental import pallas as pl
from jax.experimental.pallas import tpu as pltpu
from jax.sharding import Mesh, PartitionSpec as P

BLOCK = 128
HEAD = 128
ROWS = 4
RING = 8
NEG_FILL = -1e30
ROPE_BASE = 10000.0
STAT = 48
CHUNKS = ((0, 6), (6, 2))
GROUPS = (((0, 1), (2,), (3,), (4,)), ((0, 1, 2), (3, 4)))


def rotate(inputs, angles):
    row_count = inputs.shape[0]
    head_count = angles.shape[0]
    widened = inputs.astype(jnp.float32).reshape(row_count, head_count, -1)
    half_width = widened.shape[-1] // 2
    inv_freq = ROPE_BASE ** (-jnp.arange(half_width).astype(jnp.float32) / half_width)
    phases = angles.T[:, :, None] * inv_freq
    cos_part = jnp.cos(phases)
    sin_part = jnp.sin(phases)
    first_half = widened[..., :half_width]
    second_half = widened[..., half_width:]
    rotated = jnp.concatenate(
        [
            first_half * cos_part - second_half * sin_part,
            second_half * cos_part + first_half * sin_part,
        ],
        axis=-1,
    )
    return rotated.reshape(row_count, -1).astype(jnp.bfloat16)


def attend_kernel(offsets, heads, first, last, meta, *refs):
    count = len(offsets)
    q_ref = refs[0]
    k_refs = refs[1 : 1 + count]
    v_refs = refs[1 + count : 1 + 2 * count]
    rest = list(refs[1 + 2 * count :])
    given = None
    if not first:
        given = rest[:3]
        rest = rest[3:]
    if last:
        acc0_ref, m0_ref, l0_ref, packed_ref, acc, m_run, l_run = rest
    else:
        acc, m_run, l_run = rest
    r = pl.program_id(0)
    my_y, my_z = meta[0], meta[1]
    scale = HEAD**-0.5 * math.log2(math.e)

    if first:
        acc[...] = jnp.zeros_like(acc)
        m_run[...] = jnp.full_like(m_run, NEG_FILL)
        l_run[...] = jnp.zeros_like(l_run)
    else:
        acc[...] = given[0][...]
        m_run[...] = given[1][...]
        l_run[...] = given[2][...]

    def pair(qb, kb, k_ref, v_ref, causal):
        q_rows = pl.ds(pl.multiple_of(qb * BLOCK, BLOCK), BLOCK)
        k_rows = pl.ds(pl.multiple_of(kb * BLOCK, BLOCK), BLOCK)
        for h in range(heads):
            cols = slice(h * HEAD, (h + 1) * HEAD)
            scores = lax.dot_general(
                k_ref[k_rows, cols],
                q_ref[0, q_rows, cols],
                (((1,), (1,)), ((), ())),
                preferred_element_type=jnp.float32,
            )
            if causal:
                key_pos = lax.broadcasted_iota(jnp.int32, scores.shape, 0)
                query_pos = lax.broadcasted_iota(jnp.int32, scores.shape, 1)
                scores = jnp.where(key_pos <= query_pos, scores, NEG_FILL)
            m_old = m_run[qb, h : h + 1, :]
            m_new = jnp.maximum(m_old, jnp.max(scores, axis=0, keepdims=True))
            weights = jnp.exp2((scores - m_new) * scale)
            fade = jnp.exp2((m_old - m_new) * scale)
            m_run[qb, h : h + 1, :] = m_new
            l_run[qb, h : h + 1, :] = l_run[qb, h : h + 1, :] * fade + jnp.sum(
                weights, axis=0, keepdims=True
            )
            mixed = jnp.dot(
                v_ref[kb, cols, :], weights.astype(jnp.bfloat16), preferred_element_type=jnp.float32
            )
            acc[qb, cols, :] = acc[qb, cols, :] * fade + mixed

    @pl.when(my_y + r < ROWS)
    def _():
        def per_block(qb, carry):
            own = ((my_y + r) * RING + my_z) * 4 + qb
            if 0 in offsets:
                at = offsets.index(0)

                @pl.when(r == 0)
                def _():
                    pair(qb, qb, k_refs[at], v_refs[at], True)

            def per_pick(j, inner):
                blk = meta[2 + (r * 4 + qb) * 8 + j]
                away = lax.rem((blk // 4) % RING - my_z + RING, RING)
                here = jnp.logical_and(blk // (4 * RING) == my_y, blk != own)
                for at, offset in enumerate(offsets):

                    @pl.when(jnp.logical_and(here, away == offset % RING))
                    def _(at=at):
                        pair(qb, blk % 4, k_refs[at], v_refs[at], False)

                return inner

            return lax.fori_loop(0, 8, per_pick, carry)

        lax.fori_loop(0, 4, per_block, 0)

    if last:

        @pl.when(r == 0)
        def _():
            acc0_ref[...] = acc[...]
            m0_ref[...] = m_run[...]
            l0_ref[...] = l_run[...]

        @pl.when(r > 0)
        def _():
            def pack(qb, carry):
                m_all, l_all = m_run[qb], l_run[qb]
                pieces = []
                for value in (m_all, l_all):
                    for _ in range(3):
                        piece = value.astype(jnp.bfloat16).astype(jnp.float32)
                        pieces.append(piece)
                        value = value - piece
                packed_ref[0, qb, heads * HEAD :, :] = jnp.concatenate(pieces, axis=0).astype(
                    jnp.bfloat16
                )
                for h in range(heads):
                    cols = slice(h * HEAD, (h + 1) * HEAD)
                    total = l_run[qb, h : h + 1, :]
                    inverse = 1.0 / jnp.where(total > 0, total, 1.0)
                    packed_ref[0, qb, cols, :] = (acc[qb, cols, :] * inverse).astype(jnp.bfloat16)
                return carry

            lax.fori_loop(0, 4, pack, 0)


def attend(meta, queries, chunk, offsets, keys, values, state, last):
    first_head, heads = chunk
    width = heads * HEAD
    first = state is None
    acc_spec = pl.BlockSpec((4, width, BLOCK), lambda r, meta: (r, 0, 0))
    run_spec = pl.BlockSpec((4, 8, BLOCK), lambda r, meta: (r, 0, 0))
    state_specs = [acc_spec, run_spec, run_spec]
    in_specs = [pl.BlockSpec((1, 512, width), lambda r, meta: (r, 0, first_head // heads))]
    in_specs += [pl.BlockSpec((512, width), lambda r, meta: (0, 0)) for _ in offsets]
    in_specs += [pl.BlockSpec((4, width, BLOCK), lambda r, meta: (0, 0, 0)) for _ in offsets]
    operands = [queries, *keys, *values]
    if not first:
        in_specs += state_specs
        operands += list(state)
    f32 = jnp.float32
    scratch = []
    if last:
        out_shape = [
            jax.ShapeDtypeStruct((4, width, BLOCK), f32),
            jax.ShapeDtypeStruct((4, 8, BLOCK), f32),
            jax.ShapeDtypeStruct((4, 8, BLOCK), f32),
            jax.ShapeDtypeStruct((3, 4, width + STAT, BLOCK), jnp.bfloat16),
        ]
        out_specs = [
            pl.BlockSpec((4, width, BLOCK), lambda r, meta: (0, 0, 0)),
            pl.BlockSpec((4, 8, BLOCK), lambda r, meta: (0, 0, 0)),
            pl.BlockSpec((4, 8, BLOCK), lambda r, meta: (0, 0, 0)),
            pl.BlockSpec((1, 4, width + STAT, BLOCK), lambda r, meta: (jnp.maximum(r - 1, 0), 0, 0, 0)),
        ]
        scratch = [
            pltpu.VMEM((4, width, BLOCK), f32),
            pltpu.VMEM((4, 8, BLOCK), f32),
            pltpu.VMEM((4, 8, BLOCK), f32),
        ]
    else:
        out_shape = [
            jax.ShapeDtypeStruct((16, width, BLOCK), f32),
            jax.ShapeDtypeStruct((16, 8, BLOCK), f32),
            jax.ShapeDtypeStruct((16, 8, BLOCK), f32),
        ]
        out_specs = state_specs
    pairs = 10 * len(offsets)
    return pl.pallas_call(
        functools.partial(attend_kernel, offsets, heads, first, last),
        out_shape=out_shape,
        grid_spec=pltpu.PrefetchScalarGridSpec(
            num_scalar_prefetch=1,
            grid=(ROWS,),
            in_specs=in_specs,
            out_specs=out_specs,
            scratch_shapes=scratch,
        ),
        compiler_params=pltpu.CompilerParams(vmem_limit_bytes=40 << 20),
        cost_estimate=pl.CostEstimate(
            flops=pairs * heads * 4 * BLOCK**3,
            bytes_accessed=(4 << 20) + 16 * width * BLOCK * 8,
            transcendentals=pairs * heads * BLOCK * BLOCK,
        ),
        name=f"attend_{first_head}_{'_'.join(str(o % RING) for o in offsets)}",
    )(meta, *operands)


def join_kernel(heads, acc_ref, m_ref, l_ref, one, two, three, *rest):
    out_ref = rest[-1]
    width = heads * HEAD
    tops, sums = [m_ref[0]], [l_ref[0]]
    for part in (one, two, three):
        stats = part[0, width:, :].astype(jnp.float32)
        top = (stats[16:24] + stats[8:16]) + stats[0:8]
        total = (stats[40:48] + stats[32:40]) + stats[24:32]
        tops.append(jnp.where(total > 0, top, NEG_FILL))
        sums.append(total)
    scale = HEAD**-0.5 * math.log2(math.e)
    highest = jnp.maximum(jnp.maximum(tops[0], tops[1]), jnp.maximum(tops[2], tops[3]))
    fades = [jnp.exp2((top - highest) * scale) for top in tops]
    shares = [fades[0]] + [fades[i] * sums[i] for i in (1, 2, 3)]
    whole = fades[0] * sums[0] + shares[1] + shares[2] + shares[3]
    inverse = 1.0 / whole
    for h in range(heads):
        cols = slice(h * HEAD, (h + 1) * HEAD)
        mixed = acc_ref[0, cols, :] * shares[0][h : h + 1, :]
        for i, part in enumerate((one, two, three)):
            mixed += part[0, cols, :].astype(jnp.float32) * shares[i + 1][h : h + 1, :]
        mixed = mixed * inverse[h : h + 1, :]
        out_ref[:, cols] = mixed.T.astype(jnp.bfloat16)


def join(chunk, state, parts, out):
    first_head, heads = chunk
    width = heads * HEAD
    in_specs = [
        pl.BlockSpec((1, width, BLOCK), lambda b: (b, 0, 0)),
        pl.BlockSpec((1, 8, BLOCK), lambda b: (b, 0, 0)),
        pl.BlockSpec((1, 8, BLOCK), lambda b: (b, 0, 0)),
    ] + [pl.BlockSpec((1, width + STAT, BLOCK), lambda b: (b, 0, 0))] * 3
    operands = [*state, *parts]
    aliases = {}
    if out is not None:
        aliases = {len(operands): 0}
        in_specs.append(pl.BlockSpec(memory_space=pl.ANY))
        operands.append(out)
    return pl.pallas_call(
        functools.partial(join_kernel, heads),
        out_shape=jax.ShapeDtypeStruct((512, 1024), jnp.bfloat16),
        grid=(4,),
        in_specs=in_specs,
        out_specs=pl.BlockSpec((BLOCK, width), lambda b: (b, first_head // heads)),
        input_output_aliases=aliases,
        compiler_params=pltpu.CompilerParams(vmem_limit_bytes=24 << 20),
        cost_estimate=pl.CostEstimate(
            flops=512 * width * 10, bytes_accessed=512 * width * 14, transcendentals=0
        ),
        name=f"join_{first_head}",
    )(*operands)


def shift(value, axis, step):
    size = lax.axis_size(axis)
    return lax.ppermute(value, axis, [(i, (i + step) % size) for i in range(size)])


def to_row(value, step):
    moves = [(i, i + step) for i in range(ROWS) if 0 <= i + step < ROWS]
    return lax.ppermute(value, "y", moves)


def swap(value, axis, bit):
    size = lax.axis_size(axis)
    return lax.ppermute(value, axis, [(i, i ^ bit) for i in range(size)])


def shards(query_states, key_states, value_states, gate_logits, selected_blocks):
    my_y, my_z = lax.axis_index("y"), lax.axis_index("z")
    gate_values = jax.nn.sigmoid(gate_logits.astype(jnp.float32))
    total = jnp.sum(gate_values, axis=1, keepdims=True)
    before = jnp.zeros_like(total)
    picks = [selected_blocks] + [to_row(selected_blocks, -s) for s in (1, 2, 3)]
    for bit in (1, 2, 4):
        other = swap(total, "z", bit)
        before = before + jnp.where((my_z & bit) != 0, other, 0.0)
        total = total + other
    value_states, total = lax.optimization_barrier((value_states, total))
    value_blocks = value_states.reshape(4, BLOCK, -1).transpose(0, 2, 1)
    for bit in (1, 2):
        other = swap(total, "y", bit)
        before = before + jnp.where((my_y & bit) != 0, other, 0.0)
        total = total + other
    angles = before + jnp.cumsum(gate_values, axis=1)
    key_rot = rotate(key_states, angles)
    query_rot = rotate(query_states, angles)
    meta = jnp.concatenate(
        [jnp.stack([my_y, my_z]).astype(jnp.int32)] + [p.reshape(-1) for p in picks]
    )
    queries = jnp.stack([query_rot] + [to_row(query_rot, -s) for s in (1, 2, 3)])

    rings = []
    for first_head, heads in CHUNKS:
        lo, hi = first_head * HEAD, (first_head + heads) * HEAD
        rings.append({0: (key_rot[:, lo:hi], value_blocks[:, lo:hi])})
    for chunk, ring in zip(CHUNKS, rings):
        for sign in (1, -1):
            key, value = ring[0]
            for step in (1, 2, 3):
                value = shift(value, "z", sign)
                key = shift(key, "z", sign)
                ring[-sign * step] = (key, value)
        half = chunk[1] // 2 * HEAD
        far = [
            (
                shift(ring[-sign * 3][0][:, part], "z", sign),
                shift(ring[-sign * 3][1][:, part], "z", sign),
            )
            for sign, part in ((1, slice(0, half)), (-1, slice(half, None)))
        ]
        ring[4] = tuple(jnp.concatenate([far[0][i], far[1][i]], axis=1) for i in (0, 1))

    out = None
    for chunk, ring, groups in zip(CHUNKS, rings, GROUPS):
        state = None
        for index, group in enumerate(groups):
            offsets = []
            for distance in group:
                offsets += [distance] if distance in (0, 4) else [-distance, distance]
            state = attend(
                meta,
                queries,
                chunk,
                tuple(offsets),
                [ring[o][0] for o in offsets],
                [ring[o][1] for o in offsets],
                state,
                index == len(groups) - 1,
            )
        packed = state[3]
        parts = [to_row(packed[s - 1], s) for s in (1, 2, 3)]
        out = join(chunk, state[:3], parts, out)
    return out


def solution(mesh):
    grid = Mesh(mesh.devices.reshape(2, ROWS, RING, 4), ("dp", "y", "z", "head"))
    tokens = ("dp", "y", "z")
    placed = (
        P(tokens, "head"),
        P(tokens, "head"),
        P(tokens, "head"),
        P("head", tokens),
        P(tokens, None),
    )
    return jax.shard_map(
        shards, mesh=grid, in_specs=placed, out_specs=P(tokens, "head"), check_vma=False
    )
```

```python
import functools
import math

import jax
import jax.numpy as jnp
from jax import lax
from jax.experimental import pallas as pl
from jax.experimental.pallas import tpu as pltpu
from jax.sharding import Mesh, PartitionSpec as P

BLOCK = 128
HEAD = 128
ROWS = 4
RING = 8
NEG_FILL = -1e30
ROPE_BASE = 10000.0
STAT = 48
CHUNKS = ((0, 4), (4, 4))
GROUPS = (((0, 1), (2,), (3, 4)), ((0, 1), (2,), (3, 4)))


QUARTER = (1.5703125, 4.837512969970703e-4, 7.54978995489188216e-8)


def sin_cos(phase):
    turns = jnp.floor(phase * (2 / math.pi) + 0.5)
    x = phase
    for part in QUARTER:
        x = x - turns * part
    square = x * x
    sine = ((-1.9515295891e-4 * square + 8.3321608736e-3) * square - 1.6666654611e-1) * square
    sine = sine * x + x
    cosine = ((2.443315711809948e-5 * square - 1.388731625493765e-3) * square + 4.166664568298827e-2)
    cosine = cosine * square * square - 0.5 * square + 1.0
    quadrant = turns.astype(jnp.int32) & 3
    odd = (quadrant & 1) == 1
    sine, cosine = jnp.where(odd, cosine, sine), jnp.where(odd, sine, cosine)
    sine = jnp.where(quadrant >= 2, -sine, sine)
    cosine = jnp.where((quadrant == 1) | (quadrant == 2), -cosine, cosine)
    return sine, cosine


def rotate_kernel(angle_ref, freq_ref, q_ref, k_ref, v_ref, q_out, ka_out, *both_out):
    freq = freq_ref[...]
    lane = lax.broadcasted_iota(jnp.int32, (BLOCK, HEAD), 1)
    low = lane < HEAD // 2
    heads = q_ref.shape[1] // HEAD
    for pair in range(heads // 2):
        even = angle_ref[:, 2 * pair : 2 * pair + 1]
        odd = angle_ref[:, 2 * pair + 1 : 2 * pair + 2]
        sine, cosine = sin_cos(jnp.where(low, even, odd) * freq)
        sine_turned = pltpu.roll(sine, HEAD // 2, 1)
        cosine_turned = pltpu.roll(cosine, HEAD // 2, 1)
        for h in (2 * pair, 2 * pair + 1):
            first, second = (sine, sine_turned) if h % 2 == 0 else (sine_turned, sine)
            signed = jnp.where(low, -first, second)
            first, second = (cosine, cosine_turned) if h % 2 == 0 else (cosine_turned, cosine)
            plain = jnp.where(low, first, second)
            cols = slice(h * HEAD, (h + 1) * HEAD)

            def turn(x):
                x = x.astype(jnp.float32)
                return (x * plain + pltpu.roll(x, HEAD // 2, 1) * signed).astype(jnp.bfloat16)

            q_out[:, cols] = turn(q_ref[:, cols])
            key = turn(k_ref[:, cols])
            if h < 4:
                ka_out[0, h * HEAD : (h + 1) * HEAD, :] = key
            else:
                both_out[(h - 4) // 2][0, 0, h % 2 * HEAD : (h % 2 + 1) * HEAD, :] = key
    for i, out in enumerate(both_out):
        out[1, 0] = v_ref[0, (4 + 2 * i) * HEAD : (6 + 2 * i) * HEAD, :]


def rotate(angles, queries, keys, value_tiles):
    half = HEAD // 2
    inv_freq = ROPE_BASE ** (-jnp.arange(half).astype(jnp.float32) / half)
    inv_freq = jnp.concatenate([inv_freq, inv_freq])[None]
    heads = angles.shape[0]
    bf16 = jnp.bfloat16
    rows = pl.BlockSpec((BLOCK, heads * HEAD), lambda b: (b, 0))
    both = pl.BlockSpec((2, 1, 2 * HEAD, BLOCK), lambda b: (0, b, 0, 0))
    return pl.pallas_call(
        rotate_kernel,
        out_shape=[
            jax.ShapeDtypeStruct(queries.shape, bf16),
            jax.ShapeDtypeStruct((4, 4 * HEAD, BLOCK), bf16),
            jax.ShapeDtypeStruct((2, 4, 2 * HEAD, BLOCK), bf16),
            jax.ShapeDtypeStruct((2, 4, 2 * HEAD, BLOCK), bf16),
        ],
        grid=(4,),
        in_specs=[
            pl.BlockSpec((BLOCK, heads), lambda b: (b, 0)),
            pl.BlockSpec((1, HEAD), lambda b: (0, 0)),
            rows,
            rows,
            pl.BlockSpec((1, heads * HEAD, BLOCK), lambda b: (b, 0, 0)),
        ],
        out_specs=[rows, pl.BlockSpec((1, 4 * HEAD, BLOCK), lambda b: (b, 0, 0)), both, both],
        compiler_params=pltpu.CompilerParams(vmem_limit_bytes=24 << 20),
        cost_estimate=pl.CostEstimate(flops=5 * 10**9, bytes_accessed=6 << 20, transcendentals=0),
        name="rotate",
    )(angles.T, inv_freq, queries, keys, value_tiles)


def attend_kernel(offsets, heads, pieces, first, last, meta, *refs):
    count = len(offsets)
    q_refs, refs = refs[:ROWS], refs[ROWS:]
    flat_k = refs[: count * pieces]
    flat_v = refs[count * pieces : 2 * count * pieces]
    k_refs = [flat_k[i * pieces : (i + 1) * pieces] for i in range(count)]
    v_refs = [flat_v[i * pieces : (i + 1) * pieces] for i in range(count)]
    rest = list(refs[2 * count * pieces :])
    q_ref = rest.pop()
    given = None
    if not first:
        given = rest[:3]
        rest = rest[3:]
    if last:
        acc0_ref, m0_ref, l0_ref, packed_ref, acc, m_run, l_run = rest
    else:
        acc, m_run, l_run = rest
    r = pl.program_id(0)
    scale = HEAD**-0.5 * math.log2(math.e)

    for row in range(ROWS):

        @pl.when(r == row)
        def _(row=row):
            q_ref[...] = q_refs[row][...]

    if first:
        acc[...] = jnp.zeros_like(acc)
        m_run[...] = jnp.full_like(m_run, NEG_FILL)
        l_run[...] = jnp.zeros_like(l_run)
    else:
        acc[...] = given[0][...]
        m_run[...] = given[1][...]
        l_run[...] = given[2][...]

    def pair(qb, kb, k_ref, v_ref, causal):
        q_rows = pl.ds(pl.multiple_of(qb * BLOCK, BLOCK), BLOCK)
        span = range(heads)
        cols = [slice(h * HEAD, (h + 1) * HEAD) for h in span]
        each = heads // pieces
        part = [slice(h % each * HEAD, (h % each + 1) * HEAD) for h in span]
        m_all, l_all = m_run[qb], l_run[qb]
        scores = [
            lax.dot_general(
                k_ref[h // each][kb, part[h], :],
                q_ref[q_rows, cols[h]],
                (((1,), (1,)), ((), ())),
                preferred_element_type=jnp.float32,
            )
            for h in span
        ]
        if causal:
            key_pos = lax.broadcasted_iota(jnp.int32, scores[0].shape, 0)
            query_pos = lax.broadcasted_iota(jnp.int32, scores[0].shape, 1)
            scores = [jnp.where(key_pos <= query_pos, s, NEG_FILL) for s in scores]
        tops = [jnp.max(s, axis=0, keepdims=True) for s in scores]
        if heads < 8:
            tops.append(m_all[heads:])
        m_new = jnp.maximum(m_all, jnp.concatenate(tops, axis=0))
        fade = jnp.exp2((m_all - m_new) * scale)
        weights = [jnp.exp2((scores[h] - m_new[h : h + 1]) * scale) for h in span]
        sums = [jnp.sum(w, axis=0, keepdims=True) for w in weights]
        if heads < 8:
            sums.append(jnp.zeros((8 - heads, BLOCK), jnp.float32))
        mixed = [
            jnp.dot(
                v_ref[h // each][kb, part[h], :],
                weights[h].astype(jnp.bfloat16),
                preferred_element_type=jnp.float32,
            )
            for h in span
        ]
        whole = [acc[qb, cols[h], :] * fade[h : h + 1] + mixed[h] for h in span]
        m_run[qb] = m_new
        l_run[qb] = l_all * fade + jnp.concatenate(sums, axis=0)
        for h in span:
            acc[qb, cols[h], :] = whole[h]

    def per_block(qb, carry):
        base = (r * 4 + qb) * RING
        for at, offset in enumerate(offsets):
            code = meta[base + offset % RING]
            if offset == 0:

                @pl.when(r == 0)
                def _(at=at):
                    pair(qb, qb, k_refs[at], v_refs[at], True)

                def per_pick(kb, inner, at=at, code=code):
                    @pl.when((code >> kb) & 1 == 1)
                    def _():
                        pair(qb, kb, k_refs[at], v_refs[at], False)

                    return inner

                lax.fori_loop(0, 4, per_pick, 0)
            else:

                @pl.when(code > 0)
                def _(at=at, code=code):
                    pair(qb, code - 1, k_refs[at], v_refs[at], False)

        return carry

    lax.fori_loop(0, 4, per_block, 0)

    if last:

        @pl.when(r == 0)
        def _():
            acc0_ref[...] = acc[...]
            m0_ref[...] = m_run[...]
            l0_ref[...] = l_run[...]

        @pl.when(r > 0)
        def _():
            def pack(qb, carry):
                m_all, l_all = m_run[qb], l_run[qb]
                pieces = []
                for value in (m_all, l_all):
                    for _ in range(3):
                        piece = value.astype(jnp.bfloat16).astype(jnp.float32)
                        pieces.append(piece)
                        value = value - piece
                packed_ref[0, qb, heads * HEAD :, :] = jnp.concatenate(pieces, axis=0).astype(
                    jnp.bfloat16
                )
                for h in range(heads):
                    cols = slice(h * HEAD, (h + 1) * HEAD)
                    total = l_run[qb, h : h + 1, :]
                    inverse = 1.0 / jnp.where(total > 0, total, 1.0)
                    packed_ref[0, qb, cols, :] = (acc[qb, cols, :] * inverse).astype(jnp.bfloat16)
                return carry

            lax.fori_loop(0, 4, pack, 0)


def attend(meta, queries, chunk, offsets, keys, values, state, last):
    first_head, heads = chunk
    width = heads * HEAD
    first = state is None
    acc_spec = pl.BlockSpec((4, width, BLOCK), lambda r, meta: (r, 0, 0))
    run_spec = pl.BlockSpec((4, 8, BLOCK), lambda r, meta: (r, 0, 0))
    state_specs = [acc_spec, run_spec, run_spec]
    in_specs = [pl.BlockSpec((512, width), lambda r, meta: (0, first_head // heads))] * ROWS
    pieces = len(keys[0])
    for group, half in ((keys, 0), (values, 1)):
        for arrays in group:
            for array in arrays:
                if array.ndim == 3:
                    in_specs.append(
                        pl.BlockSpec((4, width // pieces, BLOCK), lambda r, meta: (0, 0, 0))
                    )
                else:
                    in_specs.append(
                        pl.BlockSpec(
                            (None, 4, width // pieces, BLOCK),
                            lambda r, meta, half=half: (half, 0, 0, 0),
                        )
                    )
    operands = list(queries) + [x for arrays in keys for x in arrays] + [x for arrays in values for x in arrays]
    if not first:
        in_specs += state_specs
        operands += list(state)
    f32 = jnp.float32
    scratch = []
    if last:
        out_shape = [
            jax.ShapeDtypeStruct((4, width, BLOCK), f32),
            jax.ShapeDtypeStruct((4, 8, BLOCK), f32),
            jax.ShapeDtypeStruct((4, 8, BLOCK), f32),
            jax.ShapeDtypeStruct((3, 4, width + STAT, BLOCK), jnp.bfloat16),
        ]
        out_specs = [
            pl.BlockSpec((4, width, BLOCK), lambda r, meta: (0, 0, 0)),
            pl.BlockSpec((4, 8, BLOCK), lambda r, meta: (0, 0, 0)),
            pl.BlockSpec((4, 8, BLOCK), lambda r, meta: (0, 0, 0)),
            pl.BlockSpec((1, 4, width + STAT, BLOCK), lambda r, meta: (jnp.maximum(r - 1, 0), 0, 0, 0)),
        ]
        scratch = [
            pltpu.VMEM((4, width, BLOCK), f32),
            pltpu.VMEM((4, 8, BLOCK), f32),
            pltpu.VMEM((4, 8, BLOCK), f32),
        ]
    else:
        out_shape = [
            jax.ShapeDtypeStruct((16, width, BLOCK), f32),
            jax.ShapeDtypeStruct((16, 8, BLOCK), f32),
            jax.ShapeDtypeStruct((16, 8, BLOCK), f32),
        ]
        out_specs = state_specs
    scratch.append(pltpu.VMEM((512, width), jnp.bfloat16))
    return pl.pallas_call(
        functools.partial(attend_kernel, offsets, heads, pieces, first, last),
        out_shape=out_shape,
        grid_spec=pltpu.PrefetchScalarGridSpec(
            num_scalar_prefetch=1,
            grid=(ROWS,),
            in_specs=in_specs,
            out_specs=out_specs,
            scratch_shapes=scratch,
        ),
        compiler_params=pltpu.CompilerParams(vmem_limit_bytes=40 << 20),
        cost_estimate=pl.CostEstimate(
            flops=int((3 + 4 * len(offsets)) * 1.1e9),
            bytes_accessed=1 << 20,
            transcendentals=0,
        ),
        name=f"attend_{first_head}_{'_'.join(str(o % RING) for o in offsets)}",
    )(meta, *operands)


def join_kernel(heads, acc_ref, m_ref, l_ref, one, two, three, *rest):
    out_ref = rest[-1]
    width = heads * HEAD
    tops, sums = [m_ref[0]], [l_ref[0]]
    for part in (one, two, three):
        stats = part[0, width:, :].astype(jnp.float32)
        top = (stats[16:24] + stats[8:16]) + stats[0:8]
        total = (stats[40:48] + stats[32:40]) + stats[24:32]
        tops.append(jnp.where(total > 0, top, NEG_FILL))
        sums.append(total)
    scale = HEAD**-0.5 * math.log2(math.e)
    highest = jnp.maximum(jnp.maximum(tops[0], tops[1]), jnp.maximum(tops[2], tops[3]))
    fades = [jnp.exp2((top - highest) * scale) for top in tops]
    shares = [fades[0]] + [fades[i] * sums[i] for i in (1, 2, 3)]
    whole = fades[0] * sums[0] + shares[1] + shares[2] + shares[3]
    inverse = 1.0 / whole
    for h in range(heads):
        cols = slice(h * HEAD, (h + 1) * HEAD)
        mixed = acc_ref[0, cols, :] * shares[0][h : h + 1, :]
        for i, part in enumerate((one, two, three)):
            mixed += part[0, cols, :].astype(jnp.float32) * shares[i + 1][h : h + 1, :]
        mixed = mixed * inverse[h : h + 1, :]
        out_ref[:, cols] = mixed.T.astype(jnp.bfloat16)


def join(chunk, state, parts, out):
    first_head, heads = chunk
    width = heads * HEAD
    in_specs = [
        pl.BlockSpec((1, width, BLOCK), lambda b: (b, 0, 0)),
        pl.BlockSpec((1, 8, BLOCK), lambda b: (b, 0, 0)),
        pl.BlockSpec((1, 8, BLOCK), lambda b: (b, 0, 0)),
    ] + [pl.BlockSpec((1, width + STAT, BLOCK), lambda b: (b, 0, 0))] * 3
    operands = [*state, *parts]
    aliases = {}
    if out is not None:
        aliases = {len(operands): 0}
        in_specs.append(pl.BlockSpec(memory_space=pl.ANY))
        operands.append(out)
    return pl.pallas_call(
        functools.partial(join_kernel, heads),
        out_shape=jax.ShapeDtypeStruct((512, 1024), jnp.bfloat16),
        grid=(4,),
        in_specs=in_specs,
        out_specs=pl.BlockSpec((BLOCK, width), lambda b: (b, first_head // heads)),
        input_output_aliases=aliases,
        compiler_params=pltpu.CompilerParams(vmem_limit_bytes=24 << 20),
        cost_estimate=pl.CostEstimate(
            flops=512 * width * 10, bytes_accessed=512 * width * 14, transcendentals=0
        ),
        name=f"join_{first_head}",
    )(*operands)


def shift(value, axis, step):
    size = lax.axis_size(axis)
    return lax.ppermute(value, axis, [(i, (i + step) % size) for i in range(size)])


def to_row(value, step):
    moves = [(i, i + step) for i in range(ROWS) if 0 <= i + step < ROWS]
    return lax.ppermute(value, "y", moves)


def swap(value, axis, bit):
    size = lax.axis_size(axis)
    return lax.ppermute(value, axis, [(i, i ^ bit) for i in range(size)])


def after(value, *others):
    return lax.optimization_barrier((value, *others))[0]


class Wire:
    def __init__(self, side, sign, depth=2):
        self.side, self.sign, self.depth = side, sign, depth
        self.sent = []

    def send(self, name, ring, distance, *others):
        source = ring[-self.sign * (distance - 1)]
        waits = list(others)
        if len(self.sent) >= self.depth:
            waits.append(self.sent[-self.depth])
        if waits:
            source = after(source, *waits)
        with jax.named_scope(f"{name}{distance}_{self.side}"):
            got = shift(source, "z", self.sign)
        self.sent.append(got)
        ring[-self.sign * distance if distance < 4 else 4] = got


def shards(query_states, key_states, value_states, gate_logits, selected_blocks):
    my_y, my_z = lax.axis_index("y"), lax.axis_index("z")
    gate_values = jax.nn.sigmoid(gate_logits.astype(jnp.float32))
    total = jnp.sum(gate_values, axis=1, keepdims=True)
    before = jnp.zeros_like(total)
    value_tiles = value_states.reshape(4, BLOCK, -1).transpose(0, 2, 1)
    values_a = {0: value_tiles[:, : 4 * HEAD]}
    right, left = Wire("right", 1), Wire("left", -1)
    for wire in (right, left):
        wire.send("va", values_a, 1)
    with jax.named_scope("prefix"):
        for bit in (1, 2, 4):
            other = swap(total, "z", bit)
            before = before + jnp.where((my_z & bit) != 0, other, 0.0)
            total = total + other
        total = after(total, values_a[1], values_a[-1])
        for bit in (1, 2):
            other = swap(total, "y", bit)
            before = before + jnp.where((my_y & bit) != 0, other, 0.0)
            total = total + other
    for wire in (right, left):
        wire.send("va", values_a, 2)
    angles = before + jnp.cumsum(gate_values, axis=1)
    query_rot, keys, kv_b, kv_c = rotate(angles, query_states, key_states, value_tiles)
    keys_a, both = {0: keys}, [{0: kv_b}, {0: kv_c}]
    with jax.named_scope("queries"):
        queries = [query_rot] + [to_row(query_rot, -s) for s in (1, 2, 3)]
    chosen = after(selected_blocks, total)
    with jax.named_scope("picks"):
        picks = [chosen] + [to_row(chosen, -s) for s in (1, 2, 3)]

    blocks = jnp.stack(picks).reshape(16, 1, 8)
    row = lax.broadcasted_iota(jnp.int32, (16, RING, 8), 0)
    distance = lax.broadcasted_iota(jnp.int32, (16, RING, 8), 1)
    own = ((my_y + row // 4) * RING + my_z) * 4 + row % 4
    hit = (blocks >> 5 == my_y) & (((blocks >> 2) - my_z) & 7 == distance)
    hit &= (blocks != own) & (my_y + row // 4 < ROWS)
    code = jnp.where(distance == 0, 1 << (blocks & 3), (blocks & 3) + 1)
    meta = jnp.sum(jnp.where(hit, code, 0), axis=2).reshape(-1)

    def call(part, group, state, last):
        offsets = []
        for distance in group:
            offsets += [distance] if distance in (0, 4) else [-distance, distance]
        if part == 0:
            keys = [(keys_a[o],) for o in offsets]
            values = [(values_a[o],) for o in offsets]
        else:
            keys = values = [tuple(b[o] for b in both) for o in offsets]
        return attend(meta, queries, CHUNKS[part], tuple(offsets), keys, values, state, last)

    def finish(part, state, out):
        packed = state[3]
        with jax.named_scope("partials"):
            parts = [to_row(packed[s - 1], s) for s in (1, 2, 3)]
        return join(CHUNKS[part], state[:3], parts, out)

    b, c = both
    for name, ring, distance in (("ka", keys_a, 1), ("va", values_a, 3)):
        for wire in (right, left):
            wire.send(name, ring, distance)
    for wire in (right, left):
        wire.send("ka", keys_a, 2)
    right.send("va", values_a, 4)
    left.send("kvb", b, 1)
    for wire in (right, left):
        wire.send("ka", keys_a, 3)
    right.send("kvb", b, 1)
    left.send("kvc", c, 1)
    state = call(0, GROUPS[0][0], None, False)
    right.send("ka", keys_a, 4, state[1])
    left.send("kvb", b, 2, state[1])
    right.send("kvc", c, 1)
    left.send("kvc", c, 2)
    state = call(0, GROUPS[0][1], state, False)
    right.send("kvb", b, 2, state[1])
    left.send("kvb", b, 3, state[1])
    right.send("kvc", c, 2)
    left.send("kvc", c, 3)
    state = call(0, GROUPS[0][2], state, True)
    right.send("kvb", b, 3, state[1])
    left.send("kvb", b, 4, state[1])
    right.send("kvc", c, 3)
    left.send("kvc", c, 4)
    out = finish(0, state, None)
    state = call(1, GROUPS[1][0], None, False)
    state = call(1, GROUPS[1][1], state, False)
    state = call(1, GROUPS[1][2], state, True)
    return finish(1, state, out)


def solution(mesh):
    grid = Mesh(mesh.devices.reshape(2, ROWS, RING, 4), ("dp", "y", "z", "head"))
    tokens = ("dp", "y", "z")
    placed = (
        P(tokens, "head"),
        P(tokens, "head"),
        P(tokens, "head"),
        P("head", tokens),
        P(tokens, None),
    )
    return jax.shard_map(
        shards, mesh=grid, in_specs=placed, out_specs=P(tokens, "head"), check_vma=False
    )
```

```python
import functools
import math

import jax
import jax.numpy as jnp
from jax import lax
from jax.experimental import pallas as pl
from jax.experimental.pallas import tpu as pltpu
from jax.sharding import Mesh, PartitionSpec as P

BLOCK = 128
HEAD = 128
ROWS = 4
RING = 8
NEG_FILL = -1e30
ROPE_BASE = 10000.0
VMEM_LIMIT = 24 << 20
IDLE = 4
STAT = 48
CHUNKS = ((0, 4), (4, 4))
GROUPS = (((0, 1, 2), (3, 4)), ((0, 1), (2, 3), (4,)))


QUARTER = (1.5703125, 4.837512969970703e-4, 7.54978995489188216e-8)


def sin_cos(phase):
    turns = jnp.floor(phase * (2 / math.pi) + 0.5)
    x = phase
    for part in QUARTER:
        x = x - turns * part
    square = x * x
    sine = ((-1.9515295891e-4 * square + 8.3321608736e-3) * square - 1.6666654611e-1) * square
    sine = sine * x + x
    cosine = ((2.443315711809948e-5 * square - 1.388731625493765e-3) * square + 4.166664568298827e-2)
    cosine = cosine * square * square - 0.5 * square + 1.0
    quadrant = turns.astype(jnp.int32) & 3
    odd = (quadrant & 1) == 1
    sine, cosine = jnp.where(odd, cosine, sine), jnp.where(odd, sine, cosine)
    sine = jnp.where(quadrant >= 2, -sine, sine)
    cosine = jnp.where((quadrant == 1) | (quadrant == 2), -cosine, cosine)
    return sine, cosine


def rotate_kernel(angle_ref, freq_ref, q_ref, k_ref, *outs):
    freq = freq_ref[...]
    lane = lax.broadcasted_iota(jnp.int32, (BLOCK, HEAD), 1)
    low = lane < HEAD // 2
    heads = q_ref.shape[1] // HEAD
    for pair in range(heads // 2):
        even = angle_ref[:, 2 * pair : 2 * pair + 1]
        odd = angle_ref[:, 2 * pair + 1 : 2 * pair + 2]
        sine, cosine = sin_cos(jnp.where(low, even, odd) * freq)
        sine_turned = pltpu.roll(sine, HEAD // 2, 1)
        cosine_turned = pltpu.roll(cosine, HEAD // 2, 1)
        for h in (2 * pair, 2 * pair + 1):
            first, second = (sine, sine_turned) if h % 2 == 0 else (sine_turned, sine)
            signed = jnp.where(low, -first, second)
            first, second = (cosine, cosine_turned) if h % 2 == 0 else (cosine_turned, cosine)
            plain = jnp.where(low, first, second)
            cols = slice(h * HEAD, (h + 1) * HEAD)

            def turn(x):
                x = x.astype(jnp.float32)
                return (x * plain + pltpu.roll(x, HEAD // 2, 1) * signed).astype(jnp.bfloat16)

            part = slice(h % 4 * HEAD, (h % 4 + 1) * HEAD)
            outs[0][:, cols] = turn(q_ref[:, cols])
            outs[1 + h // 4][0, part, :] = turn(k_ref[:, cols])


def rotate(angles, queries, keys):
    half = HEAD // 2
    inv_freq = ROPE_BASE ** (-jnp.arange(half).astype(jnp.float32) / half)
    inv_freq = jnp.concatenate([inv_freq, inv_freq])[None]
    heads = angles.shape[0]
    bf16 = jnp.bfloat16
    rows = pl.BlockSpec((BLOCK, heads * HEAD), lambda b: (b, 0))
    tiled = pl.BlockSpec((1, 4 * HEAD, BLOCK), lambda b: (b, 0, 0))
    return pl.pallas_call(
        rotate_kernel,
        out_shape=[
            jax.ShapeDtypeStruct(queries.shape, bf16),
            jax.ShapeDtypeStruct((4, 4 * HEAD, BLOCK), bf16),
            jax.ShapeDtypeStruct((4, 4 * HEAD, BLOCK), bf16),
        ],
        grid=(4,),
        in_specs=[
            pl.BlockSpec((BLOCK, heads), lambda b: (b, 0)),
            pl.BlockSpec((1, HEAD), lambda b: (0, 0)),
            rows,
            rows,
        ],
        out_specs=[rows, tiled, tiled],
        compiler_params=pltpu.CompilerParams(vmem_limit_bytes=VMEM_LIMIT),
        cost_estimate=pl.CostEstimate(flops=5 * 10**9, bytes_accessed=6 << 20, transcendentals=0),
        name="rotate",
    )(angles.T, inv_freq, queries, keys)


def attend_kernel(offsets, heads, first, last, meta, *refs):
    count = len(offsets)
    given_q, refs = refs[0], refs[1:]
    k_refs, v_refs = refs[:count], refs[count : 2 * count]
    rest = list(refs[2 * count :])
    acc, m_run, l_run, q_ref, k_all, v_all, todo = rest[-7:]
    rest = rest[:-7]
    given = None
    if not first:
        given, rest = rest[:3], rest[3:]
    r = pl.program_id(0)
    scale = HEAD**-0.5 * math.log2(math.e)

    @pl.when(r == 0)
    def _():
        for at in range(count):
            k_all[at] = k_refs[at][...]
            v_all[at] = v_refs[at][...]
        q_ref[IDLE * BLOCK :, :] = jnp.zeros((BLOCK, heads * HEAD), jnp.bfloat16)
        acc[IDLE] = jnp.zeros((heads * HEAD, BLOCK), jnp.float32)
        m_run[IDLE] = jnp.full((8, BLOCK), NEG_FILL)
        l_run[IDLE] = jnp.zeros((8, BLOCK), jnp.float32)

    q_ref[: IDLE * BLOCK, :] = given_q[0]
    if first:
        acc[:IDLE] = jnp.zeros((IDLE, heads * HEAD, BLOCK), jnp.float32)
        m_run[:IDLE] = jnp.full((IDLE, 8, BLOCK), NEG_FILL)
        l_run[:IDLE] = jnp.zeros((IDLE, 8, BLOCK), jnp.float32)
    else:
        acc[:IDLE] = given[0][...]
        m_run[:IDLE] = given[1][...]
        l_run[:IDLE] = given[2][...]

    span = range(heads)
    cols = [slice(h * HEAD, (h + 1) * HEAD) for h in span]

    def two(items, causal):
        olds, scores = [], []
        for qb, at, kb in items:
            q_rows = pl.ds(pl.multiple_of(qb * BLOCK, BLOCK), BLOCK)
            olds.append((m_run[qb], l_run[qb]))
            scores.append(
                [
                    lax.dot_general(
                        k_all[at, kb, cols[h], :],
                        q_ref[q_rows, cols[h]],
                        (((1,), (1,)), ((), ())),
                        preferred_element_type=jnp.float32,
                    )
                    for h in span
                ]
            )
        if causal:
            key_pos = lax.broadcasted_iota(jnp.int32, (BLOCK, BLOCK), 0)
            query_pos = lax.broadcasted_iota(jnp.int32, (BLOCK, BLOCK), 1)
            seen = key_pos <= query_pos
            scores = [[jnp.where(seen, s, NEG_FILL) for s in group] for group in scores]
        results = []
        for (qb, at, kb), (m_old, l_old), group in zip(items, olds, scores):
            tops = [jnp.max(s, axis=0, keepdims=True) for s in group]
            if heads < 8:
                tops.append(m_old[heads:])
            m_new = jnp.maximum(m_old, jnp.concatenate(tops, axis=0))
            fade = jnp.exp2((m_old - m_new) * scale)
            weights = [jnp.exp2((group[h] - m_new[h : h + 1]) * scale) for h in span]
            sums = [jnp.sum(w, axis=0, keepdims=True) for w in weights]
            if heads < 8:
                sums.append(jnp.zeros((8 - heads, BLOCK), jnp.float32))
            mixed = [
                jnp.dot(
                    v_all[at, kb, cols[h], :],
                    weights[h].astype(jnp.bfloat16),
                    preferred_element_type=jnp.float32,
                )
                for h in span
            ]
            results.append((m_new, l_old * fade + jnp.concatenate(sums, axis=0), fade, mixed))
        wholes = [
            [acc[qb, cols[h], :] * fade[h : h + 1] + mixed[h] for h in span]
            for (qb, _, _), (_, _, fade, mixed) in zip(items, results)
        ]
        for (qb, _, _), (m_new, l_new, _, _), whole in zip(items, results, wholes):
            m_run[qb] = m_new
            l_run[qb] = l_new
            for h in span:
                acc[qb, cols[h], :] = whole[h]

    if 0 in offsets:
        here = offsets.index(0)

        @pl.when(r == 0)
        def _():
            def own(i, carry):
                two([(2 * i, here, 2 * i), (2 * i + 1, here, 2 * i + 1)], True)
                return carry

            lax.fori_loop(0, 2, own, 0)

    length, newest = jnp.int32(0), jnp.int32(-1)
    for at, offset in enumerate(offsets):
        for choice in range(4 if offset == 0 else 1):
            for qb in range(4):
                code = meta[(r * 4 + qb) * RING + offset % RING]
                if offset == 0:
                    valid, kb = (code >> choice) & 1, choice
                else:
                    valid, kb = (code > 0).astype(jnp.int32), jnp.maximum(code - 1, 0)
                item = qb + at * 16 + kb * 256
                clash = valid & length & (newest == qb).astype(jnp.int32) & 1
                todo[length] = jnp.where(clash == 1, IDLE, item)
                todo[length + 1] = item
                length += valid * (1 + clash)
                newest = jnp.where(valid == 1, qb, newest)
    todo[length] = IDLE

    def step(i, carry):
        items = []
        for side in (0, 1):
            item = todo[2 * i + side]
            items.append((item & 15, (item >> 4) & 15, item >> 8))
        two(items, False)
        return carry

    lax.fori_loop(0, (length + 1) >> 1, step, 0)

    if not last:
        acc_out, m_out, l_out = rest
        acc_out[...] = acc[:IDLE]
        m_out[...] = m_run[:IDLE]
        l_out[...] = l_run[:IDLE]
    else:
        acc0_ref, m0_ref, l0_ref, packed_ref = rest

        @pl.when(r == 0)
        def _():
            acc0_ref[...] = acc[:IDLE]
            m0_ref[...] = m_run[:IDLE]
            l0_ref[...] = l_run[:IDLE]

        @pl.when(r > 0)
        def _():
            def pack(qb, carry):
                pieces = []
                for value in (m_run[qb], l_run[qb]):
                    for _ in range(3):
                        piece = value.astype(jnp.bfloat16).astype(jnp.float32)
                        pieces.append(piece)
                        value = value - piece
                packed_ref[0, qb, heads * HEAD :, :] = jnp.concatenate(pieces, axis=0).astype(
                    jnp.bfloat16
                )
                total = l_run[qb]
                inverse = 1.0 / jnp.where(total > 0, total, 1.0)
                for h in span:
                    packed_ref[0, qb, cols[h], :] = (
                        acc[qb, cols[h], :] * inverse[h : h + 1]
                    ).astype(jnp.bfloat16)
                return carry

            lax.fori_loop(0, 4, pack, 0)


def attend(meta, queries, chunk, offsets, keys, values, state, last):
    first_head, heads = chunk
    width = heads * HEAD
    first = state is None
    acc_spec = pl.BlockSpec((4, width, BLOCK), lambda r, meta: (r, 0, 0))
    run_spec = pl.BlockSpec((4, 8, BLOCK), lambda r, meta: (r, 0, 0))
    state_specs = [acc_spec, run_spec, run_spec]
    in_specs = [
        pl.BlockSpec(
            (1, 512, width),
            lambda r, meta: (jnp.minimum(meta[16 * RING] + r, ROWS - 1), 0, first_head // heads),
        )
    ]
    in_specs += [pl.BlockSpec((4, width, BLOCK), lambda r, meta: (0, 0, 0))] * (2 * len(offsets))
    operands = [queries, *keys, *values]
    if not first:
        in_specs += state_specs
        operands += list(state)
    f32 = jnp.float32
    if last:
        out_shape = [
            jax.ShapeDtypeStruct((4, width, BLOCK), f32),
            jax.ShapeDtypeStruct((4, 8, BLOCK), f32),
            jax.ShapeDtypeStruct((4, 8, BLOCK), f32),
            jax.ShapeDtypeStruct((3, 4, width + STAT, BLOCK), jnp.bfloat16),
        ]
        out_specs = [
            pl.BlockSpec((4, width, BLOCK), lambda r, meta: (0, 0, 0)),
            pl.BlockSpec((4, 8, BLOCK), lambda r, meta: (0, 0, 0)),
            pl.BlockSpec((4, 8, BLOCK), lambda r, meta: (0, 0, 0)),
            pl.BlockSpec((1, 4, width + STAT, BLOCK), lambda r, meta: (jnp.maximum(r - 1, 0), 0, 0, 0)),
        ]
    else:
        out_shape = [
            jax.ShapeDtypeStruct((16, width, BLOCK), f32),
            jax.ShapeDtypeStruct((16, 8, BLOCK), f32),
            jax.ShapeDtypeStruct((16, 8, BLOCK), f32),
        ]
        out_specs = state_specs
    count = len(offsets)
    scratch = [
        pltpu.VMEM((5, width, BLOCK), f32),
        pltpu.VMEM((5, 8, BLOCK), f32),
        pltpu.VMEM((5, 8, BLOCK), f32),
        pltpu.VMEM((5 * BLOCK, width), jnp.bfloat16),
        pltpu.VMEM((count, 4, width, BLOCK), jnp.bfloat16),
        pltpu.VMEM((count, 4, width, BLOCK), jnp.bfloat16),
        pltpu.SMEM((80,), jnp.int32),
    ]
    return list(pl.pallas_call(
        functools.partial(attend_kernel, offsets, heads, first, last),
        out_shape=out_shape,
        grid_spec=pltpu.PrefetchScalarGridSpec(
            num_scalar_prefetch=1,
            grid=(ROWS,),
            in_specs=in_specs,
            out_specs=out_specs,
            scratch_shapes=scratch,
        ),
        compiler_params=pltpu.CompilerParams(vmem_limit_bytes=VMEM_LIMIT),
        cost_estimate=pl.CostEstimate(
            flops=int((2 + 3 * len(offsets)) * 1.1e9),
            bytes_accessed=1 << 20,
            transcendentals=0,
        ),
        name=f"attend_{first_head}_{'_'.join(str(o % RING) for o in offsets)}",
    )(meta, *operands))


def join_kernel(heads, acc_ref, m_ref, l_ref, one, two, three, *rest):
    out_ref = rest[-1]
    width = heads * HEAD
    tops, sums = [m_ref[0]], [l_ref[0]]
    for part in (one, two, three):
        stats = part[0, width:, :].astype(jnp.float32)
        top = (stats[16:24] + stats[8:16]) + stats[0:8]
        total = (stats[40:48] + stats[32:40]) + stats[24:32]
        tops.append(jnp.where(total > 0, top, NEG_FILL))
        sums.append(total)
    scale = HEAD**-0.5 * math.log2(math.e)
    highest = jnp.maximum(jnp.maximum(tops[0], tops[1]), jnp.maximum(tops[2], tops[3]))
    fades = [jnp.exp2((top - highest) * scale) for top in tops]
    shares = [fades[0]] + [fades[i] * sums[i] for i in (1, 2, 3)]
    whole = fades[0] * sums[0] + shares[1] + shares[2] + shares[3]
    inverse = 1.0 / whole
    for h in range(heads):
        cols = slice(h * HEAD, (h + 1) * HEAD)
        mixed = acc_ref[0, cols, :] * shares[0][h : h + 1, :]
        for i, part in enumerate((one, two, three)):
            mixed += part[0, cols, :].astype(jnp.float32) * shares[i + 1][h : h + 1, :]
        mixed = mixed * inverse[h : h + 1, :]
        out_ref[:, cols] = mixed.T.astype(jnp.bfloat16)


def join(chunk, state, parts, out):
    first_head, heads = chunk
    width = heads * HEAD
    in_specs = [
        pl.BlockSpec((1, width, BLOCK), lambda b: (b, 0, 0)),
        pl.BlockSpec((1, 8, BLOCK), lambda b: (b, 0, 0)),
        pl.BlockSpec((1, 8, BLOCK), lambda b: (b, 0, 0)),
    ] + [pl.BlockSpec((1, width + STAT, BLOCK), lambda b: (b, 0, 0))] * 3
    operands = [*state, *parts]
    aliases = {}
    if out is not None:
        aliases = {len(operands): 0}
        in_specs.append(pl.BlockSpec(memory_space=pl.ANY))
        operands.append(out)
    return pl.pallas_call(
        functools.partial(join_kernel, heads),
        out_shape=jax.ShapeDtypeStruct((512, 1024), jnp.bfloat16),
        grid=(4,),
        in_specs=in_specs,
        out_specs=pl.BlockSpec((BLOCK, width), lambda b: (b, first_head // heads)),
        input_output_aliases=aliases,
        compiler_params=pltpu.CompilerParams(vmem_limit_bytes=VMEM_LIMIT),
        cost_estimate=pl.CostEstimate(
            flops=512 * width * 10, bytes_accessed=512 * width * 14, transcendentals=0
        ),
        name=f"join_{first_head}",
    )(*operands)


def shift(value, axis, step):
    size = lax.axis_size(axis)
    return lax.ppermute(value, axis, [(i, (i + step) % size) for i in range(size)])


def to_row(value, step):
    moves = [(i, i + step) for i in range(ROWS) if 0 <= i + step < ROWS]
    return lax.ppermute(value, "y", moves)


def swap(value, axis, bit):
    size = lax.axis_size(axis)
    return lax.ppermute(value, axis, [(i, i ^ bit) for i in range(size)])


def after(value, *others):
    return lax.optimization_barrier((value, *others))[0]


class Wire:
    def __init__(self, side, sign, depth=2):
        self.side, self.sign, self.depth = side, sign, depth
        self.sent = []

    def send(self, name, ring, distance, *others):
        source = ring[-self.sign * (distance - 1)]
        waits = list(others)
        if len(self.sent) >= self.depth:
            waits.append(self.sent[-self.depth])
        if waits:
            source = after(source, *waits)
        with jax.named_scope(f"{name}{distance}_{self.side}"):
            got = shift(source, "z", self.sign)
        self.sent.append(got)
        ring[-self.sign * distance if distance < 4 else 4] = got


def shards(query_states, key_states, value_states, gate_logits, selected_blocks):
    my_y, my_z = lax.axis_index("y"), lax.axis_index("z")
    gate_values = jax.nn.sigmoid(gate_logits.astype(jnp.float32))
    total = jnp.sum(gate_values, axis=1, keepdims=True)
    before = jnp.zeros_like(total)
    value_tiles = value_states.reshape(4, BLOCK, -1).transpose(0, 2, 1)
    va, vb = {0: value_tiles[:, : 4 * HEAD]}, {0: value_tiles[:, 4 * HEAD :]}
    right, left = Wire("right", 1), Wire("left", -1)
    for wire in (right, left):
        wire.send("va", va, 1)
    with jax.named_scope("prefix"):
        for bit in (1, 2, 4):
            other = swap(total, "z", bit)
            before = before + jnp.where((my_z & bit) != 0, other, 0.0)
            total = total + other
    for wire in (right, left):
        wire.send("vb", vb, 1, total)
    total = after(total, va[1], va[-1])
    for wire in (right, left):
        wire.send("va", va, 2)
    picks = selected_blocks.T.astype(jnp.float32)
    with jax.named_scope("prefix"):
        for bit in (1, 2):
            other = swap(jnp.concatenate([total, picks], axis=1), "y", bit)
            before = before + jnp.where((my_y & bit) != 0, other[:, :1], 0.0)
            total = total + other[:, :1]
            picks = jnp.concatenate([picks, other[:, 1:]], axis=1)
    for wire in (right, left):
        wire.send("vb", vb, 2)
    angles = before + jnp.cumsum(gate_values, axis=1)
    angles = after(angles, vb[1], vb[-1])
    query_rot, keys_a, keys_b = rotate(angles, query_states, key_states)
    ka, kb = {0: keys_a}, {0: keys_b}
    with jax.named_scope("queries"):
        queries = lax.all_gather(query_rot, "y")

    picks = picks.astype(jnp.int32).T.reshape(4, 1, 4, 8)
    wanted = (my_y + lax.broadcasted_iota(jnp.int32, (4, 4, 1, 1), 1)) ^ my_y
    turn = lax.broadcasted_iota(jnp.int32, (4, 4, 1, 1), 0)
    blocks = jnp.sum(jnp.where(wanted == turn, picks, 0), axis=0).reshape(16, 1, 8)
    row = lax.broadcasted_iota(jnp.int32, (16, RING, 8), 0)
    distance = lax.broadcasted_iota(jnp.int32, (16, RING, 8), 1)
    own = ((my_y + row // 4) * RING + my_z) * 4 + row % 4
    hit = (blocks >> 5 == my_y) & (((blocks >> 2) - my_z) & 7 == distance)
    hit &= (blocks != own) & (my_y + row // 4 < ROWS)
    code = jnp.where(distance == 0, 1 << (blocks & 3), (blocks & 3) + 1)
    meta = jnp.sum(jnp.where(hit, code, 0), axis=2).reshape(-1)
    meta = jnp.concatenate([meta, my_y.astype(jnp.int32)[None]])

    def call(part, group, state, last):
        offsets = []
        for distance in group:
            offsets += [distance] if distance in (0, 4) else [-distance, distance]
        keys, values = (ka, va) if part == 0 else (kb, vb)
        return attend(
            meta,
            queries,
            CHUNKS[part],
            tuple(offsets),
            [keys[o] for o in offsets],
            [values[o] for o in offsets],
            state,
            last,
        )

    def deliver(part, state, orders):
        parts = []
        for s in (1, 2, 3):
            packed = state[3][s - 1]
            if orders and parts:
                packed = after(packed, parts[-1])
            with jax.named_scope(f"partial{part}_{s}"):
                parts.append(to_row(packed, s))
        return parts

    for name, ring, distance in (("ka", ka, 1), ("va", va, 3), ("ka", ka, 2)):
        for wire in (right, left):
            wire.send(name, ring, distance)
    right.send("va", va, 4)
    left.send("kb", kb, 1)
    for wire in (right, left):
        wire.send("ka", ka, 3)
    state = call(0, GROUPS[0][0], None, False)
    right.send("kb", kb, 1, state[1])
    left.send("kb", kb, 2, state[1])
    right.send("ka", ka, 4, state[1])
    left.send("vb", vb, 3, state[1])
    right.send("kb", kb, 2)
    left.send("kb", kb, 3)
    state = call(0, GROUPS[0][1], state, True)
    right.send("vb", vb, 3, state[1])
    left.send("vb", vb, 4, state[1])
    right.send("kb", kb, 3, state[1])
    left.send("kb", kb, 4, state[1])
    mine_a, parts_a = state[:3], deliver(0, state, True)
    state = call(1, GROUPS[1][0], None, False)
    state[1] = after(state[1], parts_a[0])
    state = call(1, GROUPS[1][1], state, False)
    state[1] = after(state[1], parts_a[1])
    state = call(1, GROUPS[1][2], state, True)
    out = join(CHUNKS[0], mine_a, parts_a, None)
    return join(CHUNKS[1], state[:3], deliver(1, state, False), out)


def solution(mesh):
    grid = Mesh(mesh.devices.reshape(2, ROWS, RING, 4), ("dp", "y", "z", "head"))
    tokens = ("dp", "y", "z")
    placed = (
        P(tokens, "head"),
        P(tokens, "head"),
        P(tokens, "head"),
        P("head", tokens),
        P(tokens, None),
    )
    return jax.shard_map(
        shards, mesh=grid, in_specs=placed, out_specs=P(tokens, "head"), check_vma=False
    )
```

```python
import functools
import math

import jax
import jax.numpy as jnp
from jax import lax
from jax.experimental import pallas as pl
from jax.experimental.pallas import tpu as pltpu
from jax.sharding import Mesh, PartitionSpec as P

BLOCK = 128
HEAD = 128
ROWS = 4
RING = 8
NEG_FILL = -1e30
ROPE_BASE = 10000.0
VMEM_LIMIT = 24 << 20
ATTEND_VMEM = 60 << 20
IDLE = 4
STAT = 48
CHUNKS = ((0, 4), (4, 4))
GROUPS = (((0, 1, 2), (3, 4)), ((0, 1), (2, 3), (4,)))


QUARTER = (1.5703125, 4.837512969970703e-4, 7.54978995489188216e-8)


def sin_cos(phase):
    turns = jnp.floor(phase * (2 / math.pi) + 0.5)
    x = phase
    for part in QUARTER:
        x = x - turns * part
    square = x * x
    sine = ((-1.9515295891e-4 * square + 8.3321608736e-3) * square - 1.6666654611e-1) * square
    sine = sine * x + x
    cosine = ((2.443315711809948e-5 * square - 1.388731625493765e-3) * square + 4.166664568298827e-2)
    cosine = cosine * square * square - 0.5 * square + 1.0
    quadrant = turns.astype(jnp.int32) & 3
    odd = (quadrant & 1) == 1
    sine, cosine = jnp.where(odd, cosine, sine), jnp.where(odd, sine, cosine)
    sine = jnp.where(quadrant >= 2, -sine, sine)
    cosine = jnp.where((quadrant == 1) | (quadrant == 2), -cosine, cosine)
    return sine, cosine


def rotate_kernel(angle_ref, freq_ref, q_ref, k_ref, *outs):
    freq = freq_ref[...]
    lane = lax.broadcasted_iota(jnp.int32, (BLOCK, HEAD), 1)
    low = lane < HEAD // 2
    heads = q_ref.shape[1] // HEAD
    for pair in range(heads // 2):
        even = angle_ref[:, 2 * pair : 2 * pair + 1]
        odd = angle_ref[:, 2 * pair + 1 : 2 * pair + 2]
        sine, cosine = sin_cos(jnp.where(low, even, odd) * freq)
        sine_turned = pltpu.roll(sine, HEAD // 2, 1)
        cosine_turned = pltpu.roll(cosine, HEAD // 2, 1)
        for h in (2 * pair, 2 * pair + 1):
            first, second = (sine, sine_turned) if h % 2 == 0 else (sine_turned, sine)
            signed = jnp.where(low, -first, second)
            first, second = (cosine, cosine_turned) if h % 2 == 0 else (cosine_turned, cosine)
            plain = jnp.where(low, first, second)
            cols = slice(h * HEAD, (h + 1) * HEAD)

            def turn(x):
                x = x.astype(jnp.float32)
                return (x * plain + pltpu.roll(x, HEAD // 2, 1) * signed).astype(jnp.bfloat16)

            part = slice(h % 4 * HEAD, (h % 4 + 1) * HEAD)
            outs[0][:, cols] = turn(q_ref[:, cols])
            outs[1 + h // 4][0, part, :] = turn(k_ref[:, cols])


def rotate(angles, queries, keys):
    half = HEAD // 2
    inv_freq = ROPE_BASE ** (-jnp.arange(half).astype(jnp.float32) / half)
    inv_freq = jnp.concatenate([inv_freq, inv_freq])[None]
    heads = angles.shape[0]
    bf16 = jnp.bfloat16
    rows = pl.BlockSpec((BLOCK, heads * HEAD), lambda b: (b, 0))
    tiled = pl.BlockSpec((1, 4 * HEAD, BLOCK), lambda b: (b, 0, 0))
    return pl.pallas_call(
        rotate_kernel,
        out_shape=[
            jax.ShapeDtypeStruct(queries.shape, bf16),
            jax.ShapeDtypeStruct((4, 4 * HEAD, BLOCK), bf16),
            jax.ShapeDtypeStruct((4, 4 * HEAD, BLOCK), bf16),
        ],
        grid=(4,),
        in_specs=[
            pl.BlockSpec((BLOCK, heads), lambda b: (b, 0)),
            pl.BlockSpec((1, HEAD), lambda b: (0, 0)),
            rows,
            rows,
        ],
        out_specs=[rows, tiled, tiled],
        compiler_params=pltpu.CompilerParams(vmem_limit_bytes=VMEM_LIMIT),
        cost_estimate=pl.CostEstimate(flops=5 * 10**9, bytes_accessed=6 << 20, transcendentals=0),
        name="rotate",
    )(angles.T, inv_freq, queries, keys)


def attend_kernel(offsets, heads, first, last, meta, *refs):
    count = len(offsets)
    given_q, refs = refs[0], refs[1:]
    k_refs, v_refs = refs[:count], refs[count : 2 * count]
    rest = list(refs[2 * count :])
    acc, m_run, l_run, q_ref, k_all, v_all, todo = rest[-7:]
    rest = rest[:-7]
    given = None
    if not first:
        given, rest = rest[:3], rest[3:]
    r = pl.program_id(0)
    scale = HEAD**-0.5 * math.log2(math.e)

    @pl.when(r == 0)
    def _():
        def hold(kb, carry):
            for at in range(count):
                k_all[at, kb] = k_refs[at][kb]
                v_all[at, kb] = v_refs[at][kb]
            return carry

        lax.fori_loop(0, 4, hold, 0)
        q_ref[IDLE * BLOCK :, :] = jnp.zeros((BLOCK, heads * HEAD), jnp.bfloat16)
        acc[IDLE] = jnp.zeros((heads * HEAD, BLOCK), jnp.float32)
        m_run[IDLE] = jnp.full((8, BLOCK), NEG_FILL)
        l_run[IDLE] = jnp.zeros((8, BLOCK), jnp.float32)

    def enter(qb, carry):
        q_rows = pl.ds(pl.multiple_of(qb * BLOCK, BLOCK), BLOCK)
        q_ref[q_rows, :] = given_q[0, q_rows, :]
        if first:
            acc[qb] = jnp.zeros((heads * HEAD, BLOCK), jnp.float32)
            m_run[qb] = jnp.full((8, BLOCK), NEG_FILL)
            l_run[qb] = jnp.zeros((8, BLOCK), jnp.float32)
        else:
            acc[qb] = given[0][qb]
            m_run[qb] = given[1][qb]
            l_run[qb] = given[2][qb]
        return carry

    lax.fori_loop(0, 4, enter, 0)

    span = range(heads)
    cols = [slice(h * HEAD, (h + 1) * HEAD) for h in span]

    def two(items, causal):
        olds, scores = [], []
        for qb, at, kb in items:
            q_rows = pl.ds(pl.multiple_of(qb * BLOCK, BLOCK), BLOCK)
            olds.append((m_run[qb], l_run[qb]))
            scores.append(
                [
                    lax.dot_general(
                        k_all[at, kb, cols[h], :],
                        q_ref[q_rows, cols[h]],
                        (((1,), (1,)), ((), ())),
                        preferred_element_type=jnp.float32,
                    )
                    for h in span
                ]
            )
        if causal:
            key_pos = lax.broadcasted_iota(jnp.int32, (BLOCK, BLOCK), 0)
            query_pos = lax.broadcasted_iota(jnp.int32, (BLOCK, BLOCK), 1)
            seen = key_pos <= query_pos
            scores = [[jnp.where(seen, s, NEG_FILL) for s in group] for group in scores]
        results = []
        for (qb, at, kb), (m_old, l_old), group in zip(items, olds, scores):
            tops = [jnp.max(s, axis=0, keepdims=True) for s in group]
            if heads < 8:
                tops.append(m_old[heads:])
            m_new = jnp.maximum(m_old, jnp.concatenate(tops, axis=0))
            fade = jnp.exp2((m_old - m_new) * scale)
            weights = [jnp.exp2((group[h] - m_new[h : h + 1]) * scale) for h in span]
            sums = [jnp.sum(w, axis=0, keepdims=True) for w in weights]
            if heads < 8:
                sums.append(jnp.zeros((8 - heads, BLOCK), jnp.float32))
            mixed = [
                jnp.dot(
                    v_all[at, kb, cols[h], :],
                    weights[h].astype(jnp.bfloat16),
                    preferred_element_type=jnp.float32,
                )
                for h in span
            ]
            results.append((m_new, l_old * fade + jnp.concatenate(sums, axis=0), fade, mixed))
        wholes = [
            [acc[qb, cols[h], :] * fade[h : h + 1] + mixed[h] for h in span]
            for (qb, _, _), (_, _, fade, mixed) in zip(items, results)
        ]
        for (qb, _, _), (m_new, l_new, _, _), whole in zip(items, results, wholes):
            m_run[qb] = m_new
            l_run[qb] = l_new
            for h in span:
                acc[qb, cols[h], :] = whole[h]

    if 0 in offsets:
        here = offsets.index(0)

        @pl.when(r == 0)
        def _():
            def own(i, carry):
                two([(2 * i, here, 2 * i), (2 * i + 1, here, 2 * i + 1)], True)
                return carry

            lax.fori_loop(0, 2, own, 0)

    def note(at, choice, offset, qb, length, newest):
        code = meta[(r * 4 + qb) * RING + offset % RING]
        if offset == 0:
            valid, kb = (code >> choice) & 1, choice
        else:
            valid, kb = (code > 0).astype(jnp.int32), jnp.maximum(code - 1, 0)
        item = qb + at * 16 + kb * 256
        clash = valid & length & (newest == qb).astype(jnp.int32)
        todo[length] = jnp.where(clash == 1, IDLE, item)
        todo[length + 1] = item
        return length + valid * (1 + clash), jnp.where(valid == 1, qb, newest)

    found = (jnp.int32(0), jnp.int32(-1))
    for at, offset in enumerate(offsets):
        if offset == 0:
            found = lax.fori_loop(
                0, 16, lambda i, f, at=at: note(at, i >> 2, 0, i & 3, *f), found
            )
        else:
            found = lax.fori_loop(
                0, 4, lambda i, f, at=at, offset=offset: note(at, 0, offset, i, *f), found
            )
    length = found[0]
    todo[length] = IDLE

    def step(i, carry):
        items = []
        for side in (0, 1):
            item = todo[2 * i + side]
            items.append((item & 15, (item >> 4) & 15, item >> 8))
        two(items, False)
        return carry

    lax.fori_loop(0, (length + 1) >> 1, step, 0)

    def leave(acc_out, m_out, l_out):
        def copy(qb, carry):
            acc_out[qb] = acc[qb]
            m_out[qb] = m_run[qb]
            l_out[qb] = l_run[qb]
            return carry

        lax.fori_loop(0, 4, copy, 0)

    if not last:
        leave(*rest)
    else:
        packed_ref = rest[3]

        @pl.when(r == 0)
        def _():
            leave(*rest[:3])

        @pl.when(r > 0)
        def _():
            def pack(qb, carry):
                pieces = []
                for value in (m_run[qb], l_run[qb]):
                    for _ in range(3):
                        piece = value.astype(jnp.bfloat16).astype(jnp.float32)
                        pieces.append(piece)
                        value = value - piece
                packed_ref[0, qb, heads * HEAD :, :] = jnp.concatenate(pieces, axis=0).astype(
                    jnp.bfloat16
                )
                total = l_run[qb]
                inverse = 1.0 / jnp.where(total > 0, total, 1.0)
                for h in span:
                    packed_ref[0, qb, cols[h], :] = (
                        acc[qb, cols[h], :] * inverse[h : h + 1]
                    ).astype(jnp.bfloat16)
                return carry

            lax.fori_loop(0, 4, pack, 0)


def attend(meta, queries, chunk, offsets, keys, values, state, last):
    first_head, heads = chunk
    width = heads * HEAD
    first = state is None
    acc_spec = pl.BlockSpec((4, width, BLOCK), lambda r, meta: (r, 0, 0))
    run_spec = pl.BlockSpec((4, 8, BLOCK), lambda r, meta: (r, 0, 0))
    state_specs = [acc_spec, run_spec, run_spec]
    in_specs = [
        pl.BlockSpec(
            (1, 512, width),
            lambda r, meta: (jnp.minimum(meta[16 * RING] + r, ROWS - 1), 0, first_head // heads),
        )
    ]
    in_specs += [pl.BlockSpec((4, width, BLOCK), lambda r, meta: (0, 0, 0))] * (2 * len(offsets))
    operands = [queries, *keys, *values]
    if not first:
        in_specs += state_specs
        operands += list(state)
    f32 = jnp.float32
    if last:
        out_shape = [
            jax.ShapeDtypeStruct((4, width, BLOCK), f32),
            jax.ShapeDtypeStruct((4, 8, BLOCK), f32),
            jax.ShapeDtypeStruct((4, 8, BLOCK), f32),
            jax.ShapeDtypeStruct((ROWS, 4, width + STAT, BLOCK), jnp.bfloat16),
        ]
        out_specs = [
            pl.BlockSpec((4, width, BLOCK), lambda r, meta: (0, 0, 0)),
            pl.BlockSpec((4, 8, BLOCK), lambda r, meta: (0, 0, 0)),
            pl.BlockSpec((4, 8, BLOCK), lambda r, meta: (0, 0, 0)),
            pl.BlockSpec((1, 4, width + STAT, BLOCK), lambda r, meta: ((meta[16 * RING] + jnp.maximum(r, 1)) & 3, 0, 0, 0)),
        ]
    else:
        out_shape = [
            jax.ShapeDtypeStruct((16, width, BLOCK), f32),
            jax.ShapeDtypeStruct((16, 8, BLOCK), f32),
            jax.ShapeDtypeStruct((16, 8, BLOCK), f32),
        ]
        out_specs = state_specs
    count = len(offsets)
    scratch = [
        pltpu.VMEM((5, width, BLOCK), f32),
        pltpu.VMEM((5, 8, BLOCK), f32),
        pltpu.VMEM((5, 8, BLOCK), f32),
        pltpu.VMEM((5 * BLOCK, width), jnp.bfloat16),
        pltpu.VMEM((count, 4, width, BLOCK), jnp.bfloat16),
        pltpu.VMEM((count, 4, width, BLOCK), jnp.bfloat16),
        pltpu.SMEM((80,), jnp.int32),
    ]
    return list(pl.pallas_call(
        functools.partial(attend_kernel, offsets, heads, first, last),
        out_shape=out_shape,
        grid_spec=pltpu.PrefetchScalarGridSpec(
            num_scalar_prefetch=1,
            grid=(ROWS,),
            in_specs=in_specs,
            out_specs=out_specs,
            scratch_shapes=scratch,
        ),
        compiler_params=pltpu.CompilerParams(vmem_limit_bytes=ATTEND_VMEM),
        cost_estimate=pl.CostEstimate(
            flops=int((2 + 3 * len(offsets)) * 1.1e9),
            bytes_accessed=1 << 20,
            transcendentals=0,
        ),
        name=f"attend_{first_head}_{'_'.join(str(o % RING) for o in offsets)}",
    )(meta, *operands))


def join_kernel(heads, acc_ref, m_ref, l_ref, one, two, three, *rest):
    out_ref = rest[-1]
    width = heads * HEAD
    tops, sums = [m_ref[0]], [l_ref[0]]
    for part in (one, two, three):
        stats = part[0, width:, :].astype(jnp.float32)
        top = (stats[16:24] + stats[8:16]) + stats[0:8]
        total = (stats[40:48] + stats[32:40]) + stats[24:32]
        tops.append(jnp.where(total > 0, top, NEG_FILL))
        sums.append(total)
    scale = HEAD**-0.5 * math.log2(math.e)
    highest = jnp.maximum(jnp.maximum(tops[0], tops[1]), jnp.maximum(tops[2], tops[3]))
    fades = [jnp.exp2((top - highest) * scale) for top in tops]
    shares = [fades[0]] + [fades[i] * sums[i] for i in (1, 2, 3)]
    whole = fades[0] * sums[0] + shares[1] + shares[2] + shares[3]
    inverse = 1.0 / whole
    for h in range(heads):
        cols = slice(h * HEAD, (h + 1) * HEAD)
        mixed = acc_ref[0, cols, :] * shares[0][h : h + 1, :]
        for i, part in enumerate((one, two, three)):
            mixed += part[0, cols, :].astype(jnp.float32) * shares[i + 1][h : h + 1, :]
        mixed = mixed * inverse[h : h + 1, :]
        out_ref[:, cols] = mixed.T.astype(jnp.bfloat16)


def join(chunk, state, parts, out):
    first_head, heads = chunk
    width = heads * HEAD
    in_specs = [
        pl.BlockSpec((1, width, BLOCK), lambda b: (b, 0, 0)),
        pl.BlockSpec((1, 8, BLOCK), lambda b: (b, 0, 0)),
        pl.BlockSpec((1, 8, BLOCK), lambda b: (b, 0, 0)),
    ] + [pl.BlockSpec((1, width + STAT, BLOCK), lambda b: (b, 0, 0))] * 3
    operands = [*state, *parts]
    aliases = {}
    if out is not None:
        aliases = {len(operands): 0}
        in_specs.append(pl.BlockSpec(memory_space=pl.ANY))
        operands.append(out)
    return pl.pallas_call(
        functools.partial(join_kernel, heads),
        out_shape=jax.ShapeDtypeStruct((512, 1024), jnp.bfloat16),
        grid=(4,),
        in_specs=in_specs,
        out_specs=pl.BlockSpec((BLOCK, width), lambda b: (b, first_head // heads)),
        input_output_aliases=aliases,
        compiler_params=pltpu.CompilerParams(vmem_limit_bytes=VMEM_LIMIT),
        cost_estimate=pl.CostEstimate(
            flops=512 * width * 10, bytes_accessed=512 * width * 14, transcendentals=0
        ),
        name=f"join_{first_head}",
    )(*operands)


def shift(value, axis, step):
    size = lax.axis_size(axis)
    return lax.ppermute(value, axis, [(i, (i + step) % size) for i in range(size)])


def to_row(value, step):
    moves = [(i, i + step) for i in range(ROWS) if 0 <= i + step < ROWS]
    return lax.ppermute(value, "y", moves)


def swap(value, axis, bit):
    size = lax.axis_size(axis)
    return lax.ppermute(value, axis, [(i, i ^ bit) for i in range(size)])


def after(value, *others):
    return lax.optimization_barrier((value, *others))[0]


class Wire:
    def __init__(self, side, sign, depth=2):
        self.side, self.sign, self.depth = side, sign, depth
        self.sent = []

    def send(self, name, ring, distance, *others):
        source = ring[-self.sign * (distance - 1)]
        waits = list(others)
        waits += self.sent[-self.depth - 1 : -self.depth + 1] if self.sent[1:] else []
        if waits:
            source = after(source, *waits)
        with jax.named_scope(f"{name}{distance}_{self.side}"):
            got = shift(source, "z", self.sign)
        self.sent.append(got)
        ring[-self.sign * distance if distance < 4 else 4] = got


def shards(query_states, key_states, value_states, gate_logits, selected_blocks):
    my_y, my_z = lax.axis_index("y"), lax.axis_index("z")
    gate_values = jax.nn.sigmoid(gate_logits.astype(jnp.float32))
    total = jnp.sum(gate_values, axis=1, keepdims=True)
    before = jnp.zeros_like(total)
    value_tiles = value_states.reshape(4, BLOCK, -1).transpose(0, 2, 1)
    va, vb = {0: value_tiles[:, : 4 * HEAD]}, {0: value_tiles[:, 4 * HEAD :]}
    picks = selected_blocks.T.astype(jnp.float32)
    with jax.named_scope("prefix"):
        rows_before = before
        for bit in (1, 2):
            other = swap(jnp.concatenate([total, rows_before, picks], axis=1), "y", bit)
            if bit == 1:
                own_total = total
            rows_before = rows_before + jnp.where((my_y & bit) != 0, other[:, :1], 0.0)
            total = total + other[:, :1]
            picks = jnp.concatenate([picks, other[:, 2:]], axis=1)
        for bit in (1, 2, 4):
            other = swap(jnp.concatenate([own_total, rows_before], axis=1), "z", bit)
            before = before + jnp.where((my_z & bit) != 0, other[:, :1], 0.0)
            own_total = own_total + other[:, :1]
            rows_before = rows_before + other[:, 1:]
    angles = before + rows_before + jnp.cumsum(gate_values, axis=1)
    query_rot, keys_a, keys_b = rotate(angles, query_states, key_states)
    ka, kb = {0: keys_a}, {0: keys_b}
    with jax.named_scope("queries"):
        copies = jnp.broadcast_to(query_rot[None], (ROWS, *query_rot.shape))
        queries = lax.all_to_all(copies, "y", 0, 0, tiled=True)

    picks = picks.astype(jnp.int32).T.reshape(4, 1, 4, 8)
    wanted = (my_y + lax.broadcasted_iota(jnp.int32, (4, 4, 1, 1), 1)) ^ my_y
    turn = lax.broadcasted_iota(jnp.int32, (4, 4, 1, 1), 0)
    blocks = jnp.sum(jnp.where(wanted == turn, picks, 0), axis=0).reshape(16, 1, 8)
    row = lax.broadcasted_iota(jnp.int32, (16, RING, 8), 0)
    distance = lax.broadcasted_iota(jnp.int32, (16, RING, 8), 1)
    own = ((my_y + row // 4) * RING + my_z) * 4 + row % 4
    hit = (blocks >> 5 == my_y) & (((blocks >> 2) - my_z) & 7 == distance)
    hit &= (blocks != own) & (my_y + row // 4 < ROWS)
    code = jnp.where(distance == 0, 1 << (blocks & 3), (blocks & 3) + 1)
    meta = jnp.sum(jnp.where(hit, code, 0), axis=2).reshape(-1)
    meta = jnp.concatenate([meta, my_y.astype(jnp.int32)[None]])

    def call(part, group, state, last):
        offsets = []
        for distance in group:
            offsets += [distance] if distance in (0, 4) else [-distance, distance]
        keys, values = (ka, va) if part == 0 else (kb, vb)
        return attend(
            meta,
            queries,
            CHUNKS[part],
            tuple(offsets),
            [keys[o] for o in offsets],
            [values[o] for o in offsets],
            state,
            last,
        )

    def pick(rows, step):
        return lax.dynamic_index_in_dim(rows, (my_y + step) & 3, 0, keepdims=False)

    right, left = Wire("right", 1), Wire("left", -1)
    for distance in (1, 2):
        for name, ring in (("va", va), ("ka", ka)):
            for wire in (right, left):
                wire.send(name, ring, distance)
    for wire in (right, left):
        wire.send("va", va, 3)
        wire.send("ka", ka, 3)
    state = call(0, GROUPS[0][0], None, False)
    right.send("va", va, 4)
    left.send("vb", vb, 1)
    right.send("ka", ka, 4, state[1])
    left.send("kb", kb, 1, state[1])
    right.send("vb", vb, 1)
    left.send("vb", vb, 2)
    right.send("kb", kb, 1)
    left.send("kb", kb, 2)
    state = call(0, GROUPS[0][1], state, True)
    right.send("vb", vb, 2)
    left.send("vb", vb, 3)
    right.send("kb", kb, 2, state[1])
    left.send("kb", kb, 3, state[1])
    first_b = call(1, GROUPS[1][0], None, False)
    right.send("vb", vb, 3)
    left.send("vb", vb, 4)
    right.send("kb", kb, 3, first_b[1])
    left.send("kb", kb, 4, first_b[1])
    mine_a = state[:3]
    with jax.named_scope("partials_a"):
        parts_a = lax.all_to_all(state[3], "y", 0, 0, tiled=True)
    first_b[1] = after(first_b[1], parts_a)
    state = call(1, GROUPS[1][1], first_b, False)
    state = call(1, GROUPS[1][2], state, True)
    parts_b = []
    for s in (1, 2, 3):
        with jax.named_scope(f"partial_b{s}"):
            parts_b.append(to_row(pick(state[3], s), s))
    parts_a = after(parts_a, state[1])
    out = join(CHUNKS[0], mine_a, [pick(parts_a, -s) for s in (1, 2, 3)], None)
    return join(CHUNKS[1], state[:3], parts_b, out)


def solution(mesh):
    grid = Mesh(mesh.devices.reshape(2, ROWS, RING, 4), ("dp", "y", "z", "head"))
    tokens = ("dp", "y", "z")
    placed = (
        P(tokens, "head"),
        P(tokens, "head"),
        P(tokens, "head"),
        P("head", tokens),
        P(tokens, None),
    )
    return jax.shard_map(
        shards, mesh=grid, in_specs=placed, out_specs=P(tokens, "head"), check_vma=False
    )
```

```python
import functools
import math

import jax
import jax.numpy as jnp
from jax import lax
from jax.experimental import pallas as pl
from jax.experimental.pallas import tpu as pltpu
from jax.sharding import Mesh, PartitionSpec as P

BLOCK = 128
HEAD = 128
ROWS = 4
RING = 8
NEG_FILL = -1e30
ROPE_BASE = 10000.0
VMEM_LIMIT = 24 << 20
IDLE = 4
STAT = 48
CHUNKS = ((0, 4), (4, 4))
GROUPS = (((0, 1, 2), (3, 4)), ((0, 1), (2, 3), (4,)))


QUARTER = (1.5703125, 4.837512969970703e-4, 7.54978995489188216e-8)


def sin_cos(phase):
    turns = jnp.floor(phase * (2 / math.pi) + 0.5)
    x = phase
    for part in QUARTER:
        x = x - turns * part
    square = x * x
    sine = ((-1.9515295891e-4 * square + 8.3321608736e-3) * square - 1.6666654611e-1) * square
    sine = sine * x + x
    cosine = ((2.443315711809948e-5 * square - 1.388731625493765e-3) * square + 4.166664568298827e-2)
    cosine = cosine * square * square - 0.5 * square + 1.0
    quadrant = turns.astype(jnp.int32) & 3
    odd = (quadrant & 1) == 1
    sine, cosine = jnp.where(odd, cosine, sine), jnp.where(odd, sine, cosine)
    sine = jnp.where(quadrant >= 2, -sine, sine)
    cosine = jnp.where((quadrant == 1) | (quadrant == 2), -cosine, cosine)
    return sine, cosine


def rotate_kernel(angle_ref, freq_ref, q_ref, k_ref, *outs):
    freq = freq_ref[...]
    lane = lax.broadcasted_iota(jnp.int32, (BLOCK, HEAD), 1)
    low = lane < HEAD // 2
    heads = q_ref.shape[1] // HEAD
    for pair in range(heads // 2):
        even = angle_ref[:, 2 * pair : 2 * pair + 1]
        odd = angle_ref[:, 2 * pair + 1 : 2 * pair + 2]
        sine, cosine = sin_cos(jnp.where(low, even, odd) * freq)
        sine_turned = pltpu.roll(sine, HEAD // 2, 1)
        cosine_turned = pltpu.roll(cosine, HEAD // 2, 1)
        for h in (2 * pair, 2 * pair + 1):
            first, second = (sine, sine_turned) if h % 2 == 0 else (sine_turned, sine)
            signed = jnp.where(low, -first, second)
            first, second = (cosine, cosine_turned) if h % 2 == 0 else (cosine_turned, cosine)
            plain = jnp.where(low, first, second)
            cols = slice(h * HEAD, (h + 1) * HEAD)

            def turn(x):
                x = x.astype(jnp.float32)
                return (x * plain + pltpu.roll(x, HEAD // 2, 1) * signed).astype(jnp.bfloat16)

            part = slice(h % 4 * HEAD, (h % 4 + 1) * HEAD)
            query = turn(q_ref[:, cols])
            for row in range(ROWS):
                outs[0][row, :, cols] = query
            outs[1 + h // 4][0, part, :] = turn(k_ref[:, cols])


def rotate(angles, queries, keys):
    half = HEAD // 2
    inv_freq = ROPE_BASE ** (-jnp.arange(half).astype(jnp.float32) / half)
    inv_freq = jnp.concatenate([inv_freq, inv_freq])[None]
    heads = angles.shape[0]
    bf16 = jnp.bfloat16
    rows = pl.BlockSpec((BLOCK, heads * HEAD), lambda b: (b, 0))
    copies = pl.BlockSpec((ROWS, BLOCK, heads * HEAD), lambda b: (0, b, 0))
    tiled = pl.BlockSpec((1, 4 * HEAD, BLOCK), lambda b: (b, 0, 0))
    return pl.pallas_call(
        rotate_kernel,
        out_shape=[
            jax.ShapeDtypeStruct((ROWS, *queries.shape), bf16),
            jax.ShapeDtypeStruct((4, 4 * HEAD, BLOCK), bf16),
            jax.ShapeDtypeStruct((4, 4 * HEAD, BLOCK), bf16),
        ],
        grid=(4,),
        in_specs=[
            pl.BlockSpec((BLOCK, heads), lambda b: (b, 0)),
            pl.BlockSpec((1, HEAD), lambda b: (0, 0)),
            rows,
            rows,
        ],
        out_specs=[copies, tiled, tiled],
        compiler_params=pltpu.CompilerParams(vmem_limit_bytes=VMEM_LIMIT),
        cost_estimate=pl.CostEstimate(flops=5 * 10**9, bytes_accessed=6 << 20, transcendentals=0),
        name="rotate",
    )(angles.T, inv_freq, queries, keys)


def attend_kernel(offsets, heads, first, last, meta, *refs):
    count = len(offsets)
    given_q, refs = refs[0], refs[1:]
    k_refs, v_refs = refs[:count], refs[count : 2 * count]
    rest = list(refs[2 * count :])
    acc, m_run, l_run, q_ref, k_all, v_all, todo = rest[-7:]
    rest = rest[:-7]
    given = None
    if not first:
        given, rest = rest[:3], rest[3:]
    r = pl.program_id(0)
    scale = HEAD**-0.5 * math.log2(math.e)

    @pl.when(r == 0)
    def _():
        def hold(kb, carry):
            for at in range(count):
                k_all[at, kb] = k_refs[at][kb]
                v_all[at, kb] = v_refs[at][kb]
            return carry

        lax.fori_loop(0, 4, hold, 0)
        q_ref[IDLE * BLOCK :, :] = jnp.zeros((BLOCK, heads * HEAD), jnp.bfloat16)
        acc[IDLE] = jnp.zeros((heads * HEAD, BLOCK), jnp.float32)
        m_run[IDLE] = jnp.full((8, BLOCK), NEG_FILL)
        l_run[IDLE] = jnp.zeros((8, BLOCK), jnp.float32)

    def enter(qb, carry):
        q_rows = pl.ds(pl.multiple_of(qb * BLOCK, BLOCK), BLOCK)
        q_ref[q_rows, :] = given_q[0, q_rows, :]
        if first:
            acc[qb] = jnp.zeros((heads * HEAD, BLOCK), jnp.float32)
            m_run[qb] = jnp.full((8, BLOCK), NEG_FILL)
            l_run[qb] = jnp.zeros((8, BLOCK), jnp.float32)
        else:
            acc[qb] = given[0][qb]
            m_run[qb] = given[1][qb]
            l_run[qb] = given[2][qb]
        return carry

    lax.fori_loop(0, 4, enter, 0)

    span = range(heads)
    cols = [slice(h * HEAD, (h + 1) * HEAD) for h in span]

    def two(items, causal):
        olds, scores = [], []
        for qb, at, kb in items:
            q_rows = pl.ds(pl.multiple_of(qb * BLOCK, BLOCK), BLOCK)
            olds.append((m_run[qb], l_run[qb]))
            scores.append(
                [
                    lax.dot_general(
                        k_all[at, kb, cols[h], :],
                        q_ref[q_rows, cols[h]],
                        (((1,), (1,)), ((), ())),
                        preferred_element_type=jnp.float32,
                    )
                    for h in span
                ]
            )
        if causal:
            key_pos = lax.broadcasted_iota(jnp.int32, (BLOCK, BLOCK), 0)
            query_pos = lax.broadcasted_iota(jnp.int32, (BLOCK, BLOCK), 1)
            seen = key_pos <= query_pos
            scores = [[jnp.where(seen, s, NEG_FILL) for s in group] for group in scores]
        results = []
        for (qb, at, kb), (m_old, l_old), group in zip(items, olds, scores):
            tops = [jnp.max(s, axis=0, keepdims=True) for s in group]
            if heads < 8:
                tops.append(m_old[heads:])
            m_new = jnp.maximum(m_old, jnp.concatenate(tops, axis=0))
            fade = jnp.exp2((m_old - m_new) * scale)
            weights = [jnp.exp2((group[h] - m_new[h : h + 1]) * scale) for h in span]
            sums = [jnp.sum(w, axis=0, keepdims=True) for w in weights]
            if heads < 8:
                sums.append(jnp.zeros((8 - heads, BLOCK), jnp.float32))
            mixed = [
                jnp.dot(
                    v_all[at, kb, cols[h], :],
                    weights[h].astype(jnp.bfloat16),
                    preferred_element_type=jnp.float32,
                )
                for h in span
            ]
            results.append((m_new, l_old * fade + jnp.concatenate(sums, axis=0), fade, mixed))
        wholes = [
            [acc[qb, cols[h], :] * fade[h : h + 1] + mixed[h] for h in span]
            for (qb, _, _), (_, _, fade, mixed) in zip(items, results)
        ]
        for (qb, _, _), (m_new, l_new, _, _), whole in zip(items, results, wholes):
            m_run[qb] = m_new
            l_run[qb] = l_new
            for h in span:
                acc[qb, cols[h], :] = whole[h]

    if 0 in offsets:
        here = offsets.index(0)

        @pl.when(r == 0)
        def _():
            def own(i, carry):
                two([(2 * i, here, 2 * i), (2 * i + 1, here, 2 * i + 1)], True)
                return carry

            lax.fori_loop(0, 2, own, 0)

    def note(at, choice, offset, qb, length, newest):
        code = meta[(r * 4 + qb) * RING + offset % RING]
        if offset == 0:
            valid, kb = (code >> choice) & 1, choice
        else:
            valid, kb = (code > 0).astype(jnp.int32), jnp.maximum(code - 1, 0)
        item = qb + at * 16 + kb * 256
        clash = valid & length & (newest == qb).astype(jnp.int32)
        todo[length] = jnp.where(clash == 1, IDLE, item)
        todo[length + 1] = item
        return length + valid * (1 + clash), jnp.where(valid == 1, qb, newest)

    found = (jnp.int32(0), jnp.int32(-1))
    for at, offset in enumerate(offsets):
        if offset == 0:
            found = lax.fori_loop(
                0, 16, lambda i, f, at=at: note(at, i >> 2, 0, i & 3, *f), found
            )
        else:
            found = lax.fori_loop(
                0, 4, lambda i, f, at=at, offset=offset: note(at, 0, offset, i, *f), found
            )
    length = found[0]
    todo[length] = IDLE

    def step(i, carry):
        items = []
        for side in (0, 1):
            item = todo[2 * i + side]
            items.append((item & 15, (item >> 4) & 15, item >> 8))
        two(items, False)
        return carry

    lax.fori_loop(0, (length + 1) >> 1, step, 0)

    def leave(acc_out, m_out, l_out):
        def copy(qb, carry):
            acc_out[qb] = acc[qb]
            m_out[qb] = m_run[qb]
            l_out[qb] = l_run[qb]
            return carry

        lax.fori_loop(0, 4, copy, 0)

    if not last:
        leave(*rest)
    else:
        packed_refs = rest[3:]

        @pl.when(r == 0)
        def _():
            leave(*rest[:3])

        def send(packed_ref, lead):
            def pack(qb, carry):
                pieces = []
                for value in (m_run[qb], l_run[qb]):
                    for _ in range(3):
                        piece = value.astype(jnp.bfloat16).astype(jnp.float32)
                        pieces.append(piece)
                        value = value - piece
                packed_ref[(*lead, qb, slice(heads * HEAD, None), slice(None))] = jnp.concatenate(pieces, axis=0).astype(
                    jnp.bfloat16
                )
                total = l_run[qb]
                inverse = 1.0 / jnp.where(total > 0, total, 1.0)
                for h in span:
                    packed_ref[(*lead, qb, cols[h], slice(None))] = (
                        acc[qb, cols[h], :] * inverse[h : h + 1]
                    ).astype(jnp.bfloat16)
                return carry

            lax.fori_loop(0, 4, pack, 0)

        if len(packed_refs) == 1:
            pl.when(r > 0)(lambda: send(packed_refs[0], (0,)))
        else:
            for row, packed_ref in enumerate(packed_refs):
                pl.when(r == row + 1)(functools.partial(send, packed_ref, ()))


def attend(meta, queries, chunk, offsets, keys, values, state, last):
    first_head, heads = chunk
    apart = first_head > 0
    width = heads * HEAD
    first = state is None
    acc_spec = pl.BlockSpec((4, width, BLOCK), lambda r, meta: (r, 0, 0))
    run_spec = pl.BlockSpec((4, 8, BLOCK), lambda r, meta: (r, 0, 0))
    state_specs = [acc_spec, run_spec, run_spec]
    in_specs = [
        pl.BlockSpec(
            (1, 512, width),
            lambda r, meta: (jnp.minimum(meta[16 * RING] + r, ROWS - 1), 0, first_head // heads),
        )
    ]
    in_specs += [pl.BlockSpec((4, width, BLOCK), lambda r, meta: (0, 0, 0))] * (2 * len(offsets))
    operands = [queries, *keys, *values]
    if not first:
        in_specs += state_specs
        operands += list(state)
    f32 = jnp.float32
    if last:
        out_shape = [
            jax.ShapeDtypeStruct((4, width, BLOCK), f32),
            jax.ShapeDtypeStruct((4, 8, BLOCK), f32),
            jax.ShapeDtypeStruct((4, 8, BLOCK), f32),
            *(
                [jax.ShapeDtypeStruct((4, width + STAT, BLOCK), jnp.bfloat16)] * 3
                if apart
                else [jax.ShapeDtypeStruct((ROWS, 4, width + STAT, BLOCK), jnp.bfloat16)]
            ),
        ]
        out_specs = [
            pl.BlockSpec((4, width, BLOCK), lambda r, meta: (0, 0, 0)),
            pl.BlockSpec((4, 8, BLOCK), lambda r, meta: (0, 0, 0)),
            pl.BlockSpec((4, 8, BLOCK), lambda r, meta: (0, 0, 0)),
            *(
                [pl.BlockSpec((4, width + STAT, BLOCK), lambda r, meta: (0, 0, 0))] * 3
                if apart
                else [            pl.BlockSpec((1, 4, width + STAT, BLOCK), lambda r, meta: ((meta[16 * RING] + jnp.maximum(r, 1)) & 3, 0, 0, 0))]
            ),
        ]
    else:
        out_shape = [
            jax.ShapeDtypeStruct((16, width, BLOCK), f32),
            jax.ShapeDtypeStruct((16, 8, BLOCK), f32),
            jax.ShapeDtypeStruct((16, 8, BLOCK), f32),
        ]
        out_specs = state_specs
    count = len(offsets)
    scratch = [
        pltpu.VMEM((5, width, BLOCK), f32),
        pltpu.VMEM((5, 8, BLOCK), f32),
        pltpu.VMEM((5, 8, BLOCK), f32),
        pltpu.VMEM((5 * BLOCK, width), jnp.bfloat16),
        pltpu.VMEM((count, 4, width, BLOCK), jnp.bfloat16),
        pltpu.VMEM((count, 4, width, BLOCK), jnp.bfloat16),
        pltpu.SMEM((80,), jnp.int32),
    ]
    return list(pl.pallas_call(
        functools.partial(attend_kernel, offsets, heads, first, last),
        out_shape=out_shape,
        grid_spec=pltpu.PrefetchScalarGridSpec(
            num_scalar_prefetch=1,
            grid=(ROWS,),
            in_specs=in_specs,
            out_specs=out_specs,
            scratch_shapes=scratch,
        ),
        compiler_params=pltpu.CompilerParams(vmem_limit_bytes=VMEM_LIMIT),
        cost_estimate=pl.CostEstimate(
            flops=int((2 + 3 * len(offsets)) * 1.1e9),
            bytes_accessed=1 << 20,
            transcendentals=0,
        ),
        name=f"attend_{first_head}_{'_'.join(str(o % RING) for o in offsets)}",
    )(meta, *operands))


def join_kernel(heads, acc_ref, m_ref, l_ref, one, two, three, *rest):
    out_ref = rest[-1]
    width = heads * HEAD
    tops, sums = [m_ref[0]], [l_ref[0]]
    for part in (one, two, three):
        stats = part[0, width:, :].astype(jnp.float32)
        top = (stats[16:24] + stats[8:16]) + stats[0:8]
        total = (stats[40:48] + stats[32:40]) + stats[24:32]
        tops.append(jnp.where(total > 0, top, NEG_FILL))
        sums.append(total)
    scale = HEAD**-0.5 * math.log2(math.e)
    highest = jnp.maximum(jnp.maximum(tops[0], tops[1]), jnp.maximum(tops[2], tops[3]))
    fades = [jnp.exp2((top - highest) * scale) for top in tops]
    shares = [fades[0]] + [fades[i] * sums[i] for i in (1, 2, 3)]
    whole = fades[0] * sums[0] + shares[1] + shares[2] + shares[3]
    inverse = 1.0 / whole
    for h in range(heads):
        cols = slice(h * HEAD, (h + 1) * HEAD)
        mixed = acc_ref[0, cols, :] * shares[0][h : h + 1, :]
        for i, part in enumerate((one, two, three)):
            mixed += part[0, cols, :].astype(jnp.float32) * shares[i + 1][h : h + 1, :]
        mixed = mixed * inverse[h : h + 1, :]
        out_ref[:, cols] = mixed.T.astype(jnp.bfloat16)


def join(chunk, state, parts, out):
    first_head, heads = chunk
    width = heads * HEAD
    in_specs = [
        pl.BlockSpec((1, width, BLOCK), lambda b: (b, 0, 0)),
        pl.BlockSpec((1, 8, BLOCK), lambda b: (b, 0, 0)),
        pl.BlockSpec((1, 8, BLOCK), lambda b: (b, 0, 0)),
    ] + [pl.BlockSpec((1, width + STAT, BLOCK), lambda b: (b, 0, 0))] * 3
    operands = [*state, *parts]
    aliases = {}
    if out is not None:
        aliases = {len(operands): 0}
        in_specs.append(pl.BlockSpec(memory_space=pl.ANY))
        operands.append(out)
    return pl.pallas_call(
        functools.partial(join_kernel, heads),
        out_shape=jax.ShapeDtypeStruct((512, 1024), jnp.bfloat16),
        grid=(4,),
        in_specs=in_specs,
        out_specs=pl.BlockSpec((BLOCK, width), lambda b: (b, first_head // heads)),
        input_output_aliases=aliases,
        compiler_params=pltpu.CompilerParams(vmem_limit_bytes=VMEM_LIMIT),
        cost_estimate=pl.CostEstimate(
            flops=512 * width * 10, bytes_accessed=512 * width * 14, transcendentals=0
        ),
        name=f"join_{first_head}",
    )(*operands)


def shift(value, axis, step):
    size = lax.axis_size(axis)
    return lax.ppermute(value, axis, [(i, (i + step) % size) for i in range(size)])


def to_row(value, step):
    moves = [(i, i + step) for i in range(ROWS) if 0 <= i + step < ROWS]
    return lax.ppermute(value, "y", moves)


def swap(value, axis, bit):
    size = lax.axis_size(axis)
    return lax.ppermute(value, axis, [(i, i ^ bit) for i in range(size)])


def after(value, *others):
    return lax.optimization_barrier((value, *others))[0]


class Wire:
    def __init__(self, side, sign, depth=2):
        self.side, self.sign, self.depth = side, sign, depth
        self.sent = []

    def send(self, name, ring, distance, *others):
        source = ring[-self.sign * (distance - 1)]
        waits = list(others)
        waits += self.sent[-self.depth - 1 : -self.depth + 1] if self.sent[1:] else []
        if waits:
            source = after(source, *waits)
        with jax.named_scope(f"{name}{distance}_{self.side}"):
            got = shift(source, "z", self.sign)
        self.sent.append(got)
        ring[-self.sign * distance if distance < 4 else 4] = got


def shards(query_states, key_states, value_states, gate_logits, selected_blocks):
    my_y, my_z = lax.axis_index("y"), lax.axis_index("z")
    gate_values = jax.nn.sigmoid(gate_logits.astype(jnp.float32))
    total = jnp.sum(gate_values, axis=1, keepdims=True)
    before = jnp.zeros_like(total)
    value_tiles = value_states.reshape(4, BLOCK, -1).transpose(0, 2, 1)
    va, vb = {0: value_tiles[:, : 4 * HEAD]}, {0: value_tiles[:, 4 * HEAD :]}
    right, left = Wire("right", 1), Wire("left", -1)
    for name, ring in (("va", va), ("vb", vb)):
        for wire in (right, left):
            wire.send(name, ring, 1)
    picks = selected_blocks.T.astype(jnp.float32)
    with jax.named_scope("prefix"):
        rows_before = before
        for bit in (1, 2):
            other = swap(jnp.concatenate([total, rows_before, picks], axis=1), "y", bit)
            if bit == 1:
                own_total = total
            rows_before = rows_before + jnp.where((my_y & bit) != 0, other[:, :1], 0.0)
            total = total + other[:, :1]
            picks = jnp.concatenate([picks, other[:, 2:]], axis=1)
        own_total = after(own_total, va[1], va[-1], vb[1], vb[-1])
        for bit in (1, 2, 4):
            other = swap(jnp.concatenate([own_total, rows_before], axis=1), "z", bit)
            before = before + jnp.where((my_z & bit) != 0, other[:, :1], 0.0)
            own_total = own_total + other[:, :1]
            rows_before = rows_before + other[:, 1:]
    angles = before + rows_before + jnp.cumsum(gate_values, axis=1)
    query_rot, keys_a, keys_b = rotate(angles, query_states, key_states)
    ka, kb = {0: keys_a}, {0: keys_b}
    with jax.named_scope("queries"):
        queries = lax.all_to_all(query_rot, "y", 0, 0, tiled=True)

    picks = picks.astype(jnp.int32).T.reshape(4, 1, 4, 8)
    wanted = (my_y + lax.broadcasted_iota(jnp.int32, (4, 4, 1, 1), 1)) ^ my_y
    turn = lax.broadcasted_iota(jnp.int32, (4, 4, 1, 1), 0)
    blocks = jnp.sum(jnp.where(wanted == turn, picks, 0), axis=0).reshape(16, 1, 8)
    row = lax.broadcasted_iota(jnp.int32, (16, RING, 8), 0)
    distance = lax.broadcasted_iota(jnp.int32, (16, RING, 8), 1)
    own = ((my_y + row // 4) * RING + my_z) * 4 + row % 4
    hit = (blocks >> 5 == my_y) & (((blocks >> 2) - my_z) & 7 == distance)
    hit &= (blocks != own) & (my_y + row // 4 < ROWS)
    code = jnp.where(distance == 0, 1 << (blocks & 3), (blocks & 3) + 1)
    meta = jnp.sum(jnp.where(hit, code, 0), axis=2).reshape(-1)
    meta = jnp.concatenate([meta, my_y.astype(jnp.int32)[None]])

    def call(part, group, state, last):
        offsets = []
        for distance in group:
            offsets += [distance] if distance in (0, 4) else [-distance, distance]
        keys, values = (ka, va) if part == 0 else (kb, vb)
        return attend(
            meta,
            queries,
            CHUNKS[part],
            tuple(offsets),
            [keys[o] for o in offsets],
            [values[o] for o in offsets],
            state,
            last,
        )

    def pick(rows, step):
        return lax.dynamic_index_in_dim(rows, (my_y + step) & 3, 0, keepdims=False)

    for name, ring, distance in (
        ("ka", ka, 1),
        ("va", va, 2),
        ("ka", ka, 2),
        ("va", va, 3),
        ("ka", ka, 3),
    ):
        for wire in (right, left):
            wire.send(name, ring, distance)
    right.send("va", va, 4)
    right.send("ka", ka, 4)
    left.send("kb", kb, 1)
    state = call(0, GROUPS[0][0], None, False)
    right.send("kb", kb, 1)
    left.send("vb", vb, 2)
    right.send("vb", vb, 2)
    left.send("kb", kb, 2)
    state = call(0, GROUPS[0][1], state, True)
    right.send("kb", kb, 2, state[1])
    left.send("vb", vb, 3, state[1])
    right.send("vb", vb, 3)
    left.send("kb", kb, 3)
    first_b = call(1, GROUPS[1][0], None, False)
    right.send("kb", kb, 3, first_b[1])
    left.send("vb", vb, 4, first_b[1])
    left.send("kb", kb, 4)
    mine_a = state[:3]
    with jax.named_scope("partials_a"):
        parts_a = lax.all_to_all(state[3], "y", 0, 0, tiled=True)
    first_b[1] = after(first_b[1], parts_a)
    state = call(1, GROUPS[1][1], first_b, False)
    state = call(1, GROUPS[1][2], state, True)
    parts_b = []
    for s in (1, 2, 3):
        with jax.named_scope(f"partial_b{s}"):
            parts_b.append(to_row(state[2 + s], s))
    parts_a = after(parts_a, state[1])
    out = join(CHUNKS[0], mine_a, [pick(parts_a, -s) for s in (1, 2, 3)], None)
    return join(CHUNKS[1], state[:3], parts_b, out)


def solution(mesh):
    grid = Mesh(mesh.devices.reshape(2, ROWS, RING, 4), ("dp", "y", "z", "head"))
    tokens = ("dp", "y", "z")
    placed = (
        P(tokens, "head"),
        P(tokens, "head"),
        P(tokens, "head"),
        P("head", tokens),
        P(tokens, None),
    )
    return jax.shard_map(
        shards, mesh=grid, in_specs=placed, out_specs=P(tokens, "head"), check_vma=False
    )
```

```python
import functools
import math

import jax
import jax.numpy as jnp
from jax import lax
from jax.experimental import pallas as pl
from jax.experimental.pallas import tpu as pltpu
from jax.sharding import Mesh, PartitionSpec as P

BLOCK = 128
HEAD = 128
ROWS = 4
RING = 8
NEG_FILL = -1e30
ROPE_BASE = 10000.0
VMEM_LIMIT = 24 << 20
IDLE = 4
STAT = 48
CHUNKS = ((0, 4), (4, 4))
GROUPS = (((0, 1, 2), (3, 4)), ((0, 1), (2, 3), (4,)))


QUARTER = (1.5703125, 4.837512969970703e-4, 7.54978995489188216e-8)


def sin_cos(phase):
    turns = jnp.floor(phase * (2 / math.pi) + 0.5)
    x = phase
    for part in QUARTER:
        x = x - turns * part
    square = x * x
    sine = ((-1.9515295891e-4 * square + 8.3321608736e-3) * square - 1.6666654611e-1) * square
    sine = sine * x + x
    cosine = ((2.443315711809948e-5 * square - 1.388731625493765e-3) * square + 4.166664568298827e-2)
    cosine = cosine * square * square - 0.5 * square + 1.0
    quadrant = turns.astype(jnp.int32) & 3
    odd = (quadrant & 1) == 1
    sine, cosine = jnp.where(odd, cosine, sine), jnp.where(odd, sine, cosine)
    sine = jnp.where(quadrant >= 2, -sine, sine)
    cosine = jnp.where((quadrant == 1) | (quadrant == 2), -cosine, cosine)
    return sine, cosine


def rotate_kernel(angle_ref, freq_ref, q_ref, k_ref, *outs):
    freq = freq_ref[...]
    lane = lax.broadcasted_iota(jnp.int32, (BLOCK, HEAD), 1)
    low = lane < HEAD // 2
    heads = q_ref.shape[1] // HEAD
    for pair in range(heads // 2):
        even = angle_ref[:, 2 * pair : 2 * pair + 1]
        odd = angle_ref[:, 2 * pair + 1 : 2 * pair + 2]
        sine, cosine = sin_cos(jnp.where(low, even, odd) * freq)
        sine_turned = pltpu.roll(sine, HEAD // 2, 1)
        cosine_turned = pltpu.roll(cosine, HEAD // 2, 1)
        for h in (2 * pair, 2 * pair + 1):
            first, second = (sine, sine_turned) if h % 2 == 0 else (sine_turned, sine)
            signed = jnp.where(low, -first, second)
            first, second = (cosine, cosine_turned) if h % 2 == 0 else (cosine_turned, cosine)
            plain = jnp.where(low, first, second)
            cols = slice(h * HEAD, (h + 1) * HEAD)

            def turn(x):
                x = x.astype(jnp.float32)
                return (x * plain + pltpu.roll(x, HEAD // 2, 1) * signed).astype(jnp.bfloat16)

            part = slice(h % 4 * HEAD, (h % 4 + 1) * HEAD)
            query = turn(q_ref[:, cols])
            for row in range(ROWS):
                outs[0][row, :, cols] = query
            outs[1 + h // 4][0, part, :] = turn(k_ref[:, cols])


def rotate(angles, queries, keys):
    half = HEAD // 2
    inv_freq = ROPE_BASE ** (-jnp.arange(half).astype(jnp.float32) / half)
    inv_freq = jnp.concatenate([inv_freq, inv_freq])[None]
    heads = angles.shape[0]
    bf16 = jnp.bfloat16
    rows = pl.BlockSpec((BLOCK, heads * HEAD), lambda b: (b, 0))
    copies = pl.BlockSpec((ROWS, BLOCK, heads * HEAD), lambda b: (0, b, 0))
    tiled = pl.BlockSpec((1, 4 * HEAD, BLOCK), lambda b: (b, 0, 0))
    return pl.pallas_call(
        rotate_kernel,
        out_shape=[
            jax.ShapeDtypeStruct((ROWS, *queries.shape), bf16),
            jax.ShapeDtypeStruct((4, 4 * HEAD, BLOCK), bf16),
            jax.ShapeDtypeStruct((4, 4 * HEAD, BLOCK), bf16),
        ],
        grid=(4,),
        in_specs=[
            pl.BlockSpec((BLOCK, heads), lambda b: (b, 0)),
            pl.BlockSpec((1, HEAD), lambda b: (0, 0)),
            rows,
            rows,
        ],
        out_specs=[copies, tiled, tiled],
        compiler_params=pltpu.CompilerParams(vmem_limit_bytes=VMEM_LIMIT),
        cost_estimate=pl.CostEstimate(flops=5 * 10**9, bytes_accessed=6 << 20, transcendentals=0),
        name="rotate",
    )(angles.T, inv_freq, queries, keys)


def attend_kernel(offsets, heads, first, last, meta, *refs):
    count = len(offsets)
    given_q, refs = refs[0], refs[1:]
    k_refs, v_refs = refs[:count], refs[count : 2 * count]
    rest = list(refs[2 * count :])
    acc, m_run, l_run, q_ref, k_all, v_all, todo = rest[-7:]
    rest = rest[:-7]
    given = None
    if not first:
        given, rest = rest[:3], rest[3:]
    r = pl.program_id(0)
    scale = HEAD**-0.5 * math.log2(math.e)

    @pl.when(r == 0)
    def _():
        def hold(kb, carry):
            for at in range(count):
                k_all[at, kb] = k_refs[at][kb]
                v_all[at, kb] = v_refs[at][kb]
            return carry

        lax.fori_loop(0, 4, hold, 0)
        q_ref[IDLE * BLOCK :, :] = jnp.zeros((BLOCK, heads * HEAD), jnp.bfloat16)
        acc[IDLE] = jnp.zeros((heads * HEAD, BLOCK), jnp.float32)
        m_run[IDLE] = jnp.full((8, BLOCK), NEG_FILL)
        l_run[IDLE] = jnp.zeros((8, BLOCK), jnp.float32)

    def enter(qb, carry):
        q_rows = pl.ds(pl.multiple_of(qb * BLOCK, BLOCK), BLOCK)
        q_ref[q_rows, :] = given_q[0, q_rows, :]
        if first:
            acc[qb] = jnp.zeros((heads * HEAD, BLOCK), jnp.float32)
            m_run[qb] = jnp.full((8, BLOCK), NEG_FILL)
            l_run[qb] = jnp.zeros((8, BLOCK), jnp.float32)
        else:
            acc[qb] = given[0][qb]
            m_run[qb] = given[1][qb]
            l_run[qb] = given[2][qb]
        return carry

    lax.fori_loop(0, 4, enter, 0)

    span = range(heads)
    cols = [slice(h * HEAD, (h + 1) * HEAD) for h in span]

    def two(items, causal):
        olds, scores = [], []
        for qb, at, kb in items:
            q_rows = pl.ds(pl.multiple_of(qb * BLOCK, BLOCK), BLOCK)
            olds.append((m_run[qb], l_run[qb]))
            scores.append(
                [
                    lax.dot_general(
                        k_all[at, kb, cols[h], :],
                        q_ref[q_rows, cols[h]],
                        (((1,), (1,)), ((), ())),
                        preferred_element_type=jnp.float32,
                    )
                    for h in span
                ]
            )
        if causal:
            key_pos = lax.broadcasted_iota(jnp.int32, (BLOCK, BLOCK), 0)
            query_pos = lax.broadcasted_iota(jnp.int32, (BLOCK, BLOCK), 1)
            seen = key_pos <= query_pos
            scores = [[jnp.where(seen, s, NEG_FILL) for s in group] for group in scores]
        results = []
        for (qb, at, kb), (m_old, l_old), group in zip(items, olds, scores):
            tops = [jnp.max(s, axis=0, keepdims=True) for s in group]
            if heads < 8:
                tops.append(m_old[heads:])
            m_new = jnp.maximum(m_old, jnp.concatenate(tops, axis=0))
            fade = jnp.exp2((m_old - m_new) * scale)
            weights = [jnp.exp2((group[h] - m_new[h : h + 1]) * scale) for h in span]
            sums = [jnp.sum(w, axis=0, keepdims=True) for w in weights]
            if heads < 8:
                sums.append(jnp.zeros((8 - heads, BLOCK), jnp.float32))
            mixed = [
                jnp.dot(
                    v_all[at, kb, cols[h], :],
                    weights[h].astype(jnp.bfloat16),
                    preferred_element_type=jnp.float32,
                )
                for h in span
            ]
            results.append((m_new, l_old * fade + jnp.concatenate(sums, axis=0), fade, mixed))
        wholes = [
            [acc[qb, cols[h], :] * fade[h : h + 1] + mixed[h] for h in span]
            for (qb, _, _), (_, _, fade, mixed) in zip(items, results)
        ]
        for (qb, _, _), (m_new, l_new, _, _), whole in zip(items, results, wholes):
            m_run[qb] = m_new
            l_run[qb] = l_new
            for h in span:
                acc[qb, cols[h], :] = whole[h]

    if 0 in offsets:
        here = offsets.index(0)

        @pl.when(r == 0)
        def _():
            def own(i, carry):
                two([(2 * i, here, 2 * i), (2 * i + 1, here, 2 * i + 1)], True)
                return carry

            lax.fori_loop(0, 2, own, 0)

    def note(at, choice, offset, qb, length, newest):
        code = meta[(r * 4 + qb) * RING + offset % RING]
        if offset == 0:
            valid, kb = (code >> choice) & 1, choice
        else:
            valid, kb = (code > 0).astype(jnp.int32), jnp.maximum(code - 1, 0)
        item = qb + at * 16 + kb * 256
        clash = valid & length & (newest == qb).astype(jnp.int32)
        todo[length] = jnp.where(clash == 1, IDLE, item)
        todo[length + 1] = item
        return length + valid * (1 + clash), jnp.where(valid == 1, qb, newest)

    found = (jnp.int32(0), jnp.int32(-1))
    for at, offset in enumerate(offsets):
        if offset == 0:
            found = lax.fori_loop(
                0, 16, lambda i, f, at=at: note(at, i >> 2, 0, i & 3, *f), found
            )
        else:
            found = lax.fori_loop(
                0, 4, lambda i, f, at=at, offset=offset: note(at, 0, offset, i, *f), found
            )
    length = found[0]
    todo[length] = IDLE

    def step(i, carry):
        items = []
        for side in (0, 1):
            item = todo[2 * i + side]
            items.append((item & 15, (item >> 4) & 15, item >> 8))
        two(items, False)
        return carry

    lax.fori_loop(0, (length + 1) >> 1, step, 0)

    def leave(acc_out, m_out, l_out):
        def copy(qb, carry):
            acc_out[qb] = acc[qb]
            m_out[qb] = m_run[qb]
            l_out[qb] = l_run[qb]
            return carry

        lax.fori_loop(0, 4, copy, 0)

    if not last:
        leave(*rest)
    else:
        packed_refs = rest[3:]

        @pl.when(r == 0)
        def _():
            leave(*rest[:3])

        def send(packed_ref, lead):
            def pack(qb, carry):
                pieces = []
                for value in (m_run[qb], l_run[qb]):
                    for _ in range(3):
                        piece = value.astype(jnp.bfloat16).astype(jnp.float32)
                        pieces.append(piece)
                        value = value - piece
                packed_ref[(*lead, qb, slice(heads * HEAD, None), slice(None))] = jnp.concatenate(pieces, axis=0).astype(
                    jnp.bfloat16
                )
                total = l_run[qb]
                inverse = 1.0 / jnp.where(total > 0, total, 1.0)
                for h in span:
                    packed_ref[(*lead, qb, cols[h], slice(None))] = (
                        acc[qb, cols[h], :] * inverse[h : h + 1]
                    ).astype(jnp.bfloat16)
                return carry

            lax.fori_loop(0, 4, pack, 0)

        if len(packed_refs) == 1:
            pl.when(r > 0)(lambda: send(packed_refs[0], (0,)))
        else:
            for row, packed_ref in enumerate(packed_refs):
                pl.when(r == row + 1)(functools.partial(send, packed_ref, ()))


def attend(meta, queries, chunk, offsets, keys, values, state, last):
    first_head, heads = chunk
    apart = first_head > 0
    width = heads * HEAD
    first = state is None
    acc_spec = pl.BlockSpec((4, width, BLOCK), lambda r, meta: (r, 0, 0))
    run_spec = pl.BlockSpec((4, 8, BLOCK), lambda r, meta: (r, 0, 0))
    state_specs = [acc_spec, run_spec, run_spec]
    in_specs = [
        pl.BlockSpec(
            (1, 512, width),
            lambda r, meta: (jnp.minimum(meta[16 * RING] + r, ROWS - 1), 0, first_head // heads),
        )
    ]
    in_specs += [pl.BlockSpec((4, width, BLOCK), lambda r, meta: (0, 0, 0))] * (2 * len(offsets))
    operands = [queries, *keys, *values]
    if not first:
        in_specs += state_specs
        operands += list(state)
    f32 = jnp.float32
    if last:
        out_shape = [
            jax.ShapeDtypeStruct((4, width, BLOCK), f32),
            jax.ShapeDtypeStruct((4, 8, BLOCK), f32),
            jax.ShapeDtypeStruct((4, 8, BLOCK), f32),
            *(
                [jax.ShapeDtypeStruct((4, width + STAT, BLOCK), jnp.bfloat16)] * 3
                if apart
                else [jax.ShapeDtypeStruct((ROWS, 4, width + STAT, BLOCK), jnp.bfloat16)]
            ),
        ]
        out_specs = [
            pl.BlockSpec((4, width, BLOCK), lambda r, meta: (0, 0, 0)),
            pl.BlockSpec((4, 8, BLOCK), lambda r, meta: (0, 0, 0)),
            pl.BlockSpec((4, 8, BLOCK), lambda r, meta: (0, 0, 0)),
            *(
                [pl.BlockSpec((4, width + STAT, BLOCK), lambda r, meta: (0, 0, 0))] * 3
                if apart
                else [            pl.BlockSpec((1, 4, width + STAT, BLOCK), lambda r, meta: ((meta[16 * RING] + jnp.maximum(r, 1)) & 3, 0, 0, 0))]
            ),
        ]
    else:
        out_shape = [
            jax.ShapeDtypeStruct((16, width, BLOCK), f32),
            jax.ShapeDtypeStruct((16, 8, BLOCK), f32),
            jax.ShapeDtypeStruct((16, 8, BLOCK), f32),
        ]
        out_specs = state_specs
    count = len(offsets)
    scratch = [
        pltpu.VMEM((5, width, BLOCK), f32),
        pltpu.VMEM((5, 8, BLOCK), f32),
        pltpu.VMEM((5, 8, BLOCK), f32),
        pltpu.VMEM((5 * BLOCK, width), jnp.bfloat16),
        pltpu.VMEM((count, 4, width, BLOCK), jnp.bfloat16),
        pltpu.VMEM((count, 4, width, BLOCK), jnp.bfloat16),
        pltpu.SMEM((80,), jnp.int32),
    ]
    return list(pl.pallas_call(
        functools.partial(attend_kernel, offsets, heads, first, last),
        out_shape=out_shape,
        grid_spec=pltpu.PrefetchScalarGridSpec(
            num_scalar_prefetch=1,
            grid=(ROWS,),
            in_specs=in_specs,
            out_specs=out_specs,
            scratch_shapes=scratch,
        ),
        compiler_params=pltpu.CompilerParams(vmem_limit_bytes=VMEM_LIMIT),
        cost_estimate=pl.CostEstimate(
            flops=int((2 + 3 * len(offsets)) * 1.1e9),
            bytes_accessed=1 << 20,
            transcendentals=0,
        ),
        name=f"attend_{first_head}_{'_'.join(str(o % RING) for o in offsets)}",
    )(meta, *operands))


def join_kernel(heads, acc_ref, m_ref, l_ref, one, two, three, *rest):
    out_ref = rest[-1]
    width = heads * HEAD
    tops, sums = [m_ref[0]], [l_ref[0]]
    for part in (one, two, three):
        stats = part[0, width:, :].astype(jnp.float32)
        top = (stats[16:24] + stats[8:16]) + stats[0:8]
        total = (stats[40:48] + stats[32:40]) + stats[24:32]
        tops.append(jnp.where(total > 0, top, NEG_FILL))
        sums.append(total)
    scale = HEAD**-0.5 * math.log2(math.e)
    highest = jnp.maximum(jnp.maximum(tops[0], tops[1]), jnp.maximum(tops[2], tops[3]))
    fades = [jnp.exp2((top - highest) * scale) for top in tops]
    shares = [fades[0]] + [fades[i] * sums[i] for i in (1, 2, 3)]
    whole = fades[0] * sums[0] + shares[1] + shares[2] + shares[3]
    inverse = 1.0 / whole
    for h in range(heads):
        cols = slice(h * HEAD, (h + 1) * HEAD)
        mixed = acc_ref[0, cols, :] * shares[0][h : h + 1, :]
        for i, part in enumerate((one, two, three)):
            mixed += part[0, cols, :].astype(jnp.float32) * shares[i + 1][h : h + 1, :]
        mixed = mixed * inverse[h : h + 1, :]
        out_ref[:, cols] = mixed.T.astype(jnp.bfloat16)


def join(chunk, state, parts, out):
    first_head, heads = chunk
    width = heads * HEAD
    in_specs = [
        pl.BlockSpec((1, width, BLOCK), lambda b: (b, 0, 0)),
        pl.BlockSpec((1, 8, BLOCK), lambda b: (b, 0, 0)),
        pl.BlockSpec((1, 8, BLOCK), lambda b: (b, 0, 0)),
    ] + [pl.BlockSpec((1, width + STAT, BLOCK), lambda b: (b, 0, 0))] * 3
    operands = [*state, *parts]
    aliases = {}
    if out is not None:
        aliases = {len(operands): 0}
        in_specs.append(pl.BlockSpec(memory_space=pl.ANY))
        operands.append(out)
    return pl.pallas_call(
        functools.partial(join_kernel, heads),
        out_shape=jax.ShapeDtypeStruct((512, 1024), jnp.bfloat16),
        grid=(4,),
        in_specs=in_specs,
        out_specs=pl.BlockSpec((BLOCK, width), lambda b: (b, first_head // heads)),
        input_output_aliases=aliases,
        compiler_params=pltpu.CompilerParams(vmem_limit_bytes=VMEM_LIMIT),
        cost_estimate=pl.CostEstimate(
            flops=512 * width * 10, bytes_accessed=512 * width * 14, transcendentals=0
        ),
        name=f"join_{first_head}",
    )(*operands)


def shift(value, axis, step):
    size = lax.axis_size(axis)
    return lax.ppermute(value, axis, [(i, (i + step) % size) for i in range(size)])


def to_row(value, step):
    moves = [(i, i + step) for i in range(ROWS) if 0 <= i + step < ROWS]
    return lax.ppermute(value, "y", moves)


def swap(value, axis, bit):
    size = lax.axis_size(axis)
    return lax.ppermute(value, axis, [(i, i ^ bit) for i in range(size)])


def after(value, *others):
    return lax.optimization_barrier((value, *others))[0]


class Wire:
    def __init__(self, side, sign, depth=2):
        self.side, self.sign, self.depth = side, sign, depth
        self.sent = []

    def send(self, name, ring, distance, *others):
        source = ring[-self.sign * (distance - 1)]
        waits = list(others)
        waits += self.sent[-self.depth - 1 : -self.depth + 1] if self.sent[1:] else []
        if waits:
            source = after(source, *waits)
        with jax.named_scope(f"{name}{distance}_{self.side}"):
            got = shift(source, "z", self.sign)
        self.sent.append(got)
        ring[-self.sign * distance if distance < 4 else 4] = got


def shards(query_states, key_states, value_states, gate_logits, selected_blocks):
    my_y, my_z = lax.axis_index("y"), lax.axis_index("z")
    gate_values = jax.nn.sigmoid(gate_logits.astype(jnp.float32))
    total = jnp.sum(gate_values, axis=1, keepdims=True)
    before = jnp.zeros_like(total)
    value_tiles = value_states.reshape(4, BLOCK, -1).transpose(0, 2, 1)
    va, vb = {0: value_tiles[:, : 4 * HEAD]}, {0: value_tiles[:, 4 * HEAD :]}
    right, left = Wire("right", 1), Wire("left", -1)
    for wire in (right, left):
        wire.send("va", va, 1)
    picks = selected_blocks.T.astype(jnp.float32)
    with jax.named_scope("prefix"):
        rows_before = before
        for bit in (1, 2):
            other = swap(jnp.concatenate([total, rows_before, picks], axis=1), "y", bit)
            if bit == 1:
                own_total = total
            rows_before = rows_before + jnp.where((my_y & bit) != 0, other[:, :1], 0.0)
            total = total + other[:, :1]
            picks = jnp.concatenate([picks, other[:, 2:]], axis=1)
        own_total = after(own_total, va[1], va[-1])
        for bit in (1, 2, 4):
            other = swap(jnp.concatenate([own_total, rows_before], axis=1), "z", bit)
            before = before + jnp.where((my_z & bit) != 0, other[:, :1], 0.0)
            own_total = own_total + other[:, :1]
            rows_before = rows_before + other[:, 1:]
    angles = before + rows_before + jnp.cumsum(gate_values, axis=1)
    query_rot, keys_a, keys_b = rotate(angles, query_states, key_states)
    ka, kb = {0: keys_a}, {0: keys_b}
    with jax.named_scope("queries"):
        queries = lax.all_to_all(query_rot, "y", 0, 0, tiled=True)

    picks = picks.astype(jnp.int32).T.reshape(4, 1, 4, 8)
    wanted = (my_y + lax.broadcasted_iota(jnp.int32, (4, 4, 1, 1), 1)) ^ my_y
    turn = lax.broadcasted_iota(jnp.int32, (4, 4, 1, 1), 0)
    blocks = jnp.sum(jnp.where(wanted == turn, picks, 0), axis=0).reshape(16, 1, 8)
    row = lax.broadcasted_iota(jnp.int32, (16, RING, 8), 0)
    distance = lax.broadcasted_iota(jnp.int32, (16, RING, 8), 1)
    own = ((my_y + row // 4) * RING + my_z) * 4 + row % 4
    hit = (blocks >> 5 == my_y) & (((blocks >> 2) - my_z) & 7 == distance)
    hit &= (blocks != own) & (my_y + row // 4 < ROWS)
    code = jnp.where(distance == 0, 1 << (blocks & 3), (blocks & 3) + 1)
    meta = jnp.sum(jnp.where(hit, code, 0), axis=2).reshape(-1)
    meta = jnp.concatenate([meta, my_y.astype(jnp.int32)[None]])

    def call(part, group, state, last):
        offsets = []
        for distance in group:
            offsets += [distance] if distance in (0, 4) else [-distance, distance]
        keys, values = (ka, va) if part == 0 else (kb, vb)
        return attend(
            meta,
            queries,
            CHUNKS[part],
            tuple(offsets),
            [keys[o] for o in offsets],
            [values[o] for o in offsets],
            state,
            last,
        )

    def pick(rows, step):
        return lax.dynamic_index_in_dim(rows, (my_y + step) & 3, 0, keepdims=False)

    for wire in (right, left):
        wire.send("vb", vb, 1, own_total)
    for name, ring, distance in (
        ("ka", ka, 1),
        ("va", va, 2),
        ("ka", ka, 2),
        ("va", va, 3),
        ("ka", ka, 3),
    ):
        for wire in (right, left):
            wire.send(name, ring, distance)
    right.send("va", va, 4)
    left.send("kb", kb, 1)
    right.send("kb", kb, 1)
    left.send("vb", vb, 2)
    state = call(0, GROUPS[0][0], None, False)
    right.send("ka", ka, 4, state[1])
    left.send("kb", kb, 2, state[1])
    right.send("vb", vb, 2, state[1])
    left.send("vb", vb, 3, state[1])
    state = call(0, GROUPS[0][1], state, True)
    right.send("kb", kb, 2, state[1])
    left.send("kb", kb, 3, state[1])
    right.send("vb", vb, 3, state[1])
    left.send("vb", vb, 4, state[1])
    first_b = call(1, GROUPS[1][0], None, False)
    right.send("kb", kb, 3, first_b[1])
    left.send("kb", kb, 4, first_b[1])
    mine_a = state[:3]
    with jax.named_scope("partials_a"):
        parts_a = lax.all_to_all(state[3], "y", 0, 0, tiled=True)
    first_b[1] = after(first_b[1], parts_a)
    state = call(1, GROUPS[1][1], first_b, False)
    state = call(1, GROUPS[1][2], state, True)
    parts_b = []
    for s in (1, 2, 3):
        with jax.named_scope(f"partial_b{s}"):
            parts_b.append(to_row(state[2 + s], s))
    parts_a = after(parts_a, state[1])
    out = join(CHUNKS[0], mine_a, [pick(parts_a, -s) for s in (1, 2, 3)], None)
    return join(CHUNKS[1], state[:3], parts_b, out)


def solution(mesh):
    grid = Mesh(mesh.devices.reshape(2, ROWS, RING, 4), ("dp", "y", "z", "head"))
    tokens = ("dp", "y", "z")
    placed = (
        P(tokens, "head"),
        P(tokens, "head"),
        P(tokens, "head"),
        P("head", tokens),
        P(tokens, None),
    )
    return jax.shard_map(
        shards, mesh=grid, in_specs=placed, out_specs=P(tokens, "head"), check_vma=False
    )
```

```python
import functools
import math

import jax
import jax.numpy as jnp
from jax import lax
from jax.experimental import pallas as pl
from jax.experimental.pallas import tpu as pltpu
from jax.sharding import Mesh, PartitionSpec as P

BLOCK = 128
HEAD = 128
ROWS = 4
RING = 8
NEG_FILL = -1e30
ROPE_BASE = 10000.0
VMEM_LIMIT = 24 << 20
IDLE = 4
STAT = 48
CHUNKS = ((0, 4), (4, 4))
GROUPS = (((0, 1, 2), (3, 4)), ((0, 1), (2,), (3, 4)))


QUARTER = (1.5703125, 4.837512969970703e-4, 7.54978995489188216e-8)


def sin_cos(phase):
    turns = jnp.floor(phase * (2 / math.pi) + 0.5)
    x = phase
    for part in QUARTER:
        x = x - turns * part
    square = x * x
    sine = ((-1.9515295891e-4 * square + 8.3321608736e-3) * square - 1.6666654611e-1) * square
    sine = sine * x + x
    cosine = ((2.443315711809948e-5 * square - 1.388731625493765e-3) * square + 4.166664568298827e-2)
    cosine = cosine * square * square - 0.5 * square + 1.0
    quadrant = turns.astype(jnp.int32) & 3
    odd = (quadrant & 1) == 1
    sine, cosine = jnp.where(odd, cosine, sine), jnp.where(odd, sine, cosine)
    sine = jnp.where(quadrant >= 2, -sine, sine)
    cosine = jnp.where((quadrant == 1) | (quadrant == 2), -cosine, cosine)
    return sine, cosine


def rotate_kernel(angle_ref, freq_ref, q_ref, k_ref, *outs):
    freq = freq_ref[...]
    lane = lax.broadcasted_iota(jnp.int32, (BLOCK, HEAD), 1)
    low = lane < HEAD // 2
    heads = q_ref.shape[1] // HEAD
    for pair in range(heads // 2):
        even = angle_ref[:, 2 * pair : 2 * pair + 1]
        odd = angle_ref[:, 2 * pair + 1 : 2 * pair + 2]
        sine, cosine = sin_cos(jnp.where(low, even, odd) * freq)
        sine_turned = pltpu.roll(sine, HEAD // 2, 1)
        cosine_turned = pltpu.roll(cosine, HEAD // 2, 1)
        for h in (2 * pair, 2 * pair + 1):
            first, second = (sine, sine_turned) if h % 2 == 0 else (sine_turned, sine)
            signed = jnp.where(low, -first, second)
            first, second = (cosine, cosine_turned) if h % 2 == 0 else (cosine_turned, cosine)
            plain = jnp.where(low, first, second)
            cols = slice(h * HEAD, (h + 1) * HEAD)

            def turn(x):
                x = x.astype(jnp.float32)
                return (x * plain + pltpu.roll(x, HEAD // 2, 1) * signed).astype(jnp.bfloat16)

            part = slice(h % 4 * HEAD, (h % 4 + 1) * HEAD)
            query = turn(q_ref[:, cols])
            for row in range(ROWS):
                outs[0][row, :, cols] = query
            outs[1 + h // 4][0, part, :] = turn(k_ref[:, cols])


def rotate(angles, queries, keys):
    half = HEAD // 2
    inv_freq = ROPE_BASE ** (-jnp.arange(half).astype(jnp.float32) / half)
    inv_freq = jnp.concatenate([inv_freq, inv_freq])[None]
    heads = angles.shape[0]
    bf16 = jnp.bfloat16
    rows = pl.BlockSpec((BLOCK, heads * HEAD), lambda b: (b, 0))
    copies = pl.BlockSpec((ROWS, BLOCK, heads * HEAD), lambda b: (0, b, 0))
    tiled = pl.BlockSpec((1, 4 * HEAD, BLOCK), lambda b: (b, 0, 0))
    return pl.pallas_call(
        rotate_kernel,
        out_shape=[
            jax.ShapeDtypeStruct((ROWS, *queries.shape), bf16),
            jax.ShapeDtypeStruct((4, 4 * HEAD, BLOCK), bf16),
            jax.ShapeDtypeStruct((4, 4 * HEAD, BLOCK), bf16),
        ],
        grid=(4,),
        in_specs=[
            pl.BlockSpec((BLOCK, heads), lambda b: (b, 0)),
            pl.BlockSpec((1, HEAD), lambda b: (0, 0)),
            rows,
            rows,
        ],
        out_specs=[copies, tiled, tiled],
        compiler_params=pltpu.CompilerParams(vmem_limit_bytes=60 << 20),
        cost_estimate=pl.CostEstimate(flops=5 * 10**9, bytes_accessed=6 << 20, transcendentals=0),
        name="rotate",
    )(angles.T, inv_freq, queries, keys)


def attend_kernel(offsets, heads, first, last, meta, *refs):
    count = len(offsets)
    given_q, refs = refs[0], refs[1:]
    k_refs, v_refs = refs[:count], refs[count : 2 * count]
    rest = list(refs[2 * count :])
    acc, m_run, l_run, q_ref, k_all, v_all, todo = rest[-7:]
    rest = rest[:-7]
    given = None
    if not first:
        given, rest = rest[:3], rest[3:]
    r = pl.program_id(0)
    scale = HEAD**-0.5 * math.log2(math.e)

    @pl.when(r == 0)
    def _():
        def hold(kb, carry):
            for at in range(count):
                k_all[at, kb] = k_refs[at][kb]
                v_all[at, kb] = v_refs[at][kb]
            return carry

        lax.fori_loop(0, 4, hold, 0)
        q_ref[IDLE * BLOCK :, :] = jnp.zeros((BLOCK, heads * HEAD), jnp.bfloat16)
        acc[IDLE] = jnp.zeros((heads * HEAD, BLOCK), jnp.float32)
        m_run[IDLE] = jnp.full((8, BLOCK), NEG_FILL)
        l_run[IDLE] = jnp.zeros((8, BLOCK), jnp.float32)

    def enter(qb, carry):
        q_rows = pl.ds(pl.multiple_of(qb * BLOCK, BLOCK), BLOCK)
        q_ref[q_rows, :] = given_q[0, q_rows, :]
        if first:
            acc[qb] = jnp.zeros((heads * HEAD, BLOCK), jnp.float32)
            m_run[qb] = jnp.full((8, BLOCK), NEG_FILL)
            l_run[qb] = jnp.zeros((8, BLOCK), jnp.float32)
        else:
            acc[qb] = given[0][qb]
            m_run[qb] = given[1][qb]
            l_run[qb] = given[2][qb]
        return carry

    lax.fori_loop(0, 4, enter, 0)

    span = range(heads)
    cols = [slice(h * HEAD, (h + 1) * HEAD) for h in span]

    def two(items, causal):
        olds, scores = [], []
        for qb, at, kb in items:
            q_rows = pl.ds(pl.multiple_of(qb * BLOCK, BLOCK), BLOCK)
            olds.append((m_run[qb], l_run[qb]))
            scores.append(
                [
                    lax.dot_general(
                        k_all[at, kb, cols[h], :],
                        q_ref[q_rows, cols[h]],
                        (((1,), (1,)), ((), ())),
                        preferred_element_type=jnp.float32,
                    )
                    for h in span
                ]
            )
        if causal:
            key_pos = lax.broadcasted_iota(jnp.int32, (BLOCK, BLOCK), 0)
            query_pos = lax.broadcasted_iota(jnp.int32, (BLOCK, BLOCK), 1)
            seen = key_pos <= query_pos
            scores = [[jnp.where(seen, s, NEG_FILL) for s in group] for group in scores]
        results = []
        for (qb, at, kb), (m_old, l_old), group in zip(items, olds, scores):
            tops = [jnp.max(s, axis=0, keepdims=True) for s in group]
            if heads < 8:
                tops.append(m_old[heads:])
            m_new = jnp.maximum(m_old, jnp.concatenate(tops, axis=0))
            fade = jnp.exp2((m_old - m_new) * scale)
            weights = [jnp.exp2((group[h] - m_new[h : h + 1]) * scale) for h in span]
            sums = [jnp.sum(w, axis=0, keepdims=True) for w in weights]
            if heads < 8:
                sums.append(jnp.zeros((8 - heads, BLOCK), jnp.float32))
            mixed = [
                jnp.dot(
                    v_all[at, kb, cols[h], :],
                    weights[h].astype(jnp.bfloat16),
                    preferred_element_type=jnp.float32,
                )
                for h in span
            ]
            results.append((m_new, l_old * fade + jnp.concatenate(sums, axis=0), fade, mixed))
        wholes = [
            [acc[qb, cols[h], :] * fade[h : h + 1] + mixed[h] for h in span]
            for (qb, _, _), (_, _, fade, mixed) in zip(items, results)
        ]
        for (qb, _, _), (m_new, l_new, _, _), whole in zip(items, results, wholes):
            m_run[qb] = m_new
            l_run[qb] = l_new
            for h in span:
                acc[qb, cols[h], :] = whole[h]

    if 0 in offsets:
        here = offsets.index(0)

        @pl.when(r == 0)
        def _():
            def own(i, carry):
                two([(2 * i, here, 2 * i), (2 * i + 1, here, 2 * i + 1)], True)
                return carry

            lax.fori_loop(0, 2, own, 0)

    def note(at, choice, offset, qb, length, newest):
        code = meta[(r * 4 + qb) * RING + offset % RING]
        if offset == 0:
            valid, kb = (code >> choice) & 1, choice
        else:
            valid, kb = (code > 0).astype(jnp.int32), jnp.maximum(code - 1, 0)
        item = qb + at * 16 + kb * 256
        clash = valid & length & (newest == qb).astype(jnp.int32)
        todo[length] = jnp.where(clash == 1, IDLE, item)
        todo[length + 1] = item
        return length + valid * (1 + clash), jnp.where(valid == 1, qb, newest)

    found = (jnp.int32(0), jnp.int32(-1))
    for at, offset in enumerate(offsets):
        if offset == 0:
            found = lax.fori_loop(
                0, 16, lambda i, f, at=at: note(at, i >> 2, 0, i & 3, *f), found
            )
        else:
            found = lax.fori_loop(
                0, 4, lambda i, f, at=at, offset=offset: note(at, 0, offset, i, *f), found
            )
    length = found[0]
    todo[length] = IDLE

    def step(i, carry):
        items = []
        for side in (0, 1):
            item = todo[2 * i + side]
            items.append((item & 15, (item >> 4) & 15, item >> 8))
        two(items, False)
        return carry

    lax.fori_loop(0, (length + 1) >> 1, step, 0)

    def leave(acc_out, m_out, l_out):
        def copy(qb, carry):
            acc_out[qb] = acc[qb]
            m_out[qb] = m_run[qb]
            l_out[qb] = l_run[qb]
            return carry

        lax.fori_loop(0, 4, copy, 0)

    if not last:
        leave(*rest)
    else:
        packed_refs = rest[3:]

        @pl.when(r == 0)
        def _():
            leave(*rest[:3])

        def send(packed_ref, lead):
            def pack(qb, carry):
                pieces = []
                for value in (m_run[qb], l_run[qb]):
                    for _ in range(3):
                        piece = value.astype(jnp.bfloat16).astype(jnp.float32)
                        pieces.append(piece)
                        value = value - piece
                packed_ref[(*lead, qb, slice(heads * HEAD, None), slice(None))] = jnp.concatenate(pieces, axis=0).astype(
                    jnp.bfloat16
                )
                total = l_run[qb]
                inverse = 1.0 / jnp.where(total > 0, total, 1.0)
                for h in span:
                    packed_ref[(*lead, qb, cols[h], slice(None))] = (
                        acc[qb, cols[h], :] * inverse[h : h + 1]
                    ).astype(jnp.bfloat16)
                return carry

            lax.fori_loop(0, 4, pack, 0)

        if len(packed_refs) == 1:
            pl.when(r > 0)(lambda: send(packed_refs[0], (0,)))
        else:
            for row, packed_ref in enumerate(packed_refs):
                pl.when(r == row + 1)(functools.partial(send, packed_ref, ()))


def attend(meta, queries, chunk, offsets, keys, values, state, last):
    first_head, heads = chunk
    apart = first_head > 0
    width = heads * HEAD
    first = state is None
    acc_spec = pl.BlockSpec((4, width, BLOCK), lambda r, meta: (r, 0, 0))
    run_spec = pl.BlockSpec((4, 8, BLOCK), lambda r, meta: (r, 0, 0))
    state_specs = [acc_spec, run_spec, run_spec]
    in_specs = [
        pl.BlockSpec(
            (1, 512, width),
            lambda r, meta: (jnp.minimum(meta[16 * RING] + r, ROWS - 1), 0, first_head // heads),
        )
    ]
    in_specs += [pl.BlockSpec((4, width, BLOCK), lambda r, meta: (0, 0, 0))] * (2 * len(offsets))
    operands = [queries, *keys, *values]
    if not first:
        in_specs += state_specs
        operands += list(state)
    f32 = jnp.float32
    if last:
        out_shape = [
            jax.ShapeDtypeStruct((4, width, BLOCK), f32),
            jax.ShapeDtypeStruct((4, 8, BLOCK), f32),
            jax.ShapeDtypeStruct((4, 8, BLOCK), f32),
            *(
                [jax.ShapeDtypeStruct((4, width + STAT, BLOCK), jnp.bfloat16)] * 3
                if apart
                else [jax.ShapeDtypeStruct((ROWS, 4, width + STAT, BLOCK), jnp.bfloat16)]
            ),
        ]
        out_specs = [
            pl.BlockSpec((4, width, BLOCK), lambda r, meta: (0, 0, 0)),
            pl.BlockSpec((4, 8, BLOCK), lambda r, meta: (0, 0, 0)),
            pl.BlockSpec((4, 8, BLOCK), lambda r, meta: (0, 0, 0)),
            *(
                [pl.BlockSpec((4, width + STAT, BLOCK), lambda r, meta: (0, 0, 0))] * 3
                if apart
                else [            pl.BlockSpec((1, 4, width + STAT, BLOCK), lambda r, meta: ((meta[16 * RING] + jnp.maximum(r, 1)) & 3, 0, 0, 0))]
            ),
        ]
    else:
        out_shape = [
            jax.ShapeDtypeStruct((16, width, BLOCK), f32),
            jax.ShapeDtypeStruct((16, 8, BLOCK), f32),
            jax.ShapeDtypeStruct((16, 8, BLOCK), f32),
        ]
        out_specs = state_specs
    count = len(offsets)
    scratch = [
        pltpu.VMEM((5, width, BLOCK), f32),
        pltpu.VMEM((5, 8, BLOCK), f32),
        pltpu.VMEM((5, 8, BLOCK), f32),
        pltpu.VMEM((5 * BLOCK, width), jnp.bfloat16),
        pltpu.VMEM((count, 4, width, BLOCK), jnp.bfloat16),
        pltpu.VMEM((count, 4, width, BLOCK), jnp.bfloat16),
        pltpu.SMEM((80,), jnp.int32),
    ]
    return list(pl.pallas_call(
        functools.partial(attend_kernel, offsets, heads, first, last),
        out_shape=out_shape,
        grid_spec=pltpu.PrefetchScalarGridSpec(
            num_scalar_prefetch=1,
            grid=(ROWS,),
            in_specs=in_specs,
            out_specs=out_specs,
            scratch_shapes=scratch,
        ),
        compiler_params=pltpu.CompilerParams(vmem_limit_bytes=VMEM_LIMIT),
        cost_estimate=pl.CostEstimate(
            flops=int((2 + 3 * len(offsets)) * 1.1e9),
            bytes_accessed=1 << 20,
            transcendentals=0,
        ),
        name=f"attend_{first_head}_{'_'.join(str(o % RING) for o in offsets)}",
    )(meta, *operands))


def join_kernel(heads, acc_ref, m_ref, l_ref, one, two, three, *rest):
    out_ref = rest[-1]
    width = heads * HEAD
    tops, sums = [m_ref[0]], [l_ref[0]]
    for part in (one, two, three):
        stats = part[0, width:, :].astype(jnp.float32)
        top = (stats[16:24] + stats[8:16]) + stats[0:8]
        total = (stats[40:48] + stats[32:40]) + stats[24:32]
        tops.append(jnp.where(total > 0, top, NEG_FILL))
        sums.append(total)
    scale = HEAD**-0.5 * math.log2(math.e)
    highest = jnp.maximum(jnp.maximum(tops[0], tops[1]), jnp.maximum(tops[2], tops[3]))
    fades = [jnp.exp2((top - highest) * scale) for top in tops]
    shares = [fades[0]] + [fades[i] * sums[i] for i in (1, 2, 3)]
    whole = fades[0] * sums[0] + shares[1] + shares[2] + shares[3]
    inverse = 1.0 / whole
    for h in range(heads):
        cols = slice(h * HEAD, (h + 1) * HEAD)
        mixed = acc_ref[0, cols, :] * shares[0][h : h + 1, :]
        for i, part in enumerate((one, two, three)):
            mixed += part[0, cols, :].astype(jnp.float32) * shares[i + 1][h : h + 1, :]
        mixed = mixed * inverse[h : h + 1, :]
        out_ref[:, cols] = mixed.T.astype(jnp.bfloat16)


def join(chunk, state, parts, out):
    first_head, heads = chunk
    width = heads * HEAD
    in_specs = [
        pl.BlockSpec((1, width, BLOCK), lambda b: (b, 0, 0)),
        pl.BlockSpec((1, 8, BLOCK), lambda b: (b, 0, 0)),
        pl.BlockSpec((1, 8, BLOCK), lambda b: (b, 0, 0)),
    ] + [pl.BlockSpec((1, width + STAT, BLOCK), lambda b: (b, 0, 0))] * 3
    operands = [*state, *parts]
    aliases = {}
    if out is not None:
        aliases = {len(operands): 0}
        in_specs.append(pl.BlockSpec(memory_space=pl.ANY))
        operands.append(out)
    return pl.pallas_call(
        functools.partial(join_kernel, heads),
        out_shape=jax.ShapeDtypeStruct((512, 1024), jnp.bfloat16),
        grid=(4,),
        in_specs=in_specs,
        out_specs=pl.BlockSpec((BLOCK, width), lambda b: (b, first_head // heads)),
        input_output_aliases=aliases,
        compiler_params=pltpu.CompilerParams(vmem_limit_bytes=VMEM_LIMIT),
        cost_estimate=pl.CostEstimate(
            flops=512 * width * 10, bytes_accessed=512 * width * 14, transcendentals=0
        ),
        name=f"join_{first_head}",
    )(*operands)


def shift(value, axis, step):
    size = lax.axis_size(axis)
    return lax.ppermute(value, axis, [(i, (i + step) % size) for i in range(size)])


def to_row(value, step):
    moves = [(i, i + step) for i in range(ROWS) if 0 <= i + step < ROWS]
    return lax.ppermute(value, "y", moves)


def swap(value, axis, bit):
    size = lax.axis_size(axis)
    return lax.ppermute(value, axis, [(i, i ^ bit) for i in range(size)])


def after(value, *others):
    return lax.optimization_barrier((value, *others))[0]


class Wire:
    def __init__(self, side, sign, depth=2):
        self.side, self.sign, self.depth = side, sign, depth
        self.sent = []

    def send(self, name, ring, distance, *others):
        source = ring[-self.sign * (distance - 1)]
        waits = list(others)
        waits += self.sent[-self.depth - 1 : -self.depth + 1] if self.sent[1:] else []
        if waits:
            source = after(source, *waits)
        with jax.named_scope(f"{name}{distance}_{self.side}"):
            got = shift(source, "z", self.sign)
        self.sent.append(got)
        ring[-self.sign * distance if distance < 4 else 4] = got


def shards(query_states, key_states, value_states, gate_logits, selected_blocks):
    my_y, my_z = lax.axis_index("y"), lax.axis_index("z")
    gate_values = jax.nn.sigmoid(gate_logits.astype(jnp.float32))
    total = jnp.sum(gate_values, axis=1, keepdims=True)
    before = jnp.zeros_like(total)
    value_tiles = value_states.reshape(4, BLOCK, -1).transpose(0, 2, 1)
    va, vb = {0: value_tiles[:, : 4 * HEAD]}, {0: value_tiles[:, 4 * HEAD :]}
    right, left = Wire("right", 1), Wire("left", -1)
    for wire in (right, left):
        wire.send("va", va, 1)
    picks = selected_blocks.T.astype(jnp.float32)
    with jax.named_scope("prefix"):
        rows_before = before
        for bit in (1, 2):
            other = swap(jnp.concatenate([total, rows_before, picks], axis=1), "y", bit)
            if bit == 1:
                own_total = total
            rows_before = rows_before + jnp.where((my_y & bit) != 0, other[:, :1], 0.0)
            total = total + other[:, :1]
            picks = jnp.concatenate([picks, other[:, 2:]], axis=1)
        own_total = after(own_total, va[1], va[-1])
        for bit in (1, 2, 4):
            other = swap(jnp.concatenate([own_total, rows_before], axis=1), "z", bit)
            before = before + jnp.where((my_z & bit) != 0, other[:, :1], 0.0)
            own_total = own_total + other[:, :1]
            rows_before = rows_before + other[:, 1:]
    angles = before + rows_before + jnp.cumsum(gate_values, axis=1)
    query_rot, keys_a, keys_b = rotate(angles, query_states, key_states)
    ka, kb = {0: keys_a}, {0: keys_b}
    with jax.named_scope("queries"):
        queries = lax.all_to_all(query_rot, "y", 0, 0, tiled=True)

    picks = picks.astype(jnp.int32).T.reshape(4, 1, 4, 8)
    wanted = (my_y + lax.broadcasted_iota(jnp.int32, (4, 4, 1, 1), 1)) ^ my_y
    turn = lax.broadcasted_iota(jnp.int32, (4, 4, 1, 1), 0)
    blocks = jnp.sum(jnp.where(wanted == turn, picks, 0), axis=0).reshape(16, 1, 8)
    row = lax.broadcasted_iota(jnp.int32, (16, RING, 8), 0)
    distance = lax.broadcasted_iota(jnp.int32, (16, RING, 8), 1)
    own = ((my_y + row // 4) * RING + my_z) * 4 + row % 4
    hit = (blocks >> 5 == my_y) & (((blocks >> 2) - my_z) & 7 == distance)
    hit &= (blocks != own) & (my_y + row // 4 < ROWS)
    code = jnp.where(distance == 0, 1 << (blocks & 3), (blocks & 3) + 1)
    meta = jnp.sum(jnp.where(hit, code, 0), axis=2).reshape(-1)
    meta = jnp.concatenate([meta, my_y.astype(jnp.int32)[None]])

    def call(part, group, state, last):
        offsets = []
        for distance in group:
            offsets += [distance] if distance in (0, 4) else [-distance, distance]
        keys, values = (ka, va) if part == 0 else (kb, vb)
        return attend(
            meta,
            queries,
            CHUNKS[part],
            tuple(offsets),
            [keys[o] for o in offsets],
            [values[o] for o in offsets],
            state,
            last,
        )

    def pick(rows, step):
        return lax.dynamic_index_in_dim(rows, (my_y + step) & 3, 0, keepdims=False)

    for name, ring, distance in (
        ("ka", ka, 1),
        ("va", va, 2),
        ("ka", ka, 2),
        ("va", va, 3),
        ("ka", ka, 3),
    ):
        for wire in (right, left):
            wire.send(name, ring, distance)
    right.send("va", va, 4)
    left.send("vb", vb, 1)
    state = call(0, GROUPS[0][0], None, False)
    right.send("ka", ka, 4, state[1])
    left.send("kb", kb, 1, state[1])
    right.send("vb", vb, 1)
    left.send("vb", vb, 2)
    right.send("kb", kb, 1)
    left.send("kb", kb, 2)
    state = call(0, GROUPS[0][1], state, True)
    right.send("vb", vb, 2, state[1])
    left.send("vb", vb, 3, state[1])
    right.send("kb", kb, 2, state[1])
    left.send("kb", kb, 3, state[1])
    first_b = call(1, GROUPS[1][0], None, False)
    right.send("vb", vb, 3, first_b[1])
    left.send("vb", vb, 4, first_b[1])
    right.send("kb", kb, 3)
    second_b = call(1, GROUPS[1][1], first_b, False)
    left.send("kb", kb, 4, second_b[1])
    mine_a = state[:3]
    with jax.named_scope("partials_a"):
        parts_a = lax.all_to_all(state[3], "y", 0, 0, tiled=True)
    second_b[1] = after(second_b[1], parts_a)
    state = call(1, GROUPS[1][2], second_b, True)
    parts_b = []
    for s in (1, 2, 3):
        with jax.named_scope(f"partial_b{s}"):
            parts_b.append(to_row(state[2 + s], s))
    parts_a = after(parts_a, state[1])
    out = join(CHUNKS[0], mine_a, [pick(parts_a, -s) for s in (1, 2, 3)], None)
    return join(CHUNKS[1], state[:3], parts_b, out)


def solution(mesh):
    grid = Mesh(mesh.devices.reshape(2, ROWS, RING, 4), ("dp", "y", "z", "head"))
    tokens = ("dp", "y", "z")
    placed = (
        P(tokens, "head"),
        P(tokens, "head"),
        P(tokens, "head"),
        P("head", tokens),
        P(tokens, None),
    )
    return jax.shard_map(
        shards, mesh=grid, in_specs=placed, out_specs=P(tokens, "head"), check_vma=False
    )
```

```python
import functools
import math

import jax
import jax.numpy as jnp
from jax import lax
from jax.experimental import pallas as pl
from jax.experimental.pallas import tpu as pltpu
from jax.sharding import Mesh, PartitionSpec as P

BLOCK = 128
HEAD = 128
ROWS = 4
RING = 8
NEG_FILL = -1e30
ROPE_BASE = 10000.0
VMEM_LIMIT = 24 << 20
IDLE = 4
STAT = 48
CHUNKS = ((0, 4), (4, 4))
GROUPS = (((0, 1, 2), (3, 4)), ((0, 1), (2,), (3, 4)))


QUARTER = (1.5703125, 4.837512969970703e-4, 7.54978995489188216e-8)


def sin_cos(phase):
    turns = jnp.floor(phase * (2 / math.pi) + 0.5)
    x = phase
    for part in QUARTER:
        x = x - turns * part
    square = x * x
    sine = ((-1.9515295891e-4 * square + 8.3321608736e-3) * square - 1.6666654611e-1) * square
    sine = sine * x + x
    cosine = ((2.443315711809948e-5 * square - 1.388731625493765e-3) * square + 4.166664568298827e-2)
    cosine = cosine * square * square - 0.5 * square + 1.0
    quadrant = turns.astype(jnp.int32) & 3
    odd = (quadrant & 1) == 1
    sine, cosine = jnp.where(odd, cosine, sine), jnp.where(odd, sine, cosine)
    sine = jnp.where(quadrant >= 2, -sine, sine)
    cosine = jnp.where((quadrant == 1) | (quadrant == 2), -cosine, cosine)
    return sine, cosine


def rotate_kernel(angle_ref, freq_ref, q_ref, k_ref, *outs):
    freq = freq_ref[...]
    lane = lax.broadcasted_iota(jnp.int32, (BLOCK, HEAD), 1)
    low = lane < HEAD // 2
    heads = q_ref.shape[1] // HEAD
    for pair in range(heads // 2):
        even = angle_ref[:, 2 * pair : 2 * pair + 1]
        odd = angle_ref[:, 2 * pair + 1 : 2 * pair + 2]
        sine, cosine = sin_cos(jnp.where(low, even, odd) * freq)
        sine_turned = pltpu.roll(sine, HEAD // 2, 1)
        cosine_turned = pltpu.roll(cosine, HEAD // 2, 1)
        for h in (2 * pair, 2 * pair + 1):
            first, second = (sine, sine_turned) if h % 2 == 0 else (sine_turned, sine)
            signed = jnp.where(low, -first, second)
            first, second = (cosine, cosine_turned) if h % 2 == 0 else (cosine_turned, cosine)
            plain = jnp.where(low, first, second)
            cols = slice(h * HEAD, (h + 1) * HEAD)

            def turn(x):
                x = x.astype(jnp.float32)
                return (x * plain + pltpu.roll(x, HEAD // 2, 1) * signed).astype(jnp.bfloat16)

            part = slice(h % 4 * HEAD, (h % 4 + 1) * HEAD)
            query = turn(q_ref[:, cols])
            for row in range(ROWS):
                outs[0][row, :, cols] = query
            outs[1 + h // 4][0, part, :] = turn(k_ref[:, cols])


def rotate(angles, queries, keys):
    half = HEAD // 2
    inv_freq = ROPE_BASE ** (-jnp.arange(half).astype(jnp.float32) / half)
    inv_freq = jnp.concatenate([inv_freq, inv_freq])[None]
    heads = angles.shape[0]
    bf16 = jnp.bfloat16
    rows = pl.BlockSpec((BLOCK, heads * HEAD), lambda b: (b, 0))
    copies = pl.BlockSpec((ROWS, BLOCK, heads * HEAD), lambda b: (0, b, 0))
    tiled = pl.BlockSpec((1, 4 * HEAD, BLOCK), lambda b: (b, 0, 0))
    return pl.pallas_call(
        rotate_kernel,
        out_shape=[
            jax.ShapeDtypeStruct((ROWS, *queries.shape), bf16),
            jax.ShapeDtypeStruct((4, 4 * HEAD, BLOCK), bf16),
            jax.ShapeDtypeStruct((4, 4 * HEAD, BLOCK), bf16),
        ],
        grid=(4,),
        in_specs=[
            pl.BlockSpec((BLOCK, heads), lambda b: (b, 0)),
            pl.BlockSpec((1, HEAD), lambda b: (0, 0)),
            rows,
            rows,
        ],
        out_specs=[copies, tiled, tiled],
        compiler_params=pltpu.CompilerParams(vmem_limit_bytes=60 << 20),
        cost_estimate=pl.CostEstimate(flops=5 * 10**9, bytes_accessed=6 << 20, transcendentals=0),
        name="rotate",
    )(angles.T, inv_freq, queries, keys)


def attend_kernel(offsets, heads, first, last, rows, meta, *refs):
    count = len(offsets)
    given_q, refs = refs[0], refs[1:]
    k_refs, v_refs = refs[:count], refs[count : 2 * count]
    rest = list(refs[2 * count :])
    acc, m_run, l_run, q_ref, k_all, v_all, todo = rest[-7:]
    rest = rest[:-7]
    given = None
    if not first:
        given, rest = rest[:3], rest[3:]
    r = pl.program_id(0) + rows[0]
    scale = HEAD**-0.5 * math.log2(math.e)

    @pl.when(pl.program_id(0) == 0)
    def _():
        def hold(kb, carry):
            for at in range(count):
                k_all[at, kb] = k_refs[at][kb]
                v_all[at, kb] = v_refs[at][kb]
            return carry

        lax.fori_loop(0, 4, hold, 0)
        q_ref[IDLE * BLOCK :, :] = jnp.zeros((BLOCK, heads * HEAD), jnp.bfloat16)
        acc[IDLE] = jnp.zeros((heads * HEAD, BLOCK), jnp.float32)
        m_run[IDLE] = jnp.full((8, BLOCK), NEG_FILL)
        l_run[IDLE] = jnp.zeros((8, BLOCK), jnp.float32)

    def enter(qb, carry):
        q_rows = pl.ds(pl.multiple_of(qb * BLOCK, BLOCK), BLOCK)
        q_ref[q_rows, :] = given_q[0, q_rows, :]
        if first:
            acc[qb] = jnp.zeros((heads * HEAD, BLOCK), jnp.float32)
            m_run[qb] = jnp.full((8, BLOCK), NEG_FILL)
            l_run[qb] = jnp.zeros((8, BLOCK), jnp.float32)
        else:
            acc[qb] = given[0][qb]
            m_run[qb] = given[1][qb]
            l_run[qb] = given[2][qb]
        return carry

    lax.fori_loop(0, 4, enter, 0)

    span = range(heads)
    cols = [slice(h * HEAD, (h + 1) * HEAD) for h in span]

    def two(items, causal):
        olds, scores = [], []
        for qb, at, kb in items:
            q_rows = pl.ds(pl.multiple_of(qb * BLOCK, BLOCK), BLOCK)
            olds.append((m_run[qb], l_run[qb]))
            scores.append(
                [
                    lax.dot_general(
                        k_all[at, kb, cols[h], :],
                        q_ref[q_rows, cols[h]],
                        (((1,), (1,)), ((), ())),
                        preferred_element_type=jnp.float32,
                    )
                    for h in span
                ]
            )
        if causal:
            key_pos = lax.broadcasted_iota(jnp.int32, (BLOCK, BLOCK), 0)
            query_pos = lax.broadcasted_iota(jnp.int32, (BLOCK, BLOCK), 1)
            seen = key_pos <= query_pos
            scores = [[jnp.where(seen, s, NEG_FILL) for s in group] for group in scores]
        results = []
        for (qb, at, kb), (m_old, l_old), group in zip(items, olds, scores):
            tops = [jnp.max(s, axis=0, keepdims=True) for s in group]
            if heads < 8:
                tops.append(m_old[heads:])
            m_new = jnp.maximum(m_old, jnp.concatenate(tops, axis=0))
            fade = jnp.exp2((m_old - m_new) * scale)
            weights = [jnp.exp2((group[h] - m_new[h : h + 1]) * scale) for h in span]
            sums = [jnp.sum(w, axis=0, keepdims=True) for w in weights]
            if heads < 8:
                sums.append(jnp.zeros((8 - heads, BLOCK), jnp.float32))
            mixed = [
                jnp.dot(
                    v_all[at, kb, cols[h], :],
                    weights[h].astype(jnp.bfloat16),
                    preferred_element_type=jnp.float32,
                )
                for h in span
            ]
            results.append((m_new, l_old * fade + jnp.concatenate(sums, axis=0), fade, mixed))
        wholes = [
            [acc[qb, cols[h], :] * fade[h : h + 1] + mixed[h] for h in span]
            for (qb, _, _), (_, _, fade, mixed) in zip(items, results)
        ]
        for (qb, _, _), (m_new, l_new, _, _), whole in zip(items, results, wholes):
            m_run[qb] = m_new
            l_run[qb] = l_new
            for h in span:
                acc[qb, cols[h], :] = whole[h]

    if 0 in offsets:
        here = offsets.index(0)

        @pl.when(r == 0)
        def _():
            def own(i, carry):
                two([(2 * i, here, 2 * i), (2 * i + 1, here, 2 * i + 1)], True)
                return carry

            lax.fori_loop(0, 2, own, 0)

    def note(at, choice, offset, qb, length, newest):
        code = meta[(r * 4 + qb) * RING + offset % RING]
        if offset == 0:
            valid, kb = (code >> choice) & 1, choice
        else:
            valid, kb = (code > 0).astype(jnp.int32), jnp.maximum(code - 1, 0)
        item = qb + at * 16 + kb * 256
        clash = valid & length & (newest == qb).astype(jnp.int32)
        todo[length] = jnp.where(clash == 1, IDLE, item)
        todo[length + 1] = item
        return length + valid * (1 + clash), jnp.where(valid == 1, qb, newest)

    found = (jnp.int32(0), jnp.int32(-1))
    for at, offset in enumerate(offsets):
        if offset == 0:
            found = lax.fori_loop(
                0, 16, lambda i, f, at=at: note(at, i >> 2, 0, i & 3, *f), found
            )
        else:
            found = lax.fori_loop(
                0, 4, lambda i, f, at=at, offset=offset: note(at, 0, offset, i, *f), found
            )
    length = found[0]
    todo[length] = IDLE

    def step(i, carry):
        items = []
        for side in (0, 1):
            item = todo[2 * i + side]
            items.append((item & 15, (item >> 4) & 15, item >> 8))
        two(items, False)
        return carry

    lax.fori_loop(0, (length + 1) >> 1, step, 0)

    def leave(acc_out, m_out, l_out):
        def copy(qb, carry):
            acc_out[qb] = acc[qb]
            m_out[qb] = m_run[qb]
            l_out[qb] = l_run[qb]
            return carry

        lax.fori_loop(0, 4, copy, 0)

    if not last:
        leave(*rest)
    else:
        packed_refs = rest
        if 0 in rows:
            packed_refs = rest[3:]

            @pl.when(r == 0)
            def _():
                leave(*rest[:3])

        def send(packed_ref, lead):
            def pack(qb, carry):
                pieces = []
                for value in (m_run[qb], l_run[qb]):
                    for _ in range(3):
                        piece = value.astype(jnp.bfloat16).astype(jnp.float32)
                        pieces.append(piece)
                        value = value - piece
                packed_ref[(*lead, qb, slice(heads * HEAD, None), slice(None))] = jnp.concatenate(pieces, axis=0).astype(
                    jnp.bfloat16
                )
                total = l_run[qb]
                inverse = 1.0 / jnp.where(total > 0, total, 1.0)
                for h in span:
                    packed_ref[(*lead, qb, cols[h], slice(None))] = (
                        acc[qb, cols[h], :] * inverse[h : h + 1]
                    ).astype(jnp.bfloat16)
                return carry

            lax.fori_loop(0, 4, pack, 0)

        if len(packed_refs) == 1:
            pl.when(r > 0)(lambda: send(packed_refs[0], (0,)))
        else:
            for row, packed_ref in enumerate(packed_refs):
                pl.when(r == row + 1)(functools.partial(send, packed_ref, ()))


def attend(meta, queries, chunk, offsets, keys, values, state, last, rows=(0, 1, 2, 3), grant=VMEM_LIMIT):
    first_head, heads = chunk
    apart = first_head > 0
    begin = rows[0]
    width = heads * HEAD
    first = state is None
    acc_spec = pl.BlockSpec((4, width, BLOCK), lambda r, meta: (r + begin, 0, 0))
    run_spec = pl.BlockSpec((4, 8, BLOCK), lambda r, meta: (r + begin, 0, 0))
    state_specs = [acc_spec, run_spec, run_spec]
    in_specs = [
        pl.BlockSpec(
            (1, 512, width),
            lambda r, meta: (jnp.minimum(meta[16 * RING] + r + begin, ROWS - 1), 0, first_head // heads),
        )
    ]
    in_specs += [pl.BlockSpec((4, width, BLOCK), lambda r, meta: (0, 0, 0))] * (2 * len(offsets))
    operands = [queries, *keys, *values]
    if not first:
        in_specs += state_specs
        operands += list(state)
    f32 = jnp.float32
    if last:
        out_shape = [
            jax.ShapeDtypeStruct((4, width, BLOCK), f32),
            jax.ShapeDtypeStruct((4, 8, BLOCK), f32),
            jax.ShapeDtypeStruct((4, 8, BLOCK), f32),
            *(
                [jax.ShapeDtypeStruct((4, width + STAT, BLOCK), jnp.bfloat16)] * 3
                if apart
                else [jax.ShapeDtypeStruct((ROWS, 4, width + STAT, BLOCK), jnp.bfloat16)]
            ),
        ]
        out_specs = [
            pl.BlockSpec((4, width, BLOCK), lambda r, meta: (0, 0, 0)),
            pl.BlockSpec((4, 8, BLOCK), lambda r, meta: (0, 0, 0)),
            pl.BlockSpec((4, 8, BLOCK), lambda r, meta: (0, 0, 0)),
            *(
                [pl.BlockSpec((4, width + STAT, BLOCK), lambda r, meta: (0, 0, 0))] * 3
                if apart
                else [            pl.BlockSpec((1, 4, width + STAT, BLOCK), lambda r, meta: ((meta[16 * RING] + jnp.maximum(r, 1)) & 3, 0, 0, 0))]
            ),
        ]
        if apart:
            out_shape = out_shape[:3] if rows == (0,) else out_shape[3:]
            out_specs = out_specs[:3] if rows == (0,) else out_specs[3:]
    else:
        out_shape = [
            jax.ShapeDtypeStruct((16, width, BLOCK), f32),
            jax.ShapeDtypeStruct((16, 8, BLOCK), f32),
            jax.ShapeDtypeStruct((16, 8, BLOCK), f32),
        ]
        out_specs = state_specs
    count = len(offsets)
    scratch = [
        pltpu.VMEM((5, width, BLOCK), f32),
        pltpu.VMEM((5, 8, BLOCK), f32),
        pltpu.VMEM((5, 8, BLOCK), f32),
        pltpu.VMEM((5 * BLOCK, width), jnp.bfloat16),
        pltpu.VMEM((count, 4, width, BLOCK), jnp.bfloat16),
        pltpu.VMEM((count, 4, width, BLOCK), jnp.bfloat16),
        pltpu.SMEM((80,), jnp.int32),
    ]
    return list(pl.pallas_call(
        functools.partial(attend_kernel, offsets, heads, first, last, rows),
        out_shape=out_shape,
        grid_spec=pltpu.PrefetchScalarGridSpec(
            num_scalar_prefetch=1,
            grid=(len(rows),),
            in_specs=in_specs,
            out_specs=out_specs,
            scratch_shapes=scratch,
        ),
        compiler_params=pltpu.CompilerParams(vmem_limit_bytes=grant),
        cost_estimate=pl.CostEstimate(
            flops=int((2 + 3 * len(offsets)) * 1.1e9),
            bytes_accessed=1 << 20,
            transcendentals=0,
        ),
        name=f"attend_{first_head}_{'_'.join(str(o % RING) for o in offsets)}_row{begin}",
    )(meta, *operands))


def join_kernel(heads, acc_ref, m_ref, l_ref, one, two, three, *rest):
    out_ref = rest[-1]
    width = heads * HEAD
    tops, sums = [m_ref[0]], [l_ref[0]]
    for part in (one, two, three):
        stats = part[0, width:, :].astype(jnp.float32)
        top = (stats[16:24] + stats[8:16]) + stats[0:8]
        total = (stats[40:48] + stats[32:40]) + stats[24:32]
        tops.append(jnp.where(total > 0, top, NEG_FILL))
        sums.append(total)
    scale = HEAD**-0.5 * math.log2(math.e)
    highest = jnp.maximum(jnp.maximum(tops[0], tops[1]), jnp.maximum(tops[2], tops[3]))
    fades = [jnp.exp2((top - highest) * scale) for top in tops]
    shares = [fades[0]] + [fades[i] * sums[i] for i in (1, 2, 3)]
    whole = fades[0] * sums[0] + shares[1] + shares[2] + shares[3]
    inverse = 1.0 / whole
    for h in range(heads):
        cols = slice(h * HEAD, (h + 1) * HEAD)
        mixed = acc_ref[0, cols, :] * shares[0][h : h + 1, :]
        for i, part in enumerate((one, two, three)):
            mixed += part[0, cols, :].astype(jnp.float32) * shares[i + 1][h : h + 1, :]
        mixed = mixed * inverse[h : h + 1, :]
        out_ref[:, cols] = mixed.T.astype(jnp.bfloat16)


def join(chunk, state, parts, out):
    first_head, heads = chunk
    width = heads * HEAD
    in_specs = [
        pl.BlockSpec((1, width, BLOCK), lambda b: (b, 0, 0)),
        pl.BlockSpec((1, 8, BLOCK), lambda b: (b, 0, 0)),
        pl.BlockSpec((1, 8, BLOCK), lambda b: (b, 0, 0)),
    ] + [pl.BlockSpec((1, width + STAT, BLOCK), lambda b: (b, 0, 0))] * 3
    operands = [*state, *parts]
    aliases = {}
    if out is not None:
        aliases = {len(operands): 0}
        in_specs.append(pl.BlockSpec(memory_space=pl.ANY))
        operands.append(out)
    return pl.pallas_call(
        functools.partial(join_kernel, heads),
        out_shape=jax.ShapeDtypeStruct((512, 1024), jnp.bfloat16),
        grid=(4,),
        in_specs=in_specs,
        out_specs=pl.BlockSpec((BLOCK, width), lambda b: (b, first_head // heads)),
        input_output_aliases=aliases,
        compiler_params=pltpu.CompilerParams(vmem_limit_bytes=VMEM_LIMIT),
        cost_estimate=pl.CostEstimate(
            flops=512 * width * 10, bytes_accessed=512 * width * 14, transcendentals=0
        ),
        name=f"join_{first_head}",
    )(*operands)


def shift(value, axis, step):
    size = lax.axis_size(axis)
    return lax.ppermute(value, axis, [(i, (i + step) % size) for i in range(size)])


def to_row(value, step):
    moves = [(i, i + step) for i in range(ROWS) if 0 <= i + step < ROWS]
    return lax.ppermute(value, "y", moves)


def swap(value, axis, bit):
    size = lax.axis_size(axis)
    return lax.ppermute(value, axis, [(i, i ^ bit) for i in range(size)])


def after(value, *others):
    return lax.optimization_barrier((value, *others))[0]


class Wire:
    def __init__(self, side, sign, depth=2):
        self.side, self.sign, self.depth = side, sign, depth
        self.sent = []

    def send(self, name, ring, distance, *others):
        source = ring[-self.sign * (distance - 1)]
        waits = list(others)
        waits += self.sent[-self.depth - 1 : -self.depth + 1] if self.sent[1:] else []
        if waits:
            source = after(source, *waits)
        with jax.named_scope(f"{name}{distance}_{self.side}"):
            got = shift(source, "z", self.sign)
        self.sent.append(got)
        ring[-self.sign * distance if distance < 4 else 4] = got


def shards(query_states, key_states, value_states, gate_logits, selected_blocks):
    my_y, my_z = lax.axis_index("y"), lax.axis_index("z")
    gate_values = jax.nn.sigmoid(gate_logits.astype(jnp.float32))
    total = jnp.sum(gate_values, axis=1, keepdims=True)
    before = jnp.zeros_like(total)
    value_tiles = value_states.reshape(4, BLOCK, -1).transpose(0, 2, 1)
    va, vb = {0: value_tiles[:, : 4 * HEAD]}, {0: value_tiles[:, 4 * HEAD :]}
    right, left = Wire("right", 1), Wire("left", -1)
    for wire in (right, left):
        wire.send("va", va, 1)
    picks = selected_blocks.T.astype(jnp.float32)
    with jax.named_scope("prefix"):
        rows_before = before
        for bit in (1, 2):
            other = swap(jnp.concatenate([total, rows_before, picks], axis=1), "y", bit)
            if bit == 1:
                own_total = total
            rows_before = rows_before + jnp.where((my_y & bit) != 0, other[:, :1], 0.0)
            total = total + other[:, :1]
            picks = jnp.concatenate([picks, other[:, 2:]], axis=1)
        own_total = after(own_total, va[1], va[-1])
        for bit in (1, 2, 4):
            other = swap(jnp.concatenate([own_total, rows_before], axis=1), "z", bit)
            before = before + jnp.where((my_z & bit) != 0, other[:, :1], 0.0)
            own_total = own_total + other[:, :1]
            rows_before = rows_before + other[:, 1:]
    angles = before + rows_before + jnp.cumsum(gate_values, axis=1)
    query_rot, keys_a, keys_b = rotate(angles, query_states, key_states)
    ka, kb = {0: keys_a}, {0: keys_b}
    with jax.named_scope("queries"):
        queries = lax.all_to_all(query_rot, "y", 0, 0, tiled=True)

    picks = picks.astype(jnp.int32).T.reshape(4, 1, 4, 8)
    wanted = (my_y + lax.broadcasted_iota(jnp.int32, (4, 4, 1, 1), 1)) ^ my_y
    turn = lax.broadcasted_iota(jnp.int32, (4, 4, 1, 1), 0)
    blocks = jnp.sum(jnp.where(wanted == turn, picks, 0), axis=0).reshape(16, 1, 8)
    row = lax.broadcasted_iota(jnp.int32, (16, RING, 8), 0)
    distance = lax.broadcasted_iota(jnp.int32, (16, RING, 8), 1)
    own = ((my_y + row // 4) * RING + my_z) * 4 + row % 4
    hit = (blocks >> 5 == my_y) & (((blocks >> 2) - my_z) & 7 == distance)
    hit &= (blocks != own) & (my_y + row // 4 < ROWS)
    code = jnp.where(distance == 0, 1 << (blocks & 3), (blocks & 3) + 1)
    meta = jnp.sum(jnp.where(hit, code, 0), axis=2).reshape(-1)
    meta = jnp.concatenate([meta, my_y.astype(jnp.int32)[None]])

    def call(part, group, state, last, **more):
        offsets = []
        for distance in group:
            offsets += [distance] if distance in (0, 4) else [-distance, distance]
        keys, values = (ka, va) if part == 0 else (kb, vb)
        return attend(
            meta,
            queries,
            CHUNKS[part],
            tuple(offsets),
            [keys[o] for o in offsets],
            [values[o] for o in offsets],
            state,
            last,
            **more,
        )

    def pick(rows, step):
        return lax.dynamic_index_in_dim(rows, (my_y + step) & 3, 0, keepdims=False)

    for name, ring, distance in (
        ("ka", ka, 1),
        ("va", va, 2),
        ("ka", ka, 2),
        ("va", va, 3),
        ("ka", ka, 3),
    ):
        for wire in (right, left):
            wire.send(name, ring, distance)
    right.send("va", va, 4)
    left.send("vb", vb, 1)
    state = call(0, GROUPS[0][0], None, False)
    right.send("ka", ka, 4, state[1])
    left.send("kb", kb, 1, state[1])
    right.send("vb", vb, 1)
    left.send("vb", vb, 2)
    right.send("kb", kb, 1)
    left.send("kb", kb, 2)
    state = call(0, GROUPS[0][1], state, True)
    right.send("vb", vb, 2, state[1])
    left.send("vb", vb, 3, state[1])
    right.send("kb", kb, 2, state[1])
    left.send("kb", kb, 3, state[1])
    first_b = call(1, GROUPS[1][0], None, False)
    right.send("vb", vb, 3, first_b[1])
    left.send("vb", vb, 4, first_b[1])
    right.send("kb", kb, 3)
    second_b = call(1, GROUPS[1][1], first_b, False, grant=60 << 20)
    left.send("kb", kb, 4, second_b[1])
    mine_a = state[:3]
    with jax.named_scope("partials_a"):
        parts_a = lax.all_to_all(state[3], "y", 0, 0, tiled=True)
    second_b[1] = after(second_b[1], parts_a)
    sends = call(1, GROUPS[1][2], second_b, True, rows=(1, 2, 3), grant=60 << 20)
    parts_b = []
    for s in (1, 2, 3):
        with jax.named_scope(f"partial_b{s}"):
            parts_b.append(to_row(sends[s - 1], s))
    second_b[1] = after(second_b[1], sends[0])
    state = call(1, GROUPS[1][2], second_b, True, rows=(0,), grant=60 << 20)
    parts_a = after(parts_a, state[1])
    out = join(CHUNKS[0], mine_a, [pick(parts_a, -s) for s in (1, 2, 3)], None)
    return join(CHUNKS[1], state[:3], parts_b, out)


def solution(mesh):
    grid = Mesh(mesh.devices.reshape(2, ROWS, RING, 4), ("dp", "y", "z", "head"))
    tokens = ("dp", "y", "z")
    placed = (
        P(tokens, "head"),
        P(tokens, "head"),
        P(tokens, "head"),
        P("head", tokens),
        P(tokens, None),
    )
    return jax.shard_map(
        shards, mesh=grid, in_specs=placed, out_specs=P(tokens, "head"), check_vma=False
    )
```

```python
import functools
import math

import jax
import jax.numpy as jnp
from jax import lax
from jax.experimental import pallas as pl
from jax.experimental.pallas import tpu as pltpu
from jax.sharding import Mesh, PartitionSpec as P

BLOCK = 128
HEAD = 128
ROWS = 4
RING = 8
NEG_FILL = -1e30
ROPE_BASE = 10000.0
VMEM_LIMIT = 24 << 20
IDLE = 4
STAT = 48
CHUNKS = ((0, 4), (4, 4))
GROUPS = (((0, 1, 2), (3, 4)), ((0, 1), (2,), (3, 4)))


QUARTER = (1.5703125, 4.837512969970703e-4, 7.54978995489188216e-8)


def sin_cos(phase):
    turns = jnp.floor(phase * (2 / math.pi) + 0.5)
    x = phase
    for part in QUARTER:
        x = x - turns * part
    square = x * x
    sine = ((-1.9515295891e-4 * square + 8.3321608736e-3) * square - 1.6666654611e-1) * square
    sine = sine * x + x
    cosine = ((2.443315711809948e-5 * square - 1.388731625493765e-3) * square + 4.166664568298827e-2)
    cosine = cosine * square * square - 0.5 * square + 1.0
    quadrant = turns.astype(jnp.int32) & 3
    odd = (quadrant & 1) == 1
    sine, cosine = jnp.where(odd, cosine, sine), jnp.where(odd, sine, cosine)
    sine = jnp.where(quadrant >= 2, -sine, sine)
    cosine = jnp.where((quadrant == 1) | (quadrant == 2), -cosine, cosine)
    return sine, cosine


def rotate_kernel(angle_ref, freq_ref, q_ref, k_ref, *outs):
    freq = freq_ref[...]
    lane = lax.broadcasted_iota(jnp.int32, (BLOCK, HEAD), 1)
    low = lane < HEAD // 2
    heads = q_ref.shape[1] // HEAD
    for pair in range(heads // 2):
        even = angle_ref[:, 2 * pair : 2 * pair + 1]
        odd = angle_ref[:, 2 * pair + 1 : 2 * pair + 2]
        sine, cosine = sin_cos(jnp.where(low, even, odd) * freq)
        sine_turned = pltpu.roll(sine, HEAD // 2, 1)
        cosine_turned = pltpu.roll(cosine, HEAD // 2, 1)
        for h in (2 * pair, 2 * pair + 1):
            first, second = (sine, sine_turned) if h % 2 == 0 else (sine_turned, sine)
            signed = jnp.where(low, -first, second)
            first, second = (cosine, cosine_turned) if h % 2 == 0 else (cosine_turned, cosine)
            plain = jnp.where(low, first, second)
            cols = slice(h * HEAD, (h + 1) * HEAD)

            def turn(x):
                x = x.astype(jnp.float32)
                return (x * plain + pltpu.roll(x, HEAD // 2, 1) * signed).astype(jnp.bfloat16)

            part = slice(h % 4 * HEAD, (h % 4 + 1) * HEAD)
            query = turn(q_ref[:, cols])
            for row in range(ROWS):
                outs[0][row, :, cols] = query
            outs[1 + h // 4][0, part, :] = turn(k_ref[:, cols])


def rotate(angles, queries, keys):
    half = HEAD // 2
    inv_freq = ROPE_BASE ** (-jnp.arange(half).astype(jnp.float32) / half)
    inv_freq = jnp.concatenate([inv_freq, inv_freq])[None]
    heads = angles.shape[0]
    bf16 = jnp.bfloat16
    rows = pl.BlockSpec((BLOCK, heads * HEAD), lambda b: (b, 0))
    copies = pl.BlockSpec((ROWS, BLOCK, heads * HEAD), lambda b: (0, b, 0))
    tiled = pl.BlockSpec((1, 4 * HEAD, BLOCK), lambda b: (b, 0, 0))
    return pl.pallas_call(
        rotate_kernel,
        out_shape=[
            jax.ShapeDtypeStruct((ROWS, *queries.shape), bf16),
            jax.ShapeDtypeStruct((4, 4 * HEAD, BLOCK), bf16),
            jax.ShapeDtypeStruct((4, 4 * HEAD, BLOCK), bf16),
        ],
        grid=(4,),
        in_specs=[
            pl.BlockSpec((BLOCK, heads), lambda b: (b, 0)),
            pl.BlockSpec((1, HEAD), lambda b: (0, 0)),
            rows,
            rows,
        ],
        out_specs=[copies, tiled, tiled],
        compiler_params=pltpu.CompilerParams(vmem_limit_bytes=60 << 20),
        cost_estimate=pl.CostEstimate(flops=5 * 10**9, bytes_accessed=6 << 20, transcendentals=0),
        name="rotate",
    )(angles.T, inv_freq, queries, keys)


def attend_kernel(offsets, heads, first, last, rows, meta, *refs):
    count = len(offsets)
    given_q, refs = refs[0], refs[1:]
    k_refs, v_refs = refs[:count], refs[count : 2 * count]
    rest = list(refs[2 * count :])
    acc, m_run, l_run, q_ref, k_all, v_all, todo = rest[-7:]
    rest = rest[:-7]
    given = None
    if not first:
        given, rest = rest[:3], rest[3:]
    r = pl.program_id(0) + rows[0]
    scale = HEAD**-0.5 * math.log2(math.e)

    @pl.when(pl.program_id(0) == 0)
    def _():
        def hold(kb, carry):
            for at in range(count):
                k_all[at, kb] = k_refs[at][kb]
                v_all[at, kb] = v_refs[at][kb]
            return carry

        lax.fori_loop(0, 4, hold, 0)
        q_ref[IDLE * BLOCK :, :] = jnp.zeros((BLOCK, heads * HEAD), jnp.bfloat16)
        acc[IDLE] = jnp.zeros((heads * HEAD, BLOCK), jnp.float32)
        m_run[IDLE] = jnp.full((8, BLOCK), NEG_FILL)
        l_run[IDLE] = jnp.zeros((8, BLOCK), jnp.float32)

    def enter(qb, carry):
        q_rows = pl.ds(pl.multiple_of(qb * BLOCK, BLOCK), BLOCK)
        q_ref[q_rows, :] = given_q[0, q_rows, :]
        if first:
            acc[qb] = jnp.zeros((heads * HEAD, BLOCK), jnp.float32)
            m_run[qb] = jnp.full((8, BLOCK), NEG_FILL)
            l_run[qb] = jnp.zeros((8, BLOCK), jnp.float32)
        else:
            acc[qb] = given[0][qb]
            m_run[qb] = given[1][qb]
            l_run[qb] = given[2][qb]
        return carry

    lax.fori_loop(0, 4, enter, 0)

    span = range(heads)
    cols = [slice(h * HEAD, (h + 1) * HEAD) for h in span]

    def two(items, causal):
        olds, scores = [], []
        for qb, at, kb in items:
            q_rows = pl.ds(pl.multiple_of(qb * BLOCK, BLOCK), BLOCK)
            olds.append((m_run[qb], l_run[qb]))
            scores.append(
                [
                    lax.dot_general(
                        k_all[at, kb, cols[h], :],
                        q_ref[q_rows, cols[h]],
                        (((1,), (1,)), ((), ())),
                        preferred_element_type=jnp.float32,
                    )
                    for h in span
                ]
            )
        if causal:
            key_pos = lax.broadcasted_iota(jnp.int32, (BLOCK, BLOCK), 0)
            query_pos = lax.broadcasted_iota(jnp.int32, (BLOCK, BLOCK), 1)
            seen = key_pos <= query_pos
            scores = [[jnp.where(seen, s, NEG_FILL) for s in group] for group in scores]
        results = []
        for (qb, at, kb), (m_old, l_old), group in zip(items, olds, scores):
            tops = [jnp.max(s, axis=0, keepdims=True) for s in group]
            if heads < 8:
                tops.append(m_old[heads:])
            m_new = jnp.maximum(m_old, jnp.concatenate(tops, axis=0))
            fade = jnp.exp2((m_old - m_new) * scale)
            weights = [jnp.exp2((group[h] - m_new[h : h + 1]) * scale) for h in span]
            sums = [jnp.sum(w, axis=0, keepdims=True) for w in weights]
            if heads < 8:
                sums.append(jnp.zeros((8 - heads, BLOCK), jnp.float32))
            mixed = [
                jnp.dot(
                    v_all[at, kb, cols[h], :],
                    weights[h].astype(jnp.bfloat16),
                    preferred_element_type=jnp.float32,
                )
                for h in span
            ]
            results.append((m_new, l_old * fade + jnp.concatenate(sums, axis=0), fade, mixed))
        wholes = [
            [acc[qb, cols[h], :] * fade[h : h + 1] + mixed[h] for h in span]
            for (qb, _, _), (_, _, fade, mixed) in zip(items, results)
        ]
        for (qb, _, _), (m_new, l_new, _, _), whole in zip(items, results, wholes):
            m_run[qb] = m_new
            l_run[qb] = l_new
            for h in span:
                acc[qb, cols[h], :] = whole[h]

    if 0 in offsets:
        here = offsets.index(0)

        @pl.when(r == 0)
        def _():
            def own(i, carry):
                two([(2 * i, here, 2 * i), (2 * i + 1, here, 2 * i + 1)], True)
                return carry

            lax.fori_loop(0, 2, own, 0)

    def note(at, choice, offset, qb, length, newest):
        code = meta[(r * 4 + qb) * RING + offset % RING]
        if offset == 0:
            valid, kb = (code >> choice) & 1, choice
        else:
            valid, kb = (code > 0).astype(jnp.int32), jnp.maximum(code - 1, 0)
        item = qb + at * 16 + kb * 256
        clash = valid & length & (newest == qb).astype(jnp.int32)
        todo[length] = jnp.where(clash == 1, IDLE, item)
        todo[length + 1] = item
        return length + valid * (1 + clash), jnp.where(valid == 1, qb, newest)

    found = (jnp.int32(0), jnp.int32(-1))
    for at, offset in enumerate(offsets):
        if offset == 0:
            found = lax.fori_loop(
                0, 16, lambda i, f, at=at: note(at, i >> 2, 0, i & 3, *f), found
            )
        else:
            found = lax.fori_loop(
                0, 4, lambda i, f, at=at, offset=offset: note(at, 0, offset, i, *f), found
            )
    length = found[0]
    todo[length] = IDLE

    def step(i, carry):
        items = []
        for side in (0, 1):
            item = todo[2 * i + side]
            items.append((item & 15, (item >> 4) & 15, item >> 8))
        two(items, False)
        return carry

    lax.fori_loop(0, (length + 1) >> 1, step, 0)

    def leave(acc_out, m_out, l_out):
        def copy(qb, carry):
            acc_out[qb] = acc[qb]
            m_out[qb] = m_run[qb]
            l_out[qb] = l_run[qb]
            return carry

        lax.fori_loop(0, 4, copy, 0)

    if not last:
        leave(*rest)
    else:
        packed_refs = rest
        if 0 in rows:
            packed_refs = rest[3:]

            @pl.when(r == 0)
            def _():
                leave(*rest[:3])

        def send(packed_ref, lead):
            def pack(qb, carry):
                pieces = []
                for value in (m_run[qb], l_run[qb]):
                    for _ in range(3):
                        piece = value.astype(jnp.bfloat16).astype(jnp.float32)
                        pieces.append(piece)
                        value = value - piece
                packed_ref[(*lead, qb, slice(heads * HEAD, None), slice(None))] = jnp.concatenate(pieces, axis=0).astype(
                    jnp.bfloat16
                )
                total = l_run[qb]
                inverse = 1.0 / jnp.where(total > 0, total, 1.0)
                for h in span:
                    packed_ref[(*lead, qb, cols[h], slice(None))] = (
                        acc[qb, cols[h], :] * inverse[h : h + 1]
                    ).astype(jnp.bfloat16)
                return carry

            lax.fori_loop(0, 4, pack, 0)

        if len(packed_refs) == 1:
            pl.when(r > 0)(lambda: send(packed_refs[0], (0,)))
        else:
            for row, packed_ref in enumerate(packed_refs):
                pl.when(r == row + 1)(functools.partial(send, packed_ref, ()))


def attend(meta, queries, chunk, offsets, keys, values, state, last, rows=(0, 1, 2, 3), grant=VMEM_LIMIT):
    first_head, heads = chunk
    apart = first_head > 0
    begin = rows[0]
    width = heads * HEAD
    first = state is None
    acc_spec = pl.BlockSpec((4, width, BLOCK), lambda r, meta: (r + begin, 0, 0))
    run_spec = pl.BlockSpec((4, 8, BLOCK), lambda r, meta: (r + begin, 0, 0))
    state_specs = [acc_spec, run_spec, run_spec]
    in_specs = [
        pl.BlockSpec(
            (1, 512, width),
            lambda r, meta: (jnp.minimum(meta[16 * RING] + r + begin, ROWS - 1), 0, first_head // heads),
        )
    ]
    in_specs += [pl.BlockSpec((4, width, BLOCK), lambda r, meta: (0, 0, 0))] * (2 * len(offsets))
    operands = [queries, *keys, *values]
    if not first:
        in_specs += state_specs
        operands += list(state)
    f32 = jnp.float32
    if last:
        out_shape = [
            jax.ShapeDtypeStruct((4, width, BLOCK), f32),
            jax.ShapeDtypeStruct((4, 8, BLOCK), f32),
            jax.ShapeDtypeStruct((4, 8, BLOCK), f32),
            *(
                [jax.ShapeDtypeStruct((4, width + STAT, BLOCK), jnp.bfloat16)] * 3
                if apart
                else [jax.ShapeDtypeStruct((ROWS, 4, width + STAT, BLOCK), jnp.bfloat16)]
            ),
        ]
        out_specs = [
            pl.BlockSpec((4, width, BLOCK), lambda r, meta: (0, 0, 0)),
            pl.BlockSpec((4, 8, BLOCK), lambda r, meta: (0, 0, 0)),
            pl.BlockSpec((4, 8, BLOCK), lambda r, meta: (0, 0, 0)),
            *(
                [pl.BlockSpec((4, width + STAT, BLOCK), lambda r, meta: (0, 0, 0))] * 3
                if apart
                else [            pl.BlockSpec((1, 4, width + STAT, BLOCK), lambda r, meta: ((meta[16 * RING] + jnp.maximum(r, 1)) & 3, 0, 0, 0))]
            ),
        ]
        if apart:
            out_shape = out_shape[:3] if rows == (0,) else out_shape[3:]
            out_specs = out_specs[:3] if rows == (0,) else out_specs[3:]
    else:
        out_shape = [
            jax.ShapeDtypeStruct((16, width, BLOCK), f32),
            jax.ShapeDtypeStruct((16, 8, BLOCK), f32),
            jax.ShapeDtypeStruct((16, 8, BLOCK), f32),
        ]
        out_specs = state_specs
    count = len(offsets)
    scratch = [
        pltpu.VMEM((5, width, BLOCK), f32),
        pltpu.VMEM((5, 8, BLOCK), f32),
        pltpu.VMEM((5, 8, BLOCK), f32),
        pltpu.VMEM((5 * BLOCK, width), jnp.bfloat16),
        pltpu.VMEM((count, 4, width, BLOCK), jnp.bfloat16),
        pltpu.VMEM((count, 4, width, BLOCK), jnp.bfloat16),
        pltpu.SMEM((80,), jnp.int32),
    ]
    return list(pl.pallas_call(
        functools.partial(attend_kernel, offsets, heads, first, last, rows),
        out_shape=out_shape,
        grid_spec=pltpu.PrefetchScalarGridSpec(
            num_scalar_prefetch=1,
            grid=(len(rows),),
            in_specs=in_specs,
            out_specs=out_specs,
            scratch_shapes=scratch,
        ),
        compiler_params=pltpu.CompilerParams(vmem_limit_bytes=grant),
        cost_estimate=pl.CostEstimate(
            flops=int((2 + 3 * len(offsets)) * 1.1e9),
            bytes_accessed=1 << 20,
            transcendentals=0,
        ),
        name=f"attend_{first_head}_{'_'.join(str(o % RING) for o in offsets)}_row{begin}",
    )(meta, *operands))


def join_kernel(heads, acc_ref, m_ref, l_ref, one, two, three, *rest):
    out_ref = rest[-1]
    width = heads * HEAD
    tops, sums = [m_ref[0]], [l_ref[0]]
    for part in (one, two, three):
        stats = part[0, width:, :].astype(jnp.float32)
        top = (stats[16:24] + stats[8:16]) + stats[0:8]
        total = (stats[40:48] + stats[32:40]) + stats[24:32]
        tops.append(jnp.where(total > 0, top, NEG_FILL))
        sums.append(total)
    scale = HEAD**-0.5 * math.log2(math.e)
    highest = jnp.maximum(jnp.maximum(tops[0], tops[1]), jnp.maximum(tops[2], tops[3]))
    fades = [jnp.exp2((top - highest) * scale) for top in tops]
    shares = [fades[0]] + [fades[i] * sums[i] for i in (1, 2, 3)]
    whole = fades[0] * sums[0] + shares[1] + shares[2] + shares[3]
    inverse = 1.0 / whole
    for h in range(heads):
        cols = slice(h * HEAD, (h + 1) * HEAD)
        mixed = acc_ref[0, cols, :] * shares[0][h : h + 1, :]
        for i, part in enumerate((one, two, three)):
            mixed += part[0, cols, :].astype(jnp.float32) * shares[i + 1][h : h + 1, :]
        mixed = mixed * inverse[h : h + 1, :]
        out_ref[:, cols] = mixed.T.astype(jnp.bfloat16)


def join(chunk, state, parts, out):
    first_head, heads = chunk
    width = heads * HEAD
    in_specs = [
        pl.BlockSpec((1, width, BLOCK), lambda b: (b, 0, 0)),
        pl.BlockSpec((1, 8, BLOCK), lambda b: (b, 0, 0)),
        pl.BlockSpec((1, 8, BLOCK), lambda b: (b, 0, 0)),
    ] + [pl.BlockSpec((1, width + STAT, BLOCK), lambda b: (b, 0, 0))] * 3
    operands = [*state, *parts]
    aliases = {}
    if out is not None:
        aliases = {len(operands): 0}
        in_specs.append(pl.BlockSpec(memory_space=pl.ANY))
        operands.append(out)
    return pl.pallas_call(
        functools.partial(join_kernel, heads),
        out_shape=jax.ShapeDtypeStruct((512, 1024), jnp.bfloat16),
        grid=(4,),
        in_specs=in_specs,
        out_specs=pl.BlockSpec((BLOCK, width), lambda b: (b, first_head // heads)),
        input_output_aliases=aliases,
        compiler_params=pltpu.CompilerParams(vmem_limit_bytes=VMEM_LIMIT),
        cost_estimate=pl.CostEstimate(
            flops=512 * width * 10, bytes_accessed=512 * width * 14, transcendentals=0
        ),
        name=f"join_{first_head}",
    )(*operands)


def shift(value, axis, step):
    size = lax.axis_size(axis)
    return lax.ppermute(value, axis, [(i, (i + step) % size) for i in range(size)])


def to_row(value, step):
    moves = [(i, i + step) for i in range(ROWS) if 0 <= i + step < ROWS]
    return lax.ppermute(value, "y", moves)


def swap(value, axis, bit):
    size = lax.axis_size(axis)
    return lax.ppermute(value, axis, [(i, i ^ bit) for i in range(size)])


def after(value, *others):
    return lax.optimization_barrier((value, *others))[0]


class Wire:
    def __init__(self, side, sign, depth=2):
        self.side, self.sign, self.depth = side, sign, depth
        self.sent = []

    def send(self, name, ring, distance, *others):
        source = ring[-self.sign * (distance - 1)]
        waits = list(others)
        waits += self.sent[-self.depth - 1 : -self.depth + 1] if self.sent[1:] else []
        if waits:
            source = after(source, *waits)
        with jax.named_scope(f"{name}{distance}_{self.side}"):
            got = shift(source, "z", self.sign)
        self.sent.append(got)
        ring[-self.sign * distance if distance < 4 else 4] = got


def shards(query_states, key_states, value_states, gate_logits, selected_blocks):
    my_y, my_z = lax.axis_index("y"), lax.axis_index("z")
    gate_values = jax.nn.sigmoid(gate_logits.astype(jnp.float32))
    total = jnp.sum(gate_values, axis=1, keepdims=True)
    before = jnp.zeros_like(total)
    value_tiles = value_states.reshape(4, BLOCK, -1).transpose(0, 2, 1)
    va, vb = {0: value_tiles[:, : 4 * HEAD]}, {0: value_tiles[:, 4 * HEAD :]}
    right, left = Wire("right", 1), Wire("left", -1)
    for wire in (right, left):
        wire.send("va", va, 1)
    picks = selected_blocks.T.astype(jnp.float32)
    with jax.named_scope("prefix"):
        rows_before = before
        for bit in (1, 2):
            other = swap(jnp.concatenate([total, rows_before, picks], axis=1), "y", bit)
            if bit == 1:
                own_total = total
            rows_before = rows_before + jnp.where((my_y & bit) != 0, other[:, :1], 0.0)
            total = total + other[:, :1]
            picks = jnp.concatenate([picks, other[:, 2:]], axis=1)
        own_total = after(own_total, va[1], va[-1])
        for bit in (1, 2, 4):
            other = swap(jnp.concatenate([own_total, rows_before], axis=1), "z", bit)
            before = before + jnp.where((my_z & bit) != 0, other[:, :1], 0.0)
            own_total = own_total + other[:, :1]
            rows_before = rows_before + other[:, 1:]
    angles = before + rows_before + jnp.cumsum(gate_values, axis=1)
    query_rot, keys_a, keys_b = rotate(angles, query_states, key_states)
    ka, kb = {0: keys_a}, {0: keys_b}
    with jax.named_scope("queries"):
        queries = lax.all_to_all(query_rot, "y", 0, 0, tiled=True)

    picks = picks.astype(jnp.int32).T.reshape(4, 1, 4, 8)
    wanted = (my_y + lax.broadcasted_iota(jnp.int32, (4, 4, 1, 1), 1)) ^ my_y
    turn = lax.broadcasted_iota(jnp.int32, (4, 4, 1, 1), 0)
    blocks = jnp.sum(jnp.where(wanted == turn, picks, 0), axis=0).reshape(16, 1, 8)
    row = lax.broadcasted_iota(jnp.int32, (16, RING, 8), 0)
    distance = lax.broadcasted_iota(jnp.int32, (16, RING, 8), 1)
    own = ((my_y + row // 4) * RING + my_z) * 4 + row % 4
    hit = (blocks >> 5 == my_y) & (((blocks >> 2) - my_z) & 7 == distance)
    hit &= (blocks != own) & (my_y + row // 4 < ROWS)
    code = jnp.where(distance == 0, 1 << (blocks & 3), (blocks & 3) + 1)
    meta = jnp.sum(jnp.where(hit, code, 0), axis=2).reshape(-1)
    meta = jnp.concatenate([meta, my_y.astype(jnp.int32)[None]])

    def call(part, group, state, last, **more):
        offsets = []
        for distance in group:
            offsets += [distance] if distance in (0, 4) else [-distance, distance]
        keys, values = (ka, va) if part == 0 else (kb, vb)
        return attend(
            meta,
            queries,
            CHUNKS[part],
            tuple(offsets),
            [keys[o] for o in offsets],
            [values[o] for o in offsets],
            state,
            last,
            **more,
        )

    def pick(rows, step):
        return lax.dynamic_index_in_dim(rows, (my_y + step) & 3, 0, keepdims=False)

    for name, ring, distance in (
        ("ka", ka, 1),
        ("va", va, 2),
        ("ka", ka, 2),
        ("va", va, 3),
        ("ka", ka, 3),
    ):
        for wire in (right, left):
            wire.send(name, ring, distance)
    right.send("va", va, 4)
    left.send("vb", vb, 1)
    state = call(0, GROUPS[0][0], None, False)
    right.send("ka", ka, 4, state[1])
    left.send("kb", kb, 1, state[1])
    right.send("vb", vb, 1)
    left.send("vb", vb, 2)
    right.send("kb", kb, 1)
    left.send("kb", kb, 2)
    state = call(0, GROUPS[0][1], state, True)
    right.send("vb", vb, 2, state[1])
    left.send("vb", vb, 3, state[1])
    right.send("kb", kb, 2, state[1])
    left.send("kb", kb, 3, state[1])
    first_b = call(1, GROUPS[1][0], None, False, grant=60 << 20)
    right.send("vb", vb, 3, first_b[1])
    left.send("vb", vb, 4, first_b[1])
    right.send("kb", kb, 3)
    second_b = call(1, GROUPS[1][1], first_b, False, grant=60 << 20)
    left.send("kb", kb, 4, second_b[1])
    mine_a = state[:3]
    with jax.named_scope("partials_a"):
        parts_a = lax.all_to_all(state[3], "y", 0, 0, tiled=True)
    second_b[1] = after(second_b[1], parts_a)
    sends = call(1, GROUPS[1][2], second_b, True, rows=(1, 2, 3), grant=60 << 20)
    parts_b = []
    for s in (1, 2, 3):
        with jax.named_scope(f"partial_b{s}"):
            parts_b.append(to_row(sends[s - 1], s))
    second_b[1] = after(second_b[1], sends[0])
    state = call(1, GROUPS[1][2], second_b, True, rows=(0,), grant=60 << 20)
    parts_a = after(parts_a, state[1])
    out = join(CHUNKS[0], mine_a, [pick(parts_a, -s) for s in (1, 2, 3)], None)
    return join(CHUNKS[1], state[:3], parts_b, out)


def solution(mesh):
    grid = Mesh(mesh.devices.reshape(2, ROWS, RING, 4), ("dp", "y", "z", "head"))
    tokens = ("dp", "y", "z")
    placed = (
        P(tokens, "head"),
        P(tokens, "head"),
        P(tokens, "head"),
        P("head", tokens),
        P(tokens, None),
    )
    return jax.shard_map(
        shards, mesh=grid, in_specs=placed, out_specs=P(tokens, "head"), check_vma=False
    )
```

```python
import functools
import math

import jax
import jax.numpy as jnp
from jax import lax
from jax.experimental import pallas as pl
from jax.experimental.pallas import tpu as pltpu
from jax.sharding import Mesh, PartitionSpec as P

BLOCK = 128
HEAD = 128
ROWS = 4
RING = 8
NEG_FILL = -1e30
ROPE_BASE = 10000.0
VMEM_LIMIT = 24 << 20
IDLE = 4
STAT = 48
CHUNKS = ((0, 4), (4, 4))
GROUPS = (((0, 1, 2), (3, 4)), ((0, 1), (2,), (3, 4)))


QUARTER = (1.5703125, 4.837512969970703e-4, 7.54978995489188216e-8)


def sin_cos(phase):
    turns = jnp.floor(phase * (2 / math.pi) + 0.5)
    x = phase
    for part in QUARTER:
        x = x - turns * part
    square = x * x
    sine = ((-1.9515295891e-4 * square + 8.3321608736e-3) * square - 1.6666654611e-1) * square
    sine = sine * x + x
    cosine = ((2.443315711809948e-5 * square - 1.388731625493765e-3) * square + 4.166664568298827e-2)
    cosine = cosine * square * square - 0.5 * square + 1.0
    quadrant = turns.astype(jnp.int32) & 3
    odd = (quadrant & 1) == 1
    sine, cosine = jnp.where(odd, cosine, sine), jnp.where(odd, sine, cosine)
    sine = jnp.where(quadrant >= 2, -sine, sine)
    cosine = jnp.where((quadrant == 1) | (quadrant == 2), -cosine, cosine)
    return sine, cosine


def rotate_kernel(angle_ref, freq_ref, q_ref, k_ref, *outs):
    freq = freq_ref[...]
    lane = lax.broadcasted_iota(jnp.int32, (BLOCK, HEAD), 1)
    low = lane < HEAD // 2
    heads = q_ref.shape[1] // HEAD
    for pair in range(heads // 2):
        even = angle_ref[:, 2 * pair : 2 * pair + 1]
        odd = angle_ref[:, 2 * pair + 1 : 2 * pair + 2]
        sine, cosine = sin_cos(jnp.where(low, even, odd) * freq)
        sine_turned = pltpu.roll(sine, HEAD // 2, 1)
        cosine_turned = pltpu.roll(cosine, HEAD // 2, 1)
        for h in (2 * pair, 2 * pair + 1):
            first, second = (sine, sine_turned) if h % 2 == 0 else (sine_turned, sine)
            signed = jnp.where(low, -first, second)
            first, second = (cosine, cosine_turned) if h % 2 == 0 else (cosine_turned, cosine)
            plain = jnp.where(low, first, second)
            cols = slice(h * HEAD, (h + 1) * HEAD)

            def turn(x):
                x = x.astype(jnp.float32)
                return (x * plain + pltpu.roll(x, HEAD // 2, 1) * signed).astype(jnp.bfloat16)

            part = slice(h % 4 * HEAD, (h % 4 + 1) * HEAD)
            query = turn(q_ref[:, cols])
            for row in range(ROWS):
                outs[0][row, :, cols] = query
            outs[1 + h // 4][0, part, :] = turn(k_ref[:, cols])


def rotate(angles, queries, keys):
    half = HEAD // 2
    inv_freq = ROPE_BASE ** (-jnp.arange(half).astype(jnp.float32) / half)
    inv_freq = jnp.concatenate([inv_freq, inv_freq])[None]
    heads = angles.shape[0]
    bf16 = jnp.bfloat16
    rows = pl.BlockSpec((BLOCK, heads * HEAD), lambda b: (b, 0))
    copies = pl.BlockSpec((ROWS, BLOCK, heads * HEAD), lambda b: (0, b, 0))
    tiled = pl.BlockSpec((1, 4 * HEAD, BLOCK), lambda b: (b, 0, 0))
    return pl.pallas_call(
        rotate_kernel,
        out_shape=[
            jax.ShapeDtypeStruct((ROWS, *queries.shape), bf16),
            jax.ShapeDtypeStruct((4, 4 * HEAD, BLOCK), bf16),
            jax.ShapeDtypeStruct((4, 4 * HEAD, BLOCK), bf16),
        ],
        grid=(4,),
        in_specs=[
            pl.BlockSpec((BLOCK, heads), lambda b: (b, 0)),
            pl.BlockSpec((1, HEAD), lambda b: (0, 0)),
            rows,
            rows,
        ],
        out_specs=[copies, tiled, tiled],
        compiler_params=pltpu.CompilerParams(vmem_limit_bytes=60 << 20),
        cost_estimate=pl.CostEstimate(flops=5 * 10**9, bytes_accessed=6 << 20, transcendentals=0),
        name="rotate",
    )(angles.T, inv_freq, queries, keys)


def attend_kernel(offsets, heads, first, last, rows, meta, *refs):
    count = len(offsets)
    given_q, refs = refs[0], refs[1:]
    k_refs, v_refs = refs[:count], refs[count : 2 * count]
    rest = list(refs[2 * count :])
    acc, m_run, l_run, q_ref, k_all, v_all, todo = rest[-7:]
    rest = rest[:-7]
    given = None
    if not first:
        given, rest = rest[:3], rest[3:]
    r = pl.program_id(0) + rows[0]
    scale = HEAD**-0.5 * math.log2(math.e)

    @pl.when(pl.program_id(0) == 0)
    def _():
        def hold(kb, carry):
            for at in range(count):
                k_all[at, kb] = k_refs[at][kb]
                v_all[at, kb] = v_refs[at][kb]
            return carry

        lax.fori_loop(0, 4, hold, 0)
        q_ref[IDLE * BLOCK :, :] = jnp.zeros((BLOCK, heads * HEAD), jnp.bfloat16)
        acc[IDLE] = jnp.zeros((heads * HEAD, BLOCK), jnp.float32)
        m_run[IDLE] = jnp.full((8, BLOCK), NEG_FILL)
        l_run[IDLE] = jnp.zeros((8, BLOCK), jnp.float32)

    def enter(qb, carry):
        q_rows = pl.ds(pl.multiple_of(qb * BLOCK, BLOCK), BLOCK)
        q_ref[q_rows, :] = given_q[0, q_rows, :]
        if first:
            acc[qb] = jnp.zeros((heads * HEAD, BLOCK), jnp.float32)
            m_run[qb] = jnp.full((8, BLOCK), NEG_FILL)
            l_run[qb] = jnp.zeros((8, BLOCK), jnp.float32)
        else:
            acc[qb] = given[0][qb]
            m_run[qb] = given[1][qb]
            l_run[qb] = given[2][qb]
        return carry

    lax.fori_loop(0, 4, enter, 0)

    span = range(heads)
    cols = [slice(h * HEAD, (h + 1) * HEAD) for h in span]

    def two(items, causal):
        olds, scores = [], []
        for qb, at, kb in items:
            q_rows = pl.ds(pl.multiple_of(qb * BLOCK, BLOCK), BLOCK)
            olds.append((m_run[qb], l_run[qb]))
            scores.append(
                [
                    lax.dot_general(
                        k_all[at, kb, cols[h], :],
                        q_ref[q_rows, cols[h]],
                        (((1,), (1,)), ((), ())),
                        preferred_element_type=jnp.float32,
                    )
                    for h in span
                ]
            )
        if causal:
            key_pos = lax.broadcasted_iota(jnp.int32, (BLOCK, BLOCK), 0)
            query_pos = lax.broadcasted_iota(jnp.int32, (BLOCK, BLOCK), 1)
            seen = key_pos <= query_pos
            scores = [[jnp.where(seen, s, NEG_FILL) for s in group] for group in scores]
        results = []
        for (qb, at, kb), (m_old, l_old), group in zip(items, olds, scores):
            tops = [jnp.max(s, axis=0, keepdims=True) for s in group]
            if heads < 8:
                tops.append(m_old[heads:])
            m_new = jnp.maximum(m_old, jnp.concatenate(tops, axis=0))
            fade = jnp.exp2((m_old - m_new) * scale)
            weights = [jnp.exp2((group[h] - m_new[h : h + 1]) * scale) for h in span]
            sums = [jnp.sum(w, axis=0, keepdims=True) for w in weights]
            if heads < 8:
                sums.append(jnp.zeros((8 - heads, BLOCK), jnp.float32))
            mixed = [
                jnp.dot(
                    v_all[at, kb, cols[h], :],
                    weights[h].astype(jnp.bfloat16),
                    preferred_element_type=jnp.float32,
                )
                for h in span
            ]
            results.append((m_new, l_old * fade + jnp.concatenate(sums, axis=0), fade, mixed))
        wholes = [
            [acc[qb, cols[h], :] * fade[h : h + 1] + mixed[h] for h in span]
            for (qb, _, _), (_, _, fade, mixed) in zip(items, results)
        ]
        for (qb, _, _), (m_new, l_new, _, _), whole in zip(items, results, wholes):
            m_run[qb] = m_new
            l_run[qb] = l_new
            for h in span:
                acc[qb, cols[h], :] = whole[h]

    if 0 in offsets:
        here = offsets.index(0)

        @pl.when(r == 0)
        def _():
            def own(i, carry):
                two([(2 * i, here, 2 * i), (2 * i + 1, here, 2 * i + 1)], True)
                return carry

            lax.fori_loop(0, 2, own, 0)

    def note(at, choice, offset, qb, length, newest):
        code = meta[(r * 4 + qb) * RING + offset % RING]
        if offset == 0:
            valid, kb = (code >> choice) & 1, choice
        else:
            valid, kb = (code > 0).astype(jnp.int32), jnp.maximum(code - 1, 0)
        item = qb + at * 16 + kb * 256
        clash = valid & length & (newest == qb).astype(jnp.int32)
        todo[length] = jnp.where(clash == 1, IDLE, item)
        todo[length + 1] = item
        return length + valid * (1 + clash), jnp.where(valid == 1, qb, newest)

    found = (jnp.int32(0), jnp.int32(-1))
    for at, offset in enumerate(offsets):
        if offset == 0:
            found = lax.fori_loop(
                0, 16, lambda i, f, at=at: note(at, i >> 2, 0, i & 3, *f), found
            )
        else:
            found = lax.fori_loop(
                0, 4, lambda i, f, at=at, offset=offset: note(at, 0, offset, i, *f), found
            )
    length = found[0]
    todo[length] = IDLE

    def step(i, carry):
        items = []
        for side in (0, 1):
            item = todo[2 * i + side]
            items.append((item & 15, (item >> 4) & 15, item >> 8))
        two(items, False)
        return carry

    lax.fori_loop(0, (length + 1) >> 1, step, 0)

    def leave(acc_out, m_out, l_out):
        def copy(qb, carry):
            acc_out[qb] = acc[qb]
            m_out[qb] = m_run[qb]
            l_out[qb] = l_run[qb]
            return carry

        lax.fori_loop(0, 4, copy, 0)

    if not last:
        leave(*rest)
    else:
        packed_refs = rest
        if 0 in rows:
            packed_refs = rest[3:]

            @pl.when(r == 0)
            def _():
                leave(*rest[:3])

        def send(packed_ref, lead):
            def pack(qb, carry):
                pieces = []
                for value in (m_run[qb], l_run[qb]):
                    for _ in range(3):
                        piece = value.astype(jnp.bfloat16).astype(jnp.float32)
                        pieces.append(piece)
                        value = value - piece
                packed_ref[(*lead, qb, slice(heads * HEAD, None), slice(None))] = jnp.concatenate(pieces, axis=0).astype(
                    jnp.bfloat16
                )
                total = l_run[qb]
                inverse = 1.0 / jnp.where(total > 0, total, 1.0)
                for h in span:
                    packed_ref[(*lead, qb, cols[h], slice(None))] = (
                        acc[qb, cols[h], :] * inverse[h : h + 1]
                    ).astype(jnp.bfloat16)
                return carry

            lax.fori_loop(0, 4, pack, 0)

        if len(packed_refs) == 1:
            pl.when(r > 0)(lambda: send(packed_refs[0], (0,)))
        else:
            for row, packed_ref in enumerate(packed_refs):
                pl.when(r == row + 1)(functools.partial(send, packed_ref, ()))


def attend(meta, queries, chunk, offsets, keys, values, state, last, rows=(0, 1, 2, 3), grant=VMEM_LIMIT):
    first_head, heads = chunk
    apart = first_head > 0
    begin = rows[0]
    width = heads * HEAD
    first = state is None
    acc_spec = pl.BlockSpec((4, width, BLOCK), lambda r, meta: (r + begin, 0, 0))
    run_spec = pl.BlockSpec((4, 8, BLOCK), lambda r, meta: (r + begin, 0, 0))
    state_specs = [acc_spec, run_spec, run_spec]
    in_specs = [
        pl.BlockSpec(
            (1, 512, width),
            lambda r, meta: (jnp.minimum(meta[16 * RING] + r + begin, ROWS - 1), 0, first_head // heads),
        )
    ]
    in_specs += [pl.BlockSpec((4, width, BLOCK), lambda r, meta: (0, 0, 0))] * (2 * len(offsets))
    operands = [queries, *keys, *values]
    if not first:
        in_specs += state_specs
        operands += list(state)
    f32 = jnp.float32
    if last:
        out_shape = [
            jax.ShapeDtypeStruct((4, width, BLOCK), f32),
            jax.ShapeDtypeStruct((4, 8, BLOCK), f32),
            jax.ShapeDtypeStruct((4, 8, BLOCK), f32),
            *(
                [jax.ShapeDtypeStruct((4, width + STAT, BLOCK), jnp.bfloat16)] * 3
                if apart
                else [jax.ShapeDtypeStruct((ROWS, 4, width + STAT, BLOCK), jnp.bfloat16)]
            ),
        ]
        out_specs = [
            pl.BlockSpec((4, width, BLOCK), lambda r, meta: (0, 0, 0)),
            pl.BlockSpec((4, 8, BLOCK), lambda r, meta: (0, 0, 0)),
            pl.BlockSpec((4, 8, BLOCK), lambda r, meta: (0, 0, 0)),
            *(
                [pl.BlockSpec((4, width + STAT, BLOCK), lambda r, meta: (0, 0, 0))] * 3
                if apart
                else [            pl.BlockSpec((1, 4, width + STAT, BLOCK), lambda r, meta: ((meta[16 * RING] + jnp.maximum(r, 1)) & 3, 0, 0, 0))]
            ),
        ]
        if apart:
            out_shape = out_shape[:3] if rows == (0,) else out_shape[3:]
            out_specs = out_specs[:3] if rows == (0,) else out_specs[3:]
    else:
        out_shape = [
            jax.ShapeDtypeStruct((16, width, BLOCK), f32),
            jax.ShapeDtypeStruct((16, 8, BLOCK), f32),
            jax.ShapeDtypeStruct((16, 8, BLOCK), f32),
        ]
        out_specs = state_specs
    count = len(offsets)
    scratch = [
        pltpu.VMEM((5, width, BLOCK), f32),
        pltpu.VMEM((5, 8, BLOCK), f32),
        pltpu.VMEM((5, 8, BLOCK), f32),
        pltpu.VMEM((5 * BLOCK, width), jnp.bfloat16),
        pltpu.VMEM((count, 4, width, BLOCK), jnp.bfloat16),
        pltpu.VMEM((count, 4, width, BLOCK), jnp.bfloat16),
        pltpu.SMEM((80,), jnp.int32),
    ]
    return list(pl.pallas_call(
        functools.partial(attend_kernel, offsets, heads, first, last, rows),
        out_shape=out_shape,
        grid_spec=pltpu.PrefetchScalarGridSpec(
            num_scalar_prefetch=1,
            grid=(len(rows),),
            in_specs=in_specs,
            out_specs=out_specs,
            scratch_shapes=scratch,
        ),
        compiler_params=pltpu.CompilerParams(vmem_limit_bytes=grant),
        cost_estimate=pl.CostEstimate(
            flops=int((2 + 3 * len(offsets)) * 1.1e9),
            bytes_accessed=1 << 20,
            transcendentals=0,
        ),
        name=f"attend_{first_head}_{'_'.join(str(o % RING) for o in offsets)}_row{begin}",
    )(meta, *operands))


def join_kernel(heads, acc_ref, m_ref, l_ref, one, two, three, *rest):
    out_ref = rest[-1]
    width = heads * HEAD
    tops, sums = [m_ref[0]], [l_ref[0]]
    for part in (one, two, three):
        stats = part[0, width:, :].astype(jnp.float32)
        top = (stats[16:24] + stats[8:16]) + stats[0:8]
        total = (stats[40:48] + stats[32:40]) + stats[24:32]
        tops.append(jnp.where(total > 0, top, NEG_FILL))
        sums.append(total)
    scale = HEAD**-0.5 * math.log2(math.e)
    highest = jnp.maximum(jnp.maximum(tops[0], tops[1]), jnp.maximum(tops[2], tops[3]))
    fades = [jnp.exp2((top - highest) * scale) for top in tops]
    shares = [fades[0]] + [fades[i] * sums[i] for i in (1, 2, 3)]
    whole = fades[0] * sums[0] + shares[1] + shares[2] + shares[3]
    inverse = 1.0 / whole
    for h in range(heads):
        cols = slice(h * HEAD, (h + 1) * HEAD)
        mixed = acc_ref[0, cols, :] * shares[0][h : h + 1, :]
        for i, part in enumerate((one, two, three)):
            mixed += part[0, cols, :].astype(jnp.float32) * shares[i + 1][h : h + 1, :]
        mixed = mixed * inverse[h : h + 1, :]
        out_ref[:, cols] = mixed.T.astype(jnp.bfloat16)


def join(chunk, state, parts, out):
    first_head, heads = chunk
    width = heads * HEAD
    in_specs = [
        pl.BlockSpec((1, width, BLOCK), lambda b: (b, 0, 0)),
        pl.BlockSpec((1, 8, BLOCK), lambda b: (b, 0, 0)),
        pl.BlockSpec((1, 8, BLOCK), lambda b: (b, 0, 0)),
    ] + [pl.BlockSpec((1, width + STAT, BLOCK), lambda b: (b, 0, 0))] * 3
    operands = [*state, *parts]
    aliases = {}
    if out is not None:
        aliases = {len(operands): 0}
        in_specs.append(pl.BlockSpec(memory_space=pl.ANY))
        operands.append(out)
    return pl.pallas_call(
        functools.partial(join_kernel, heads),
        out_shape=jax.ShapeDtypeStruct((512, 1024), jnp.bfloat16),
        grid=(4,),
        in_specs=in_specs,
        out_specs=pl.BlockSpec((BLOCK, width), lambda b: (b, first_head // heads)),
        input_output_aliases=aliases,
        compiler_params=pltpu.CompilerParams(vmem_limit_bytes=VMEM_LIMIT),
        cost_estimate=pl.CostEstimate(
            flops=512 * width * 10, bytes_accessed=512 * width * 14, transcendentals=0
        ),
        name=f"join_{first_head}",
    )(*operands)


def shift(value, axis, step):
    size = lax.axis_size(axis)
    return lax.ppermute(value, axis, [(i, (i + step) % size) for i in range(size)])


def to_row(value, step):
    moves = [(i, i + step) for i in range(ROWS) if 0 <= i + step < ROWS]
    return lax.ppermute(value, "y", moves)


def swap(value, axis, bit):
    size = lax.axis_size(axis)
    return lax.ppermute(value, axis, [(i, i ^ bit) for i in range(size)])


def after(value, *others):
    return lax.optimization_barrier((value, *others))[0]


class Wire:
    def __init__(self, side, sign, depth=2):
        self.side, self.sign, self.depth = side, sign, depth
        self.sent = []

    def send(self, name, ring, distance, *others):
        source = ring[-self.sign * (distance - 1)]
        waits = list(others)
        waits += self.sent[-self.depth - 1 : -self.depth + 1] if self.sent[1:] else []
        if waits:
            source = after(source, *waits)
        with jax.named_scope(f"{name}{distance}_{self.side}"):
            got = shift(source, "z", self.sign)
        self.sent.append(got)
        ring[-self.sign * distance if distance < 4 else 4] = got


def shards(query_states, key_states, value_states, gate_logits, selected_blocks):
    my_y, my_z = lax.axis_index("y"), lax.axis_index("z")
    gate_values = jax.nn.sigmoid(gate_logits.astype(jnp.float32))
    total = jnp.sum(gate_values, axis=1, keepdims=True)
    before = jnp.zeros_like(total)
    value_tiles = value_states.reshape(4, BLOCK, -1).transpose(0, 2, 1)
    va, vb = {0: value_tiles[:, : 4 * HEAD]}, {0: value_tiles[:, 4 * HEAD :]}
    right, left = Wire("right", 1), Wire("left", -1)
    for wire in (right, left):
        wire.send("va", va, 1)
    picks = selected_blocks.T.astype(jnp.float32)
    with jax.named_scope("prefix"):
        rows_before = before
        for bit in (1, 2):
            other = swap(jnp.concatenate([total, rows_before, picks], axis=1), "y", bit)
            if bit == 1:
                own_total = total
            rows_before = rows_before + jnp.where((my_y & bit) != 0, other[:, :1], 0.0)
            total = total + other[:, :1]
            picks = jnp.concatenate([picks, other[:, 2:]], axis=1)
        own_total = after(own_total, va[1], va[-1])
        for bit in (1, 2, 4):
            other = swap(jnp.concatenate([own_total, rows_before], axis=1), "z", bit)
            before = before + jnp.where((my_z & bit) != 0, other[:, :1], 0.0)
            own_total = own_total + other[:, :1]
            rows_before = rows_before + other[:, 1:]
    angles = before + rows_before + jnp.cumsum(gate_values, axis=1)
    query_rot, keys_a, keys_b = rotate(angles, query_states, key_states)
    ka, kb = {0: keys_a}, {0: keys_b}
    with jax.named_scope("queries"):
        queries = lax.all_to_all(query_rot, "y", 0, 0, tiled=True)

    picks = picks.astype(jnp.int32).T.reshape(4, 1, 4, 8)
    wanted = (my_y + lax.broadcasted_iota(jnp.int32, (4, 4, 1, 1), 1)) ^ my_y
    turn = lax.broadcasted_iota(jnp.int32, (4, 4, 1, 1), 0)
    blocks = jnp.sum(jnp.where(wanted == turn, picks, 0), axis=0).reshape(16, 1, 8)
    row = lax.broadcasted_iota(jnp.int32, (16, RING, 8), 0)
    distance = lax.broadcasted_iota(jnp.int32, (16, RING, 8), 1)
    own = ((my_y + row // 4) * RING + my_z) * 4 + row % 4
    hit = (blocks >> 5 == my_y) & (((blocks >> 2) - my_z) & 7 == distance)
    hit &= (blocks != own) & (my_y + row // 4 < ROWS)
    code = jnp.where(distance == 0, 1 << (blocks & 3), (blocks & 3) + 1)
    meta = jnp.sum(jnp.where(hit, code, 0), axis=2).reshape(-1)
    meta = jnp.concatenate([meta, my_y.astype(jnp.int32)[None]])

    def call(part, group, state, last, **more):
        offsets = []
        for distance in group:
            offsets += [distance] if distance in (0, 4) else [-distance, distance]
        keys, values = (ka, va) if part == 0 else (kb, vb)
        return attend(
            meta,
            queries,
            CHUNKS[part],
            tuple(offsets),
            [keys[o] for o in offsets],
            [values[o] for o in offsets],
            state,
            last,
            **more,
        )

    def pick(rows, step):
        return lax.dynamic_index_in_dim(rows, (my_y + step) & 3, 0, keepdims=False)

    for name, ring, distance in (
        ("ka", ka, 1),
        ("va", va, 2),
        ("ka", ka, 2),
        ("va", va, 3),
        ("ka", ka, 3),
    ):
        for wire in (right, left):
            wire.send(name, ring, distance)
    right.send("va", va, 4)
    left.send("vb", vb, 1)
    state = call(0, GROUPS[0][0], None, False)
    right.send("ka", ka, 4, state[1])
    left.send("kb", kb, 1, state[1])
    right.send("vb", vb, 1)
    left.send("vb", vb, 2)
    right.send("kb", kb, 1)
    left.send("kb", kb, 2)
    state = call(0, GROUPS[0][1], state, True)
    right.send("vb", vb, 2, state[1])
    left.send("vb", vb, 3, state[1])
    right.send("kb", kb, 2, state[1])
    left.send("kb", kb, 3, state[1])
    first_b = call(1, GROUPS[1][0], None, False, grant=60 << 20)
    right.send("vb", vb, 3)
    left.send("vb", vb, 4)
    right.send("kb", kb, 3, first_b[1])
    second_b = call(1, GROUPS[1][1], first_b, False, grant=60 << 20)
    left.send("kb", kb, 4, second_b[1])
    mine_a = state[:3]
    with jax.named_scope("partials_a"):
        parts_a = lax.all_to_all(state[3], "y", 0, 0, tiled=True)
    second_b[1] = after(second_b[1], parts_a)
    sends = call(1, GROUPS[1][2], second_b, True, rows=(1, 2, 3), grant=60 << 20)
    parts_b = []
    for s in (1, 2, 3):
        with jax.named_scope(f"partial_b{s}"):
            parts_b.append(to_row(sends[s - 1], s))
    second_b[1] = after(second_b[1], sends[0])
    state = call(1, GROUPS[1][2], second_b, True, rows=(0,), grant=60 << 20)
    parts_a = after(parts_a, state[1])
    out = join(CHUNKS[0], mine_a, [pick(parts_a, -s) for s in (1, 2, 3)], None)
    return join(CHUNKS[1], state[:3], parts_b, out)


def solution(mesh):
    grid = Mesh(mesh.devices.reshape(2, ROWS, RING, 4), ("dp", "y", "z", "head"))
    tokens = ("dp", "y", "z")
    placed = (
        P(tokens, "head"),
        P(tokens, "head"),
        P(tokens, "head"),
        P("head", tokens),
        P(tokens, None),
    )
    return jax.shard_map(
        shards, mesh=grid, in_specs=placed, out_specs=P(tokens, "head"), check_vma=False
    )
```
